32 devices in a mesh: dp: 16 (over z, x, core), seq: 2 (over y).
Axes of the slice: x: 2, y: 2, z: 4, core: 2. Of those that a mesh axis runs over, the one named last changes fastest.
Arguments:
- inputs: bfloat16 [32768, 768], P(('dp', 'seq')), may hold values from -6 to 6
- query_weight: bfloat16 [768, 768], P(('dp', 'seq')), may hold values from -0.21875 to 0.21875
- query_bias: bfloat16 [768], P(('dp', 'seq')), may hold values from -3 to 3
- key_weight: bfloat16 [768, 768], P(('dp', 'seq')), may hold values from -0.21875 to 0.21875
- value_weight: bfloat16 [768, 768], P(('dp', 'seq')), may hold values from -0.21875 to 0.21875
- value_bias: bfloat16 [768], P(('dp', 'seq')), may hold values from -3 to 3
- output_weight: bfloat16 [768, 768], P(('dp', 'seq')), may hold values from -1.75 to 1.75
- output_bias: bfloat16 [768], P(('dp', 'seq')), may hold values from -3 to 3
- first_gain: bfloat16 [768], P(('dp', 'seq')), may hold values from 0.5 to 1.5
- first_shift: bfloat16 [768], P(('dp', 'seq')), may hold values from -3 to 3
- inner_weight: bfloat16 [768, 3072], P(('dp', 'seq')), may hold values from -0.21875 to 0.21875
- inner_bias: bfloat16 [3072], P(('dp', 'seq')), may hold values from -3 to 3
- outer_weight: bfloat16 [3072, 768], P(('dp', 'seq')), may hold values from -0.109375 to 0.109375
- outer_bias: bfloat16 [768], P(('dp', 'seq')), may hold values from -3 to 3
- second_gain: bfloat16 [768], P(('dp', 'seq')), may hold values from 0.5 to 1.5
- second_shift: bfloat16 [768], P(('dp', 'seq')), may hold values from -3 to 3
- cotangent: bfloat16 [32768, 768], P(('dp', 'seq')), may hold values from -6 to 6
- piece_start: int32 [16, 2], P('dp'), may hold values from 0 to 1792, as said below
- memory_pos: int32 [16, 20], P('dp'), may hold values from 0 to 2047, as said below
Outputs:
- layer_out: bfloat16 [32768, 768], P(('dp', 'seq'))
- grad_inputs: float32 [32768, 768], P(('dp', 'seq'))
- grad_query_weight: float32 [768, 768], P(('dp', 'seq'))
- grad_query_bias: float32 [768], P(('dp', 'seq'))
- grad_key_weight: float32 [768, 768], P(('dp', 'seq'))
- grad_value_weight: float32 [768, 768], P(('dp', 'seq'))
- grad_value_bias: float32 [768], P(('dp', 'seq'))
- grad_output_weight: float32 [768, 768], P(('dp', 'seq'))
- grad_output_bias: float32 [768], P(('dp', 'seq'))
- grad_first_gain: float32 [768], P(('dp', 'seq'))
- grad_first_shift: float32 [768], P(('dp', 'seq'))
- grad_inner_weight: float32 [768, 3072], P(('dp', 'seq'))
- grad_inner_bias: float32 [3072], P(('dp', 'seq'))
- grad_outer_weight: float32 [3072, 768], P(('dp', 'seq'))
- grad_outer_bias: float32 [768], P(('dp', 'seq'))
- grad_second_gain: float32 [768], P(('dp', 'seq'))
- grad_second_shift: float32 [768], P(('dp', 'seq'))
The draws below stay inside these ranges and needn't reach their ends.
Inputs may be any that keep to these rules, and one draw needn't show every extreme that they name: `piece_start`: in each sequence the 2 pieces, each of 256 positions, are in ascending order and do not intersect. `memory_pos`: the 20 positions of a sequence are distinct; the first 10 are read memory rows, the last 10 write memory rows.
All inputs are finite; a program needn't handle non-finite values.
Results may differ from the reference program's by a relative error of at most 0.035.
Values may be sent and summed in bfloat16 or wider, within the bound.
No kernel may reach another device: no remote copies, remote signals or barrier semaphores. Data moves between devices by JAX's collectives and lax.ppermute only.
A program may use at most 256 MiB of HBM per device.

```python
import jax
import jax.numpy as jnp
from jax import lax

D = 768
H = 12
HD = 64
FF = 3072
LEN = 2048
SEQG = 1
PIC = 256
NPIC = 2
MEM = 10
SEQS = 16
TOKENS = 32768
N_DP = 16


def draw_piece_start(key, part):
    piece_span = LEN // NPIC
    shifts = jax.random.randint(key, (SEQS, NPIC), 0, piece_span - PIC + 1, dtype=jnp.int32)
    shifts = shifts.at[0, 0].set(0)
    shifts = shifts.at[0, NPIC - 1].set(piece_span - PIC)
    return jnp.arange(NPIC, dtype=jnp.int32)[None, :] * piece_span + shifts


def draw_memory_pos(key, part):
    row_keys = jax.random.split(key, SEQS)

    def one_row(single):
        return jax.random.permutation(single, LEN - 2)[:2 * MEM].astype(jnp.int32) + 1
    chosen = jax.vmap(one_row)(row_keys)
    chosen = chosen.at[0, 0].set(0)
    chosen = chosen.at[0, 2 * MEM - 1].set(LEN - 1)
    return chosen


def with_spikes(values, key, source, target, parts, factor):
    owner, partner = [(jnp.arange(values.shape[dim]) // (values.shape[dim] // parts)).reshape([-1 if axis == dim else 1 for axis in range(values.ndim)]) for dim in (source, target)]
    chosen = jax.random.permutation(key, parts)[partner]
    strong = (owner == chosen) | (owner == (partner + parts // 2) % parts)
    return jnp.where(strong, factor * values, values)


def level_of(own_key, shape, shards, low, high):
    level = 1.0
    for axis_at, blocks in shards:
        draws = jax.random.uniform(jax.random.fold_in(jax.random.fold_in(own_key, 6), axis_at), (blocks,), jnp.float32, low / len(shards), high / len(shards))
        level = level * jnp.repeat(jnp.exp(draws), shape[axis_at] // blocks).reshape((-1,) + (1,) * (len(shape) - 1 - axis_at))
    return level


def noise(own_key, shape, deviation, most, pieces=(), held_as=jnp.bfloat16):
    entries = deviation * jax.random.normal(own_key, shape, jnp.float32)
    if pieces:
        entries = entries * level_of(own_key, shape, pieces, -0.22, 0.18)
    return jnp.clip(entries, -most, most).astype(held_as)


def bell_draw_with(own_key, extent, scale, most, pieces, heavy, kind=jnp.bfloat16):
    array = scale * jax.random.normal(own_key, extent, jnp.float32)
    if pieces:
        array = array * level_of(own_key, extent, pieces, -0.22, 0.18)
    return jnp.clip(with_spikes(array, jax.random.fold_in(own_key, 3), *heavy), -most, most).astype(kind)


def setup_inputs(seed: int = 0) -> dict:
    splits = jax.random.split(jax.random.key(seed), 20)
    inputs = bell_draw_with(splits[0], (TOKENS, D), 1.0, 6.0, ((0, 32),), (0, 1, 32, 2.75))
    query_weight = noise(splits[1], (D, D), D ** -0.5, 0.21875, ((0, 32),))
    query_bias = noise(splits[2], (D,), 0.5, 3.0, ((0, 32),))
    key_weight = noise(splits[3], (D, D), D ** -0.5, 0.21875, ((0, 32),))
    value_weight = noise(splits[4], (D, D), D ** -0.5, 0.21875, ((0, 32),))
    value_bias = noise(splits[5], (D,), 0.5, 3.0, ((0, 32),))
    output_weight = noise(splits[6], (D, D), (max(1, D // 64)) ** -0.5, 1.75, ((0, 32),))
    output_bias = noise(splits[7], (D,), 0.5, 3.0, ((0, 32),))
    first_gain = jnp.clip(1.0 + 0.1 * jax.random.normal(splits[8], (D,), jnp.float32), 0.5, 1.5).astype(jnp.bfloat16)
    first_shift = noise(splits[9], (D,), 0.5, 3.0, ((0, 32),))
    inner_weight = noise(splits[10], (D, FF), D ** -0.5, 0.21875, ((0, 32),))
    inner_bias = noise(splits[11], (FF,), 0.5, 3.0, ((0, 32),))
    outer_weight = noise(splits[12], (FF, D), FF ** -0.5, 0.109375, ((0, 32),))
    outer_bias = noise(splits[13], (D,), 0.5, 3.0, ((0, 32),))
    second_gain = jnp.clip(1.0 + 0.1 * jax.random.normal(splits[14], (D,), jnp.float32), 0.5, 1.5).astype(jnp.bfloat16)
    second_shift = noise(splits[15], (D,), 0.5, 3.0, ((0, 32),))
    cotangent = bell_draw_with(splits[16], (TOKENS, D), 1.0, 6.0, ((0, 32),), (0, 1, 32, 2.75))
    piece_start = draw_piece_start(jax.random.fold_in(splits[19], 71), 0)
    memory_pos = draw_memory_pos(jax.random.fold_in(splits[19], 71), 0)
    return {"inputs": inputs, "query_weight": query_weight, "query_bias": query_bias, "key_weight": key_weight, "value_weight": value_weight, "value_bias": value_bias, "output_weight": output_weight, "output_bias": output_bias, "first_gain": first_gain, "first_shift": first_shift, "inner_weight": inner_weight, "inner_bias": inner_bias, "outer_weight": outer_weight, "outer_bias": outer_bias, "second_gain": second_gain, "second_shift": second_shift, "cotangent": cotangent, "piece_start": piece_start, "memory_pos": memory_pos}


@jax.custom_vjp
def low(v):
    return lax.optimization_barrier(v.astype(jnp.bfloat16)).astype(jnp.float32)

@jax.custom_vjp
def low_back(v):
    return v

def low_keep(v):
    return (low(v), None)

def low_pass(kept, grad):
    return (grad,)

def back_keep(v):
    return (v, None)

def back_low(kept, grad):
    return (low(grad),)
low.defvjp(low_keep, low_pass)
low_back.defvjp(back_keep, back_low)
norm_epsilon = 1e-05
masked_score = -1e+30
highest = lax.Precision.HIGHEST

def dense(left, right):
    return jnp.dot(left, right, precision=highest)

def normalize(values, gain, shift):
    centre = lax.optimization_barrier(jnp.mean(values, -1, keepdims=True))
    centred = values - centre
    spread = lax.optimization_barrier(jnp.mean(centred * centred, -1, keepdims=True))
    return centred * lax.rsqrt(spread + norm_epsilon) * gain + shift

def gelu_exact(values):
    return jax.nn.gelu(values, approximate=False)

def visible(positions, starts, memories):
    columns = jnp.arange(LEN, dtype=jnp.int32)
    labels = jnp.arange(NPIC, dtype=jnp.int32)[:, None] + 1
    in_cols = (columns[None, :] >= starts[:, None]) & (columns[None, :] < starts[:, None] + PIC)
    in_rows = (positions[None, :] >= starts[:, None]) & (positions[None, :] < starts[:, None] + PIC)
    piece_cols = lax.optimization_barrier(jnp.sum(jnp.where(in_cols, labels, 0), 0))
    piece_rows = lax.optimization_barrier(jnp.sum(jnp.where(in_rows, labels, 0), 0))
    same_piece = (piece_rows[:, None] == piece_cols[None, :]) & (piece_rows[:, None] > 0)
    read_cols = jnp.any(columns[None, :] == memories[:MEM, None], 0)
    write_rows = jnp.any(positions[None, :] == memories[MEM:, None], 0)
    causal = columns[None, :] <= positions[:, None]
    return causal | same_piece | read_cols[None, :] | write_rows[:, None]

def attend_block(block_index, query, keys, values, starts, memories):
    block_rows = min(512, LEN)
    positions = block_index * block_rows + jnp.arange(block_rows, dtype=jnp.int32)
    block_query = lax.dynamic_slice_in_dim(query, block_index * block_rows, block_rows, 0).reshape(block_rows, H, HD)
    scores = jnp.einsum('qhd,khd->hqk', block_query, keys.reshape(LEN, H, HD), precision=highest) * HD ** (-0.5)
    scores = low_back(scores)
    allowed = visible(positions, starts, memories)
    scores = jnp.where(allowed[None], scores, masked_score)
    chances = low(jax.nn.softmax(scores, axis=-1))
    blended = jnp.einsum('hqk,khd->qhd', chances, values.reshape(LEN, H, HD), precision=highest)
    return blended.reshape(block_rows, H * HD)

def attend_sequence(query, keys, values, starts, memories):
    block_rows = min(512, LEN)
    blockwise = jax.checkpoint(attend_block)

    def scan_step(carry, block_index):
        return (carry, blockwise(block_index, query, keys, values, starts, memories))
    unused, blocks = lax.scan(scan_step, jnp.zeros((), jnp.float32), jnp.arange(LEN // block_rows, dtype=jnp.int32))
    return blocks.reshape(LEN, H * HD)

def layer(params, features, starts, memories):
    w_query, b_query, w_key, w_value, b_value, w_output, b_output, g_first, s_first, w_inner, b_inner, w_outer, b_outer, g_second, s_second = params
    query = low(low_back(dense(features, w_query)) + b_query)
    keys = low(low_back(dense(features, w_key)))
    values = low(low_back(dense(features, w_value)) + b_value)
    shaped = (query.reshape(SEQG, LEN, D), keys.reshape(SEQG, LEN, D), values.reshape(SEQG, LEN, D), starts, memories)
    attended = lax.map(lambda bundle: attend_sequence(*bundle), shaped).reshape(SEQG * LEN, D)
    attended = low(low_back(attended))
    mixed = features + low_back(dense(attended, w_output)) + b_output
    hidden_norm = normalize(mixed, g_first, s_first)
    inner = low_back(dense(low(hidden_norm), w_inner)) + b_inner
    activated = low(gelu_exact(inner))
    second_in = hidden_norm + low_back(dense(activated, w_outer)) + b_outer
    return normalize(second_in, g_second, s_second)

def reference(inputs, query_weight, query_bias, key_weight, value_weight, value_bias, output_weight, output_bias, first_gain, first_shift, inner_weight, inner_bias, outer_weight, outer_bias, second_gain, second_shift, cotangent, piece_start, memory_pos):
    params = tuple((weight.astype(jnp.float32) for weight in (query_weight, query_bias, key_weight, value_weight, value_bias, output_weight, output_bias, first_gain, first_shift, inner_weight, inner_bias, outer_weight, outer_bias, second_gain, second_shift)))
    features = inputs.astype(jnp.float32).reshape(N_DP, SEQG * LEN, D)
    cotangents = cotangent.astype(jnp.float32).reshape(N_DP, SEQG * LEN, D)
    starts = piece_start.reshape(N_DP, SEQG, NPIC)
    memories = memory_pos.reshape(N_DP, SEQG, 2 * MEM)

    def group_step(totals, bundle):
        feature, grad_out, start_rows, memory_rows = bundle
        result, pullback = jax.vjp(lambda weights, rows_in: layer(weights, rows_in, start_rows, memory_rows), params, feature)
        weight_grads, input_grad = pullback(grad_out)
        totals = tuple((running + gradient for running, gradient in zip(totals, weight_grads)))
        return (totals, (result.astype(jnp.bfloat16), input_grad))
    initial = tuple((jnp.zeros_like(weight) for weight in params))
    totals, (results, input_grads) = lax.scan(group_step, initial, (features, cotangents, starts, memories))
    return (results.reshape(TOKENS, D), input_grads.reshape(TOKENS, D), totals[0], totals[1], totals[2], totals[3], totals[4], totals[5], totals[6], totals[7], totals[8], totals[9], totals[10], totals[11], totals[12], totals[13], totals[14])
```

```python
from functools import partial

import jax
import jax.numpy as jnp
from jax import lax
from jax.experimental import pallas as pl
from jax.experimental.pallas import tpu as pltpu
from jax.sharding import PartitionSpec as P


H = 12
HD = 64
LEN = 2048
PIC = 256
NPIC = 2
MEM = 10


norm_epsilon = 1e-05
masked_score = -1e30


def normalize(values, gain, shift):
    centre = jnp.mean(values, -1, keepdims=True)
    centred = values - centre
    spread = jnp.mean(centred * centred, -1, keepdims=True)
    return centred * lax.rsqrt(spread + norm_epsilon) * gain + shift


def gelu_exact(values):
    return jax.nn.gelu(values, approximate=False)


def visible_cols(positions, columns, starts, memories):
    labels = jnp.arange(NPIC, dtype=jnp.int32)[:, None] + 1
    in_cols = (columns[None, :] >= starts[:, None]) & (columns[None, :] < starts[:, None] + PIC)
    in_rows = (positions[None, :] >= starts[:, None]) & (positions[None, :] < starts[:, None] + PIC)
    piece_cols = jnp.sum(jnp.where(in_cols, labels, 0), 0)
    piece_rows = jnp.sum(jnp.where(in_rows, labels, 0), 0)
    same_piece = (piece_rows[:, None] == piece_cols[None, :]) & (piece_rows[:, None] > 0)
    read_cols = jnp.any(columns[None, :] == memories[:MEM, None], 0)
    write_rows = jnp.any(positions[None, :] == memories[MEM:, None], 0)
    causal = columns[None, :] <= positions[:, None]
    return causal | same_piece | read_cols[None, :] | write_rows[:, None]


def visible(positions, starts, memories):
    return visible_cols(positions, jnp.arange(LEN, dtype=jnp.int32), starts, memories)


def dense(left, right):
    return jnp.dot(left, right, preferred_element_type=jnp.float32)


def outer_product(left, right):
    return jnp.einsum("ta,tb->ab", left, right, preferred_element_type=jnp.float32)


def back_product(gradient, weight):
    return jnp.einsum("tb,ab->ta", gradient, weight, preferred_element_type=jnp.float32)


def body(
    inputs,
    query_weight,
    query_bias,
    key_weight,
    value_weight,
    value_bias,
    output_weight,
    output_bias,
    first_gain,
    first_shift,
    inner_weight,
    inner_bias,
    outer_weight,
    outer_bias,
    second_gain,
    second_shift,
    cotangent,
    piece_start,
    memory_pos,
):
    shards = (
        query_weight,
        key_weight,
        value_weight,
        output_weight,
        inner_weight,
        outer_weight,
        query_bias,
        value_bias,
        output_bias,
        first_gain,
        first_shift,
        inner_bias,
        outer_bias,
        second_gain,
        second_shift,
    )
    gathered = (
        lax.all_gather(shards[0], ("dp", "seq"), axis=0, tiled=True),
        lax.all_gather(shards[1], ("dp", "seq"), axis=0, tiled=True),
        lax.all_gather(shards[2], ("dp", "seq"), axis=0, tiled=True),
        lax.all_gather(shards[3], ("dp", "seq"), axis=0, tiled=True),
        lax.all_gather(shards[4], ("dp", "seq"), axis=0, tiled=True),
        lax.all_gather(shards[5], ("dp", "seq"), axis=0, tiled=True),
        lax.all_gather(shards[6], ("dp", "seq"), axis=0, tiled=True),
        lax.all_gather(shards[7], ("dp", "seq"), axis=0, tiled=True),
        lax.all_gather(shards[8], ("dp", "seq"), axis=0, tiled=True),
        lax.all_gather(shards[9], ("dp", "seq"), axis=0, tiled=True),
        lax.all_gather(shards[10], ("dp", "seq"), axis=0, tiled=True),
        lax.all_gather(shards[11], ("dp", "seq"), axis=0, tiled=True),
        lax.all_gather(shards[12], ("dp", "seq"), axis=0, tiled=True),
        lax.all_gather(shards[13], ("dp", "seq"), axis=0, tiled=True),
        lax.all_gather(shards[14], ("dp", "seq"), axis=0, tiled=True),
    )
    w_query, w_key, w_value, w_output, w_inner, w_outer = gathered[:6]
    vectors = [vector.astype(jnp.float32) for vector in gathered[6:]]
    b_query, b_value, b_output, g_first, s_first, b_inner, b_outer, g_second, s_second = vectors
    local_rows = inputs.shape[0]
    model_width = inputs.shape[1]
    score_scale = HD ** (-0.5)
    pair_count = H // 2
    pair_width = 2 * HD
    block_rows = min(512, local_rows, LEN)
    block_count = local_rows // block_rows
    first_row = lax.axis_index("seq") * local_rows
    query_low = (dense(inputs, w_query) + b_query).astype(jnp.bfloat16)
    key_low = dense(inputs, w_key).astype(jnp.bfloat16)
    value_low = (dense(inputs, w_value) + b_value).astype(jnp.bfloat16)
    group_keys, group_values = (
        lax.all_gather(key_low, "seq", axis=0, tiled=True),
        lax.all_gather(value_low, "seq", axis=0, tiled=True),
    )
    group_rows = group_keys.shape[0]

    def context(block_index):
        row_start = first_row + block_index * block_rows
        seq_index = row_start // LEN
        positions = row_start - seq_index * LEN + jnp.arange(block_rows, dtype=jnp.int32)
        starts = piece_start[0]
        memories = memory_pos[0]
        allowed = visible(positions, starts, memories)
        return (seq_index, allowed, group_keys, group_values)

    def pair_part(matrix, pair_index, count):
        return lax.dynamic_slice_in_dim(matrix, pair_index * pair_width, pair_width, 1).reshape(
            count, 2, HD
        )

    def pair_scores(query_pair, key_pair, allowed):
        raw = (
            jnp.einsum("qhd,khd->hqk", query_pair, key_pair, preferred_element_type=jnp.float32)
            * score_scale
        )
        return jnp.where(allowed[None], raw, masked_score)

    def forward_block(block_index):
        seq_index, allowed, seq_keys, seq_values = context(block_index)
        block_query = lax.dynamic_slice_in_dim(query_low, block_index * block_rows, block_rows, 0)

        def forward_pair_step(carry, pair_index):
            out_buffer, total_buffer = carry
            query_pair = pair_part(block_query, pair_index, block_rows)
            key_pair = pair_part(seq_keys, pair_index, LEN)
            value_pair = pair_part(seq_values, pair_index, LEN)
            scores = pair_scores(query_pair, key_pair, allowed)
            peak = jnp.max(scores, -1, keepdims=True)
            expo_terms = jnp.exp(scores - peak)
            row_sum = jnp.sum(expo_terms, -1, keepdims=True)
            chances_low = (expo_terms / row_sum).astype(jnp.bfloat16)
            blended = jnp.einsum(
                "hqk,khd->qhd", chances_low, value_pair, preferred_element_type=jnp.float32
            )
            blended = blended.reshape(block_rows, pair_width).astype(jnp.bfloat16)
            out_buffer = lax.dynamic_update_slice_in_dim(
                out_buffer, blended, pair_index * pair_width, 1
            )
            log_pair = (peak + jnp.log(row_sum))[:, :, 0]
            total_buffer = lax.dynamic_update_slice_in_dim(
                total_buffer, log_pair, pair_index * 2, 0
            )
            return ((out_buffer, total_buffer), None)

        initial = (
            jnp.zeros((block_rows, model_width), jnp.bfloat16),
            jnp.zeros((H, block_rows), jnp.float32),
        )
        (out_buffer, total_buffer), unused = lax.scan(
            forward_pair_step, initial, jnp.arange(pair_count)
        )
        return (out_buffer, total_buffer)

    attended_blocks, log_totals = lax.map(forward_block, jnp.arange(block_count))
    attended = attended_blocks.reshape(local_rows, model_width)
    mixed = inputs.astype(jnp.float32) + dense(attended, w_output) + b_output
    hidden_norm, first_pull = jax.vjp(normalize, mixed, g_first, s_first)
    hidden_low = hidden_norm.astype(jnp.bfloat16)
    inner = dense(hidden_low, w_inner) + b_inner
    activated_full, gelu_pull = jax.vjp(gelu_exact, inner)
    activated = activated_full.astype(jnp.bfloat16)
    second_in = hidden_norm + dense(activated, w_outer) + b_outer
    normed_out, second_pull = jax.vjp(normalize, second_in, g_second, s_second)
    layer_out = normed_out.astype(jnp.bfloat16)
    back_weights = (
        lax.all_gather(query_weight, ("dp", "seq"), axis=0, tiled=True),
        lax.all_gather(key_weight, ("dp", "seq"), axis=0, tiled=True),
        lax.all_gather(value_weight, ("dp", "seq"), axis=0, tiled=True),
        lax.all_gather(output_weight, ("dp", "seq"), axis=0, tiled=True),
        lax.all_gather(inner_weight, ("dp", "seq"), axis=0, tiled=True),
        lax.all_gather(outer_weight, ("dp", "seq"), axis=0, tiled=True),
    )
    v_query, v_key, v_value, v_output, v_inner, v_outer = back_weights
    grad_second_in, grad_second_gain, grad_second_shift = second_pull(cotangent.astype(jnp.float32))
    grad_outer_bias = jnp.sum(grad_second_in, 0)
    second_low = grad_second_in.astype(jnp.bfloat16)
    grad_outer_weight = outer_product(activated, second_low)
    (grad_inner,) = gelu_pull(back_product(second_low, v_outer))
    grad_inner_bias = jnp.sum(grad_inner, 0)
    inner_low = grad_inner.astype(jnp.bfloat16)
    grad_inner_weight = outer_product(hidden_low, inner_low)
    grad_hidden = grad_second_in + back_product(inner_low, v_inner)
    grad_mixed, grad_first_gain, grad_first_shift = first_pull(grad_hidden)
    grad_output_bias = jnp.sum(grad_mixed, 0)
    mixed_low = grad_mixed.astype(jnp.bfloat16)
    grad_output_weight = outer_product(attended, mixed_low)
    grad_attended = back_product(mixed_low, v_output).astype(jnp.bfloat16)

    def backward_block(carry, block_index, with_keys):
        seq_index, allowed, seq_keys, seq_values = context(block_index)
        block_query = lax.dynamic_slice_in_dim(query_low, block_index * block_rows, block_rows, 0)
        block_grad = lax.dynamic_slice_in_dim(
            grad_attended, block_index * block_rows, block_rows, 0
        )
        block_total = log_totals[block_index]

        def backward_pair_step(inner_carry, pair_index):
            query_grad, term_buffer = (inner_carry[0], inner_carry[1])
            query_pair = pair_part(block_query, pair_index, block_rows)
            key_pair = pair_part(seq_keys, pair_index, LEN)
            value_pair = pair_part(seq_values, pair_index, LEN)
            grad_pair = pair_part(block_grad, pair_index, block_rows)
            scores = pair_scores(query_pair, key_pair, allowed)
            total_pair = lax.dynamic_slice_in_dim(block_total, pair_index * 2, 2, 0)
            chances = jnp.exp(scores - total_pair[:, :, None])
            chance_grad = jnp.einsum(
                "qhd,khd->hqk", grad_pair, value_pair, preferred_element_type=jnp.float32
            )
            row_terms = jnp.sum(chances * chance_grad, -1, keepdims=True)
            score_grad = (chances * (chance_grad - row_terms)).astype(jnp.bfloat16)
            query_part = jnp.einsum(
                "hqk,khd->qhd", score_grad, key_pair, preferred_element_type=jnp.float32
            )
            query_part = query_part.reshape(block_rows, pair_width) * score_scale
            query_grad = lax.dynamic_update_slice_in_dim(
                query_grad, query_part, pair_index * pair_width, 1
            )
            term_buffer = lax.dynamic_update_slice_in_dim(
                term_buffer, row_terms[:, :, 0], pair_index * 2, 0
            )
            seq_key_grad, seq_value_grad = (inner_carry[2], inner_carry[3])
            chances_low = chances.astype(jnp.bfloat16)
            key_part = jnp.einsum(
                "hqk,qhd->khd", score_grad, query_pair, preferred_element_type=jnp.float32
            )
            value_part = jnp.einsum(
                "hqk,qhd->khd", chances_low, grad_pair, preferred_element_type=jnp.float32
            )
            key_part = key_part.reshape(LEN, pair_width) * score_scale
            value_part = value_part.reshape(LEN, pair_width)
            seq_key_grad = lax.dynamic_update_slice_in_dim(
                seq_key_grad, key_part, pair_index * pair_width, 1
            )
            seq_value_grad = lax.dynamic_update_slice_in_dim(
                seq_value_grad, value_part, pair_index * pair_width, 1
            )
            return ((query_grad, term_buffer, seq_key_grad, seq_value_grad), None)

        initial = (
            jnp.zeros((block_rows, model_width), jnp.float32),
            jnp.zeros((H, block_rows), jnp.float32),
        )
        initial = initial + (
            jnp.zeros((LEN, model_width), jnp.float32),
            jnp.zeros((LEN, model_width), jnp.float32),
        )
        finals, unused = lax.scan(backward_pair_step, initial, jnp.arange(pair_count))
        key_grads, value_grads = carry
        key_grads = key_grads + finals[2]
        value_grads = value_grads + finals[3]
        carry = (key_grads, value_grads)
        return (carry, (finals[0], finals[1]))

    group_zero = jnp.zeros((group_rows, model_width), jnp.float32)
    (key_grads, value_grads), (query_blocks, term_blocks) = lax.scan(
        partial(backward_block, with_keys=True), (group_zero, group_zero), jnp.arange(block_count)
    )
    key_sum, value_sum = (
        lax.psum_scatter(
            key_grads.astype(jnp.bfloat16), "seq", scatter_dimension=0, tiled=True
        ).astype(jnp.float32),
        lax.psum_scatter(
            value_grads.astype(jnp.bfloat16), "seq", scatter_dimension=0, tiled=True
        ).astype(jnp.float32),
    )
    query_sum = query_blocks.reshape(local_rows, model_width)
    grad_query_bias = jnp.sum(query_sum, 0)
    grad_value_bias = jnp.sum(value_sum, 0)
    query_grad_low = query_sum.astype(jnp.bfloat16)
    key_grad_low = key_sum.astype(jnp.bfloat16)
    value_grad_low = value_sum.astype(jnp.bfloat16)
    grad_query_weight = outer_product(inputs, query_grad_low)
    grad_key_weight = outer_product(inputs, key_grad_low)
    grad_value_weight = outer_product(inputs, value_grad_low)
    grad_inputs = (
        grad_mixed
        + back_product(query_grad_low, v_query)
        + back_product(key_grad_low, v_key)
        + back_product(value_grad_low, v_value)
    )
    grads = (
        grad_query_weight,
        grad_key_weight,
        grad_value_weight,
        grad_output_weight,
        grad_inner_weight,
        grad_outer_weight,
        grad_query_bias,
        grad_value_bias,
        grad_output_bias,
        grad_first_gain,
        grad_first_shift,
        grad_inner_bias,
        grad_outer_bias,
        grad_second_gain,
        grad_second_shift,
    )
    owned = (
        lax.psum_scatter(grads[0], ("dp", "seq"), scatter_dimension=0, tiled=True),
        lax.psum_scatter(grads[1], ("dp", "seq"), scatter_dimension=0, tiled=True),
        lax.psum_scatter(grads[2], ("dp", "seq"), scatter_dimension=0, tiled=True),
        lax.psum_scatter(grads[3], ("dp", "seq"), scatter_dimension=0, tiled=True),
        lax.psum_scatter(grads[4], ("dp", "seq"), scatter_dimension=0, tiled=True),
        lax.psum_scatter(grads[5], ("dp", "seq"), scatter_dimension=0, tiled=True),
        lax.psum_scatter(grads[6], ("dp", "seq"), scatter_dimension=0, tiled=True),
        lax.psum_scatter(grads[7], ("dp", "seq"), scatter_dimension=0, tiled=True),
        lax.psum_scatter(grads[8], ("dp", "seq"), scatter_dimension=0, tiled=True),
        lax.psum_scatter(grads[9], ("dp", "seq"), scatter_dimension=0, tiled=True),
        lax.psum_scatter(grads[10], ("dp", "seq"), scatter_dimension=0, tiled=True),
        lax.psum_scatter(grads[11], ("dp", "seq"), scatter_dimension=0, tiled=True),
        lax.psum_scatter(grads[12], ("dp", "seq"), scatter_dimension=0, tiled=True),
        lax.psum_scatter(grads[13], ("dp", "seq"), scatter_dimension=0, tiled=True),
        lax.psum_scatter(grads[14], ("dp", "seq"), scatter_dimension=0, tiled=True),
    )
    return (
        layer_out,
        grad_inputs,
        owned[0],
        owned[6],
        owned[1],
        owned[2],
        owned[7],
        owned[3],
        owned[8],
        owned[9],
        owned[10],
        owned[4],
        owned[11],
        owned[5],
        owned[12],
        owned[13],
        owned[14],
    )


F32=jnp.float32; BF=jnp.bfloat16
NT=(((1,),(1,)),((),()))
NN=(((1,),(0,)),((),()))
TN=(((0,),(0,)),((),()))
def mm(a,b,dims=NN):
    return lax.dot_general(a,b,dims,preferred_element_type=F32)
GROUP=16

def half_mask(shape, head, dim):
    lanes=lax.broadcasted_iota(jnp.int32,shape,dim)
    return (lanes<64) if head==0 else (lanes>=64)

def only(x, head):
    return jnp.where(half_mask(x.shape,head,1),x,jnp.zeros_like(x))

def take_rows(ref, pos_ref, first):
    width=ref.shape[1]
    out=jnp.zeros((GROUP,width),F32)
    rows=lax.broadcasted_iota(jnp.int32,(GROUP,width),0)
    for m in range(MEM):
        pos=pos_ref[first+m]
        start=pl.multiple_of((pos//GROUP)*GROUP,GROUP)
        part=ref[pl.ds(start,GROUP),:].astype(F32)
        row=jnp.sum(jnp.where(rows==pos-start,part,0.0),0,keepdims=True)
        out=jnp.where(rows==m,row,out)
    return out.astype(BF)

def put_rows(ref, pos_ref, first, values, add):
    width=ref.shape[1]
    rows=lax.broadcasted_iota(jnp.int32,(GROUP,width),0)
    for m in range(MEM):
        pos=pos_ref[first+m]
        start=pl.multiple_of((pos//GROUP)*GROUP,GROUP)
        old=ref[pl.ds(start,GROUP),:].astype(F32)
        row=values[m:m+1,:]
        new=jnp.where(rows==pos-start,old+row if add else row,old)
        ref[pl.ds(start,GROUP),:]=new.astype(ref.dtype)


def transposed(x):
    return jnp.transpose(x.astype(F32)).astype(BF)

def fwd_kernel(pos_ref, posv_ref, limit_ref, write_ref, qkv_ref, o_ref, lse_ref, vt_ref, qt_ref, acc_ref, *, bq, np_, qb0, qb1):
    rows_all=qkv_ref.shape[0]
    nq=rows_all//bq
    W=np_*128
    nh=2*np_
    cols=lambda part,p:slice(part*W+p*128,part*W+p*128+128)
    hr=lambda h:slice(80*h,80*h+80)
    mem=take_rows(qkv_ref,pos_ref,0)
    kr=[only(mem[:,cols(1,h//2)],h%2) for h in range(nh)]
    ones16=jnp.ones((16,GROUP),BF)
    vrt=[]
    for p in range(np_):
        vt=transposed(qkv_ref[:,cols(2,p)])
        mt=transposed(mem[:,cols(2,p)])
        qt_ref[p*128:p*128+128,:]=transposed(qkv_ref[:,cols(0,p)])
        for h in range(2):
            vt_ref[80*(2*p+h):80*(2*p+h)+64,:]=vt[64*h:64*h+64]
            vt_ref[80*(2*p+h)+64:80*(2*p+h)+80,:]=jnp.ones((16,rows_all),BF)
            vrt.append(jnp.concatenate([mt[64*h:64*h+64],ones16],0))
    read_pos=posv_ref[...]
    def q_step(qb, unused):
        q0=pl.multiple_of(qb*bq,bq)
        limit=limit_ref[:,pl.ds(q0,bq)][0:1]
        key_iota=lax.broadcasted_iota(jnp.int32,(bq,bq),0)
        zq=jnp.zeros((64,bq),BF)
        def qh(h):
            own=qt_ref[64*h:64*h+64,pl.ds(q0,bq)]
            return jnp.concatenate([own,zq] if h%2==0 else [zq,own],0)
        def soft(h,s,vt,m):
            m2=jnp.maximum(m,jnp.max(s,0,keepdims=True))
            fix=jnp.exp2(m-m2)
            p=jnp.exp2(s-m2)
            acc_ref[hr(h),:]=acc_ref[hr(h),:]*fix+mm(vt,p.astype(BF))
            return m2
        def block(kb,carry,mask):
            k0=pl.multiple_of(kb*bq,bq)
            ss=[mm(qkv_ref[pl.ds(k0,bq),cols(1,h//2)],qh(h)) for h in range(nh)]
            if mask:
                ss=[jnp.where(key_iota+k0<=limit,s,masked_score) for s in ss]
            return tuple(soft(h,ss[h],vt_ref[hr(h),pl.ds(k0,bq)],carry[h]) for h in range(nh))
        acc_ref[...]=jnp.zeros_like(acc_ref)
        carry=tuple(jnp.full((1,bq),masked_score,F32) for _ in range(nh))
        carry=block(qb,carry,True)
        carry=tuple(soft(h,jnp.where(read_pos>limit,mm(kr[h],qh(h)),masked_score),vrt[h],carry[h]) for h in range(nh))
        carry=lax.fori_loop(0,qb,lambda kb,c:block(kb,c,False),carry)
        far=jnp.max(limit)>=q0+bq
        carry=lax.cond(far,lambda c:block(jnp.minimum(qb+1,nq-1),c,True),lambda c:c,carry)
        wr=write_ref[:,pl.ds(q0,bq)][0:1]
        outs=[]
        for h in range(nh):
            l=acc_ref[80*h+64:80*h+65,:]
            outs.append(acc_ref[80*h:80*h+64,:]/l)
            lse=carry[h]+jnp.log2(l)
            lse_ref[h:h+1,pl.ds(q0,bq)]=jnp.where(wr>0,1e30,lse)
        o_ref[pl.ds(q0,bq),:]=jnp.transpose(jnp.concatenate(outs,0)).astype(BF)
        return unused
    lax.fori_loop(qb0,qb1,q_step,0)
    rows=take_rows(qkv_ref,pos_ref,MEM)
    out=[]
    for p in range(np_):
        total=jnp.zeros((GROUP,128),F32)
        qw=rows[:,cols(0,p)]
        for h in range(2):
            s=mm(only(qw,h),qkv_ref[:,cols(1,p)],NT)
            m=jnp.max(s,1,keepdims=True)
            e=jnp.exp2(s-m)
            l=jnp.sum(e,1,keepdims=True)
            ow=mm(e.astype(BF),qkv_ref[:,cols(2,p)])/l
            total=total+jnp.where(half_mask((GROUP,128),h,1),ow,0.0)
        out.append(total)
    put_rows(o_ref,pos_ref,MEM,jnp.concatenate(out,1),False)

LN2=0.6931471805599453
def bwd_kernel(pos_ref, posv_ref, limit_ref, qkv_ref, do_ref, o_ref, lse_ref,
               dqkv_ref, bias_ref, qt_ref, kt_ref, dot_ref, dk_acc, dv_acc, dq_acc, dr_acc, *, bq, scale, np_):
    rows_all=qkv_ref.shape[0]
    nq=rows_all//bq
    W=np_*128
    nh=2*np_
    cols=lambda part,p:slice(part*W+p*128,part*W+p*128+128)
    pc=lambda p:slice(p*128,p*128+128)
    hr=lambda h:slice(64*h,64*h+64)
    for p in range(np_):
        qt_ref[pc(p),:]=transposed(qkv_ref[:,cols(0,p)])
        kt_ref[pc(p),:]=transposed(qkv_ref[:,cols(1,p)])
        dot_ref[pc(p),:]=transposed(do_ref[:,pc(p)])
    mem=take_rows(qkv_ref,pos_ref,0)
    kr=[mem[:,cols(1,p)] for p in range(np_)]
    vr=[mem[:,cols(2,p)] for p in range(np_)]
    krt=[transposed(kr[p]) for p in range(np_)]
    read_pos=posv_ref[...]
    rows=take_rows(qkv_ref,pos_ref,MEM)
    dow_all=take_rows(do_ref,pos_ref,MEM)
    valid=lax.broadcasted_iota(jnp.int32,(GROUP,1),0)<MEM
    dqw_all=[]
    for pr in range(np_):
        qw=rows[:,cols(0,pr)]
        dow=dow_all[:,pc(pr)]
        qwt=transposed(qw); dowt=transposed(dow)
        dqw=jnp.zeros((GROUP,128),F32)
        for h in range(2):
            s=mm(only(qw,h),qkv_ref[:,cols(1,pr)],NT)
            m=jnp.max(s,1,keepdims=True)
            p=jnp.exp2(s-m)
            p=p*jnp.where(valid,1.0/jnp.sum(p,1,keepdims=True),0.0)
            dp=mm(only(dow,h),qkv_ref[:,cols(2,pr)],NT)
            ds=(p*(dp-jnp.sum(p*dp,1,keepdims=True))).astype(BF)
            dqw=dqw+jnp.where(half_mask((GROUP,128),h,1),mm(ds,qkv_ref[:,cols(1,pr)]),0.0)
            dk_acc[hr(2*pr+h),:]=mm(qwt[64*h:64*h+64],ds)
            dv_acc[hr(2*pr+h),:]=mm(dowt[64*h:64*h+64],p.astype(BF))
        dqw_all.append(dqw)
    dr_acc[...]=jnp.zeros_like(dr_acc)
    def q_step(qb, unused):
        q0=pl.multiple_of(qb*bq,bq)
        limit=limit_ref[:,pl.ds(q0,bq)][0:1]
        zq=jnp.zeros((64,bq),BF)
        def padded(ref,h):
            own=ref[hr(h),pl.ds(q0,bq)]
            return jnp.concatenate([own,zq] if h%2==0 else [zq,own],0)
        prod=jnp.transpose(do_ref[pl.ds(q0,bq),:].astype(F32)*o_ref[pl.ds(q0,bq),:].astype(F32))
        delta=[jnp.sum(prod[hr(h)],0,keepdims=True) for h in range(nh)]
        lse=[lse_ref[h:h+1,pl.ds(q0,bq)] for h in range(nh)]
        key_iota=lax.broadcasted_iota(jnp.int32,(bq,bq),0)
        dq_acc[...]=jnp.zeros_like(dq_acc)
        def grads(h,s,v):
            p=jnp.exp2(s-lse[h])
            dp=mm(v,padded(dot_ref,h))
            return (p*(dp-delta[h])).astype(BF),p.astype(BF)
        def block(kb,mask):
            k0=pl.multiple_of(kb*bq,bq)
            ks=pl.ds(k0,bq)
            held={}
            def front(h):
                s=mm(qkv_ref[ks,cols(1,h//2)],padded(qt_ref,h))
                if mask:
                    s=jnp.where(key_iota+k0<=limit,s,masked_score)
                held[h]=(s,mm(qkv_ref[ks,cols(2,h//2)],padded(dot_ref,h)))
            def middle(h):
                s,dp=held[h]
                p=jnp.exp2(s-lse[h])
                held[h]=((p*(dp-delta[h])).astype(BF),p.astype(BF))
            def back(h):
                ds,p=held[h]
                dq_acc[hr(h),:]+=mm(kt_ref[hr(h),ks],ds)
                dk_acc[hr(h),ks]+=mm(qt_ref[hr(h),pl.ds(q0,bq)],ds,NT)
                dv_acc[hr(h),ks]+=mm(dot_ref[hr(h),pl.ds(q0,bq)],p,NT)
            for h in range(nh+2):
                if h<nh:
                    front(h)
                if 0<=h-1<nh:
                    middle(h-1)
                if h>=2:
                    back(h-2)
        block(qb,True)
        for h in range(nh):
            s=jnp.where(read_pos>limit,mm(kr[h//2],padded(qt_ref,h)),masked_score)
            ds,p=grads(h,s,vr[h//2])
            dr_acc[0,hr(h),:]+=mm(qt_ref[hr(h),pl.ds(q0,bq)],ds,NT)
            dr_acc[1,hr(h),:]+=mm(dot_ref[hr(h),pl.ds(q0,bq)],p,NT)
            dq_acc[hr(h),:]+=mm(krt[h//2][64*(h%2):64*(h%2)+64,:],ds)
        def step(kb,c):
            block(kb,False)
            return c
        lax.fori_loop(0,qb,step,0)
        @pl.when(jnp.max(limit)>=q0+bq)
        def _():
            block(jnp.minimum(qb+1,nq-1),True)
        dqkv_ref[pl.ds(q0,bq),0:W]=(jnp.transpose(dq_acc[...])*scale).astype(BF)
        return unused
    lax.fori_loop(0,nq,q_step,0)
    put_rows(dqkv_ref.at[:,0:W],pos_ref,MEM,jnp.concatenate(dqw_all,1)*scale,False)
    for p in range(np_):
        dqkv_ref[:,cols(1,p)]=(jnp.transpose(dk_acc[pc(p),:])*LN2).astype(BF)
        dqkv_ref[:,cols(2,p)]=jnp.transpose(dv_acc[pc(p),:]).astype(BF)
    put_rows(dqkv_ref.at[:,W:2*W],pos_ref,0,jnp.transpose(dr_acc[0])*LN2,True)
    put_rows(dqkv_ref.at[:,2*W:3*W],pos_ref,0,jnp.transpose(dr_acc[1]),True)
    rows8=lax.broadcasted_iota(jnp.int32,(8,W),0)
    bq_sum=jnp.sum(dqkv_ref[:,0:W].astype(F32),0,keepdims=True)
    bv_sum=jnp.sum(dqkv_ref[:,2*W:3*W].astype(F32),0,keepdims=True)
    bias_ref[...]=jnp.where(rows8==0,bq_sum,jnp.where(rows8==1,bv_sum,0.0))

ONCE=pl.Buffered(1)
def attn_fwd(qkv, pos, posv, limit, write, np_, bq=256, qb0=0, qb1=None):
    L=qkv.shape[0]; W=np_*128
    row8=pl.BlockSpec((8,L),lambda i:(0,0),pipeline_mode=ONCE)
    full=lambda w:pl.BlockSpec((L,w),lambda i:(0,0),pipeline_mode=ONCE)
    return pl.pallas_call(partial(fwd_kernel,bq=bq,np_=np_,qb0=qb0,qb1=L//bq if qb1 is None else qb1),
        grid=(1,),
        in_specs=[pl.BlockSpec(memory_space=pltpu.SMEM),pl.BlockSpec((GROUP,1),lambda i:(0,0)),row8,row8,full(3*W)],
        out_specs=[full(W),row8],
        out_shape=[jax.ShapeDtypeStruct((L,W),BF),jax.ShapeDtypeStruct((8,L),F32)],
        scratch_shapes=[pltpu.VMEM((np_*160,L),BF),pltpu.VMEM((W,L),BF),pltpu.VMEM((np_*160,bq),F32)],
        name="attn_fwd",
    )(pos,posv,limit,write,qkv)

def attn_bwd(qkv, pos, posv, limit, do, o, lse, np_, scale, bq=256):
    L=qkv.shape[0]; W=np_*128
    row8=pl.BlockSpec((8,L),lambda i:(0,0),pipeline_mode=ONCE)
    full=lambda w:pl.BlockSpec((L,w),lambda i:(0,0),pipeline_mode=ONCE)
    return pl.pallas_call(partial(bwd_kernel,bq=bq,scale=scale,np_=np_),
        grid=(1,),
        in_specs=[pl.BlockSpec(memory_space=pltpu.SMEM),pl.BlockSpec((GROUP,1),lambda i:(0,0)),row8,full(3*W),full(W),full(W),row8],
        out_specs=[full(3*W),pl.BlockSpec((8,W),lambda i:(0,0))],
        out_shape=[jax.ShapeDtypeStruct((L,3*W),BF),jax.ShapeDtypeStruct((8,W),F32)],
        scratch_shapes=[pltpu.VMEM((W,L),BF)]*3+[pltpu.VMEM((W,L),F32)]*2+[pltpu.VMEM((W,bq),F32),pltpu.VMEM((2,W,GROUP),F32)],
        name="attn_bwd",
    )(pos,posv,limit,qkv,do,o,lse)


LOG2E = 1.4426950408889634
ALL = ("dp", "seq")
RSQRT2 = 0.7071067811865476
RSQRT2PI = 0.3989422804014327


def bit_swap(x, axis, size, bit):
    return lax.ppermute(x, axis, [(i, i ^ bit) for i in range(size)])


def side(flag, own, peer, axis):
    low = jnp.where(flag, peer, own)
    high = jnp.where(flag, own, peer)
    return jnp.concatenate([low, high], axis)


def bits_of(size):
    out = []
    bit = 1
    while bit < size:
        out.append(bit)
        bit *= 2
    return out


def gather_dp(block, size):
    bits = bits_of(size)[::-1]
    index = lax.axis_index("dp")
    out = block
    for bit in bits:
        other = bit_swap(out, "dp", size, bit)
        up = (index & bit) != 0
        out = jnp.stack([jnp.where(up, other, out), jnp.where(up, out, other)])
    count = len(bits)
    out = out.transpose(tuple(range(count))[::-1] + tuple(range(count, out.ndim)))
    return out.reshape((size,) + block.shape)


def scatter_dp(blocks, size):
    index = lax.axis_index("dp")
    tail = blocks.shape[1:]
    rest = blocks
    for bit in bits_of(size):
        groups = rest.shape[0] // 2
        rest = rest.reshape((groups, 2) + tail)
        up = (index & bit) != 0
        give = jnp.where(up, rest[:, 0], rest[:, 1]).astype(BF)
        keep = jnp.where(up, rest[:, 1], rest[:, 0])
        rest = keep + bit_swap(give, "dp", size, bit).astype(F32)
    return rest[0]


def norm_parts(values):
    centre = jnp.mean(values, -1, keepdims=True)
    centred = values - centre
    spread = jnp.mean(centred * centred, -1, keepdims=True)
    factor = lax.rsqrt(spread + norm_epsilon)
    return centred * factor, factor


def norm_back(gradient, unit, factor):
    return factor * (
        gradient
        - jnp.mean(gradient, -1, keepdims=True)
        - unit * jnp.mean(gradient * unit, -1, keepdims=True)
    )


def fast_body(
    inputs,
    query_weight,
    query_bias,
    key_weight,
    value_weight,
    value_bias,
    output_weight,
    output_bias,
    first_gain,
    first_shift,
    inner_weight,
    inner_bias,
    outer_weight,
    outer_bias,
    second_gain,
    second_shift,
    cotangent,
    piece_start,
    memory_pos,
    *,
    n_dp,
):
    rows, width = inputs.shape
    inner_width = inner_weight.shape[1]
    devices = 2 * n_dp
    part = width // devices
    inner_part = inner_width // devices
    ratio = inner_width // width
    half = width // 2
    seq = lax.axis_index("seq")
    dp = lax.axis_index("dp")
    upper = seq == 1
    swap = lambda x: bit_swap(x, "seq", 2, 1)
    wide = inner_weight.reshape(part, ratio, width).transpose(1, 0, 2).reshape(ratio * part, width)
    packed = jnp.concatenate([output_weight, wide, outer_weight], 0)
    late = lax.all_gather(packed, ALL, axis=0, tiled=False)
    peer_inputs = swap(inputs)
    vectors = jnp.concatenate(
        [
            query_bias,
            value_bias,
            output_bias,
            first_gain,
            first_shift,
            outer_bias,
            second_gain,
            second_shift,
            inner_bias,
        ]
    )
    count = vectors.shape[0]
    three = jnp.stack([query_weight, key_weight, value_weight], 1)
    three = three.reshape(part, 3, 2, half)
    line = jnp.pad(vectors, (0, 3 * half - count))[None, :]
    line = jnp.pad(line, ((0, 7), (0, 0)))

    def columns(upper_half):
        kept = jnp.where(upper_half, three[:, :, 1], three[:, :, 0]).reshape(part, 3 * half)
        return jnp.concatenate([kept, line], 0)

    pair = side(upper, columns(upper)[None], swap(columns(jnp.logical_not(upper)))[None], 0)
    early = gather_dp(pair, n_dp).reshape(devices, part + 8, 3 * half)
    w_three = early[:, :part].reshape(width, 3 * half)
    lines = early[:, part, :count].astype(F32)
    vector = lambda k: lines[:, k * part : (k + 1) * part].reshape(width)
    b_query, b_value, b_output, g_first, s_first, b_outer, g_second, s_second = map(vector, range(8))
    b_inner = lines[:, 8 * part :].reshape(inner_width)
    own_half = lambda v: jnp.where(upper, v[half:], v[:half])
    features = side(upper, inputs, peer_inputs, 0)
    scale = HD ** (-0.5)
    shift = jnp.concatenate([own_half(b_query), jnp.zeros((half,), F32), own_half(b_value)])
    grow = jnp.concatenate([jnp.full((half,), scale * LOG2E, F32), jnp.ones((2 * half,), F32)])
    qkv = ((dense(features, w_three) + shift) * grow).astype(BF)
    positions = jnp.arange(2 * rows, dtype=jnp.int32)
    limit = positions
    for piece in range(NPIC):
        start = piece_start[0, piece]
        inside = (positions >= start) & (positions < start + PIC)
        limit = jnp.where(inside, start + PIC - 1, limit)
    memories = memory_pos[0]
    writes = jnp.any(positions[None, :] == memories[MEM:, None], 0).astype(jnp.int32)
    limit = jnp.broadcast_to(limit, (8, 2 * rows))
    writes = jnp.broadcast_to(writes, (8, 2 * rows))
    reads = jnp.pad(memories[:MEM], (0, GROUP - MEM), constant_values=-1)[:, None]
    pairs = half // (2 * HD)
    out_heads, totals = attn_fwd(qkv, memories, reads, limit, writes, pairs)
    other_rows = jnp.where(upper, out_heads[:rows], out_heads[rows:])
    own_rows = jnp.where(upper, out_heads[rows:], out_heads[:rows])
    attended = side(upper, own_rows, swap(other_rows), 1)
    w_output = late[:, :part].reshape(width, width)
    w_inner = (
        late[:, part : part + ratio * part]
        .reshape(devices, ratio, part, width)
        .transpose(0, 2, 1, 3)
        .reshape(width, inner_width)
    )
    w_outer = late[:, part + ratio * part :].reshape(inner_width, width)
    mixed = inputs.astype(F32) + dense(attended, w_output) + b_output
    first_unit, first_factor = norm_parts(mixed)
    hidden_norm = first_unit * g_first + s_first
    hidden_low = hidden_norm.astype(BF)
    inner = dense(hidden_low, w_inner) + b_inner
    chance = 0.5 * (1.0 + lax.erf(inner * RSQRT2))
    activated = (inner * chance).astype(BF)
    slope = (chance + inner * (RSQRT2PI * jnp.exp(-0.5 * inner * inner))).astype(BF)
    activated, slope = lax.optimization_barrier((activated, slope))
    second_in = hidden_norm + dense(activated, w_outer) + b_outer
    second_unit, second_factor = norm_parts(second_in)
    layer_out = (second_unit * g_second + s_second).astype(BF)
    cot = cotangent.astype(F32)
    grad_second_gain = jnp.sum(cot * second_unit, 0)
    grad_second_shift = jnp.sum(cot, 0)
    grad_second_in = norm_back(cot * g_second, second_unit, second_factor)
    grad_outer_bias = jnp.sum(grad_second_in, 0)
    second_low = grad_second_in.astype(BF)
    grad_inner = back_product(second_low, w_outer) * slope.astype(F32)
    grad_inner_bias = jnp.sum(grad_inner, 0)
    inner_low = grad_inner.astype(BF)
    grad_hidden = grad_second_in + back_product(inner_low, w_inner)
    grad_first_gain = jnp.sum(grad_hidden * first_unit, 0)
    grad_first_shift = jnp.sum(grad_hidden, 0)
    grad_mixed = norm_back(grad_hidden * g_first, first_unit, first_factor)
    grad_output_bias = jnp.sum(grad_mixed, 0)
    mixed_low = grad_mixed.astype(BF)
    grad_attended = back_product(mixed_low, w_output).astype(BF)
    grad_other = jnp.where(upper, grad_attended[:, :half], grad_attended[:, half:])
    grad_own = jnp.where(upper, grad_attended[:, half:], grad_attended[:, :half])
    grad_heads = side(upper, grad_own, swap(grad_other), 0)
    grad_outer_weight = outer_product(activated, second_low).astype(BF)
    grad_inner_weight = outer_product(hidden_low, inner_low).astype(BF)
    grad_output_weight = outer_product(attended, mixed_low).astype(BF)
    thin = [
        grad_output_bias,
        grad_first_gain,
        grad_first_shift,
        grad_outer_bias,
        grad_second_gain,
        grad_second_shift,
    ]
    thin = jnp.concatenate(
        [v.reshape(devices, part) for v in thin] + [grad_inner_bias.reshape(devices, inner_part)], 1
    ).astype(BF)
    thin_count = thin.shape[1]
    thin = jnp.pad(thin[:, None, :], ((0, 0), (0, 15), (0, width - thin_count)))
    bundle = jnp.concatenate(
        [
            grad_output_weight.reshape(devices, part, width),
            grad_inner_weight.reshape(devices, part, ratio, width)
            .transpose(0, 2, 1, 3)
            .reshape(devices, ratio * part, width),
            grad_outer_weight.reshape(devices, inner_part, width),
            thin,
        ],
        1,
    )
    bundle_rows = bundle.shape[1]
    reduced = lax.psum_scatter(
        bundle.reshape(devices * bundle_rows, width), ALL, scatter_dimension=0, tiled=True
    )
    grads, bias_sums = attn_bwd(
        qkv, memories, reads, limit, grad_heads, out_heads, totals, pairs, scale
    )
    other_grads = jnp.where(upper, grads[:rows], grads[rows:])
    own_grads = jnp.where(upper, grads[rows:], grads[:rows])
    sent = swap(back_product(other_grads, w_three).astype(BF))
    grad_inputs = grad_mixed + back_product(own_grads, w_three) + sent.astype(F32)
    three_grad = outer_product(features, grads).reshape(devices, part, 3 * half)
    full = lambda v: side(upper, v, jnp.zeros_like(v), 0).reshape(devices, part)
    tails = jnp.concatenate([full(bias_sums[0]), full(bias_sums[1])], 1)
    tails = jnp.pad(tails[:, None, :], ((0, 0), (0, 7), (0, 3 * half - 2 * part)))
    blocks = jnp.concatenate([three_grad, tails], 1).reshape(n_dp, 2, part + 8, 3 * half)
    mine = scatter_dp(blocks, n_dp)
    give = jnp.where(upper, mine[0], mine[1])
    keep = jnp.where(upper, mine[1], mine[0])
    got = swap(give.astype(BF)).astype(F32)
    tail_sum = keep[part] + got[part]
    keep = keep[:part].reshape(part, 3, half)
    got = got[:part].reshape(part, 3, half)
    matrices = side(upper, keep, got, 2)
    reduced = reduced.astype(F32)
    thin_row = reduced[bundle_rows - 16]
    thin_part = lambda k: thin_row[k * part : (k + 1) * part]
    own_inner = (
        reduced[part : part + ratio * part]
        .reshape(ratio, part, width)
        .transpose(1, 0, 2)
        .reshape(part, inner_width)
    )
    own_outer = reduced[part + ratio * part : part + ratio * part + inner_part]
    return (
        layer_out,
        grad_inputs,
        matrices[:, 0],
        tail_sum[:part],
        matrices[:, 1],
        matrices[:, 2],
        tail_sum[part : 2 * part],
        reduced[:part],
        thin_part(0),
        thin_part(1),
        thin_part(2),
        own_inner,
        thin_row[6 * part : 6 * part + inner_part],
        own_outer,
        thin_part(3),
        thin_part(4),
        thin_part(5),
    )


def solution(mesh):
    in_specs = (
        P(("dp", "seq"), None),
        P(("dp", "seq"), None),
        P(("dp", "seq")),
        P(("dp", "seq"), None),
        P(("dp", "seq"), None),
        P(("dp", "seq")),
        P(("dp", "seq"), None),
        P(("dp", "seq")),
        P(("dp", "seq")),
        P(("dp", "seq")),
        P(("dp", "seq"), None),
        P(("dp", "seq")),
        P(("dp", "seq"), None),
        P(("dp", "seq")),
        P(("dp", "seq")),
        P(("dp", "seq")),
        P(("dp", "seq"), None),
        P("dp", None),
        P("dp", None),
    )
    out_specs = (
        P(("dp", "seq"), None),
        P(("dp", "seq"), None),
        P(("dp", "seq"), None),
        P(("dp", "seq")),
        P(("dp", "seq"), None),
        P(("dp", "seq"), None),
        P(("dp", "seq")),
        P(("dp", "seq"), None),
        P(("dp", "seq")),
        P(("dp", "seq")),
        P(("dp", "seq")),
        P(("dp", "seq"), None),
        P(("dp", "seq")),
        P(("dp", "seq"), None),
        P(("dp", "seq")),
        P(("dp", "seq")),
        P(("dp", "seq")),
    )
    n_dp = mesh.shape["dp"]
    if mesh.shape["seq"] == 2 and n_dp & (n_dp - 1) == 0:
        chosen = partial(fast_body, n_dp=n_dp)
    else:
        chosen = body
    return jax.shard_map(chosen, mesh=mesh, in_specs=in_specs, out_specs=out_specs, check_vma=False)
```

```python
from functools import partial

import jax
import jax.numpy as jnp
from jax import lax
from jax.experimental import pallas as pl
from jax.experimental.pallas import tpu as pltpu
from jax.sharding import PartitionSpec as P


H = 12
HD = 64
LEN = 2048
PIC = 256
NPIC = 2
MEM = 10


norm_epsilon = 1e-05
masked_score = -1e30


def normalize(values, gain, shift):
    centre = jnp.mean(values, -1, keepdims=True)
    centred = values - centre
    spread = jnp.mean(centred * centred, -1, keepdims=True)
    return centred * lax.rsqrt(spread + norm_epsilon) * gain + shift


def gelu_exact(values):
    return jax.nn.gelu(values, approximate=False)


def visible_cols(positions, columns, starts, memories):
    labels = jnp.arange(NPIC, dtype=jnp.int32)[:, None] + 1
    in_cols = (columns[None, :] >= starts[:, None]) & (columns[None, :] < starts[:, None] + PIC)
    in_rows = (positions[None, :] >= starts[:, None]) & (positions[None, :] < starts[:, None] + PIC)
    piece_cols = jnp.sum(jnp.where(in_cols, labels, 0), 0)
    piece_rows = jnp.sum(jnp.where(in_rows, labels, 0), 0)
    same_piece = (piece_rows[:, None] == piece_cols[None, :]) & (piece_rows[:, None] > 0)
    read_cols = jnp.any(columns[None, :] == memories[:MEM, None], 0)
    write_rows = jnp.any(positions[None, :] == memories[MEM:, None], 0)
    causal = columns[None, :] <= positions[:, None]
    return causal | same_piece | read_cols[None, :] | write_rows[:, None]


def visible(positions, starts, memories):
    return visible_cols(positions, jnp.arange(LEN, dtype=jnp.int32), starts, memories)


def dense(left, right):
    return jnp.dot(left, right, preferred_element_type=jnp.float32)


def outer_product(left, right):
    return jnp.einsum("ta,tb->ab", left, right, preferred_element_type=jnp.float32)


def back_product(gradient, weight):
    return jnp.einsum("tb,ab->ta", gradient, weight, preferred_element_type=jnp.float32)


def body(
    inputs,
    query_weight,
    query_bias,
    key_weight,
    value_weight,
    value_bias,
    output_weight,
    output_bias,
    first_gain,
    first_shift,
    inner_weight,
    inner_bias,
    outer_weight,
    outer_bias,
    second_gain,
    second_shift,
    cotangent,
    piece_start,
    memory_pos,
):
    shards = (
        query_weight,
        key_weight,
        value_weight,
        output_weight,
        inner_weight,
        outer_weight,
        query_bias,
        value_bias,
        output_bias,
        first_gain,
        first_shift,
        inner_bias,
        outer_bias,
        second_gain,
        second_shift,
    )
    gathered = (
        lax.all_gather(shards[0], ("dp", "seq"), axis=0, tiled=True),
        lax.all_gather(shards[1], ("dp", "seq"), axis=0, tiled=True),
        lax.all_gather(shards[2], ("dp", "seq"), axis=0, tiled=True),
        lax.all_gather(shards[3], ("dp", "seq"), axis=0, tiled=True),
        lax.all_gather(shards[4], ("dp", "seq"), axis=0, tiled=True),
        lax.all_gather(shards[5], ("dp", "seq"), axis=0, tiled=True),
        lax.all_gather(shards[6], ("dp", "seq"), axis=0, tiled=True),
        lax.all_gather(shards[7], ("dp", "seq"), axis=0, tiled=True),
        lax.all_gather(shards[8], ("dp", "seq"), axis=0, tiled=True),
        lax.all_gather(shards[9], ("dp", "seq"), axis=0, tiled=True),
        lax.all_gather(shards[10], ("dp", "seq"), axis=0, tiled=True),
        lax.all_gather(shards[11], ("dp", "seq"), axis=0, tiled=True),
        lax.all_gather(shards[12], ("dp", "seq"), axis=0, tiled=True),
        lax.all_gather(shards[13], ("dp", "seq"), axis=0, tiled=True),
        lax.all_gather(shards[14], ("dp", "seq"), axis=0, tiled=True),
    )
    w_query, w_key, w_value, w_output, w_inner, w_outer = gathered[:6]
    vectors = [vector.astype(jnp.float32) for vector in gathered[6:]]
    b_query, b_value, b_output, g_first, s_first, b_inner, b_outer, g_second, s_second = vectors
    local_rows = inputs.shape[0]
    model_width = inputs.shape[1]
    score_scale = HD ** (-0.5)
    pair_count = H // 2
    pair_width = 2 * HD
    block_rows = min(512, local_rows, LEN)
    block_count = local_rows // block_rows
    first_row = lax.axis_index("seq") * local_rows
    query_low = (dense(inputs, w_query) + b_query).astype(jnp.bfloat16)
    key_low = dense(inputs, w_key).astype(jnp.bfloat16)
    value_low = (dense(inputs, w_value) + b_value).astype(jnp.bfloat16)
    group_keys, group_values = (
        lax.all_gather(key_low, "seq", axis=0, tiled=True),
        lax.all_gather(value_low, "seq", axis=0, tiled=True),
    )
    group_rows = group_keys.shape[0]

    def context(block_index):
        row_start = first_row + block_index * block_rows
        seq_index = row_start // LEN
        positions = row_start - seq_index * LEN + jnp.arange(block_rows, dtype=jnp.int32)
        starts = piece_start[0]
        memories = memory_pos[0]
        allowed = visible(positions, starts, memories)
        return (seq_index, allowed, group_keys, group_values)

    def pair_part(matrix, pair_index, count):
        return lax.dynamic_slice_in_dim(matrix, pair_index * pair_width, pair_width, 1).reshape(
            count, 2, HD
        )

    def pair_scores(query_pair, key_pair, allowed):
        raw = (
            jnp.einsum("qhd,khd->hqk", query_pair, key_pair, preferred_element_type=jnp.float32)
            * score_scale
        )
        return jnp.where(allowed[None], raw, masked_score)

    def forward_block(block_index):
        _, allowed, seq_keys, seq_values = context(block_index)
        block_query = lax.dynamic_slice_in_dim(query_low, block_index * block_rows, block_rows, 0)

        def forward_pair_step(carry, pair_index):
            out_buffer, total_buffer = carry
            query_pair = pair_part(block_query, pair_index, block_rows)
            key_pair = pair_part(seq_keys, pair_index, LEN)
            value_pair = pair_part(seq_values, pair_index, LEN)
            scores = pair_scores(query_pair, key_pair, allowed)
            peak = jnp.max(scores, -1, keepdims=True)
            expo_terms = jnp.exp(scores - peak)
            row_sum = jnp.sum(expo_terms, -1, keepdims=True)
            chances_low = (expo_terms / row_sum).astype(jnp.bfloat16)
            blended = jnp.einsum(
                "hqk,khd->qhd", chances_low, value_pair, preferred_element_type=jnp.float32
            )
            blended = blended.reshape(block_rows, pair_width).astype(jnp.bfloat16)
            out_buffer = lax.dynamic_update_slice_in_dim(
                out_buffer, blended, pair_index * pair_width, 1
            )
            log_pair = (peak + jnp.log(row_sum))[:, :, 0]
            total_buffer = lax.dynamic_update_slice_in_dim(
                total_buffer, log_pair, pair_index * 2, 0
            )
            return ((out_buffer, total_buffer), None)

        initial = (
            jnp.zeros((block_rows, model_width), jnp.bfloat16),
            jnp.zeros((H, block_rows), jnp.float32),
        )
        (out_buffer, total_buffer), unused = lax.scan(
            forward_pair_step, initial, jnp.arange(pair_count)
        )
        return (out_buffer, total_buffer)

    attended_blocks, log_totals = lax.map(forward_block, jnp.arange(block_count))
    attended = attended_blocks.reshape(local_rows, model_width)
    mixed = inputs.astype(jnp.float32) + dense(attended, w_output) + b_output
    hidden_norm, first_pull = jax.vjp(normalize, mixed, g_first, s_first)
    hidden_low = hidden_norm.astype(jnp.bfloat16)
    inner = dense(hidden_low, w_inner) + b_inner
    activated_full, gelu_pull = jax.vjp(gelu_exact, inner)
    activated = activated_full.astype(jnp.bfloat16)
    second_in = hidden_norm + dense(activated, w_outer) + b_outer
    normed_out, second_pull = jax.vjp(normalize, second_in, g_second, s_second)
    layer_out = normed_out.astype(jnp.bfloat16)
    back_weights = (
        lax.all_gather(query_weight, ("dp", "seq"), axis=0, tiled=True),
        lax.all_gather(key_weight, ("dp", "seq"), axis=0, tiled=True),
        lax.all_gather(value_weight, ("dp", "seq"), axis=0, tiled=True),
        lax.all_gather(output_weight, ("dp", "seq"), axis=0, tiled=True),
        lax.all_gather(inner_weight, ("dp", "seq"), axis=0, tiled=True),
        lax.all_gather(outer_weight, ("dp", "seq"), axis=0, tiled=True),
    )
    v_query, v_key, v_value, v_output, v_inner, v_outer = back_weights
    grad_second_in, grad_second_gain, grad_second_shift = second_pull(cotangent.astype(jnp.float32))
    grad_outer_bias = jnp.sum(grad_second_in, 0)
    second_low = grad_second_in.astype(jnp.bfloat16)
    grad_outer_weight = outer_product(activated, second_low)
    (grad_inner,) = gelu_pull(back_product(second_low, v_outer))
    grad_inner_bias = jnp.sum(grad_inner, 0)
    inner_low = grad_inner.astype(jnp.bfloat16)
    grad_inner_weight = outer_product(hidden_low, inner_low)
    grad_hidden = grad_second_in + back_product(inner_low, v_inner)
    grad_mixed, grad_first_gain, grad_first_shift = first_pull(grad_hidden)
    grad_output_bias = jnp.sum(grad_mixed, 0)
    mixed_low = grad_mixed.astype(jnp.bfloat16)
    grad_output_weight = outer_product(attended, mixed_low)
    grad_attended = back_product(mixed_low, v_output).astype(jnp.bfloat16)

    def backward_block(carry, block_index):
        _, allowed, seq_keys, seq_values = context(block_index)
        block_query = lax.dynamic_slice_in_dim(query_low, block_index * block_rows, block_rows, 0)
        block_grad = lax.dynamic_slice_in_dim(
            grad_attended, block_index * block_rows, block_rows, 0
        )
        block_total = log_totals[block_index]

        def backward_pair_step(inner_carry, pair_index):
            query_grad, term_buffer = (inner_carry[0], inner_carry[1])
            query_pair = pair_part(block_query, pair_index, block_rows)
            key_pair = pair_part(seq_keys, pair_index, LEN)
            value_pair = pair_part(seq_values, pair_index, LEN)
            grad_pair = pair_part(block_grad, pair_index, block_rows)
            scores = pair_scores(query_pair, key_pair, allowed)
            total_pair = lax.dynamic_slice_in_dim(block_total, pair_index * 2, 2, 0)
            chances = jnp.exp(scores - total_pair[:, :, None])
            chance_grad = jnp.einsum(
                "qhd,khd->hqk", grad_pair, value_pair, preferred_element_type=jnp.float32
            )
            row_terms = jnp.sum(chances * chance_grad, -1, keepdims=True)
            score_grad = (chances * (chance_grad - row_terms)).astype(jnp.bfloat16)
            query_part = jnp.einsum(
                "hqk,khd->qhd", score_grad, key_pair, preferred_element_type=jnp.float32
            )
            query_part = query_part.reshape(block_rows, pair_width) * score_scale
            query_grad = lax.dynamic_update_slice_in_dim(
                query_grad, query_part, pair_index * pair_width, 1
            )
            term_buffer = lax.dynamic_update_slice_in_dim(
                term_buffer, row_terms[:, :, 0], pair_index * 2, 0
            )
            seq_key_grad, seq_value_grad = (inner_carry[2], inner_carry[3])
            chances_low = chances.astype(jnp.bfloat16)
            key_part = jnp.einsum(
                "hqk,qhd->khd", score_grad, query_pair, preferred_element_type=jnp.float32
            )
            value_part = jnp.einsum(
                "hqk,qhd->khd", chances_low, grad_pair, preferred_element_type=jnp.float32
            )
            key_part = key_part.reshape(LEN, pair_width) * score_scale
            value_part = value_part.reshape(LEN, pair_width)
            seq_key_grad = lax.dynamic_update_slice_in_dim(
                seq_key_grad, key_part, pair_index * pair_width, 1
            )
            seq_value_grad = lax.dynamic_update_slice_in_dim(
                seq_value_grad, value_part, pair_index * pair_width, 1
            )
            return ((query_grad, term_buffer, seq_key_grad, seq_value_grad), None)

        initial = (
            jnp.zeros((block_rows, model_width), jnp.float32),
            jnp.zeros((H, block_rows), jnp.float32),
        )
        initial = initial + (
            jnp.zeros((LEN, model_width), jnp.float32),
            jnp.zeros((LEN, model_width), jnp.float32),
        )
        finals, _ = lax.scan(backward_pair_step, initial, jnp.arange(pair_count))
        key_grads, value_grads = carry
        key_grads = key_grads + finals[2]
        value_grads = value_grads + finals[3]
        carry = (key_grads, value_grads)
        return (carry, (finals[0], finals[1]))

    group_zero = jnp.zeros((group_rows, model_width), jnp.float32)
    (key_grads, value_grads), (query_blocks, term_blocks) = lax.scan(
        backward_block, (group_zero, group_zero), jnp.arange(block_count)
    )
    key_sum, value_sum = (
        lax.psum_scatter(
            key_grads.astype(jnp.bfloat16), "seq", scatter_dimension=0, tiled=True
        ).astype(jnp.float32),
        lax.psum_scatter(
            value_grads.astype(jnp.bfloat16), "seq", scatter_dimension=0, tiled=True
        ).astype(jnp.float32),
    )
    query_sum = query_blocks.reshape(local_rows, model_width)
    grad_query_bias = jnp.sum(query_sum, 0)
    grad_value_bias = jnp.sum(value_sum, 0)
    query_grad_low = query_sum.astype(jnp.bfloat16)
    key_grad_low = key_sum.astype(jnp.bfloat16)
    value_grad_low = value_sum.astype(jnp.bfloat16)
    grad_query_weight = outer_product(inputs, query_grad_low)
    grad_key_weight = outer_product(inputs, key_grad_low)
    grad_value_weight = outer_product(inputs, value_grad_low)
    grad_inputs = (
        grad_mixed
        + back_product(query_grad_low, v_query)
        + back_product(key_grad_low, v_key)
        + back_product(value_grad_low, v_value)
    )
    grads = (
        grad_query_weight,
        grad_key_weight,
        grad_value_weight,
        grad_output_weight,
        grad_inner_weight,
        grad_outer_weight,
        grad_query_bias,
        grad_value_bias,
        grad_output_bias,
        grad_first_gain,
        grad_first_shift,
        grad_inner_bias,
        grad_outer_bias,
        grad_second_gain,
        grad_second_shift,
    )
    owned = (
        lax.psum_scatter(grads[0], ("dp", "seq"), scatter_dimension=0, tiled=True),
        lax.psum_scatter(grads[1], ("dp", "seq"), scatter_dimension=0, tiled=True),
        lax.psum_scatter(grads[2], ("dp", "seq"), scatter_dimension=0, tiled=True),
        lax.psum_scatter(grads[3], ("dp", "seq"), scatter_dimension=0, tiled=True),
        lax.psum_scatter(grads[4], ("dp", "seq"), scatter_dimension=0, tiled=True),
        lax.psum_scatter(grads[5], ("dp", "seq"), scatter_dimension=0, tiled=True),
        lax.psum_scatter(grads[6], ("dp", "seq"), scatter_dimension=0, tiled=True),
        lax.psum_scatter(grads[7], ("dp", "seq"), scatter_dimension=0, tiled=True),
        lax.psum_scatter(grads[8], ("dp", "seq"), scatter_dimension=0, tiled=True),
        lax.psum_scatter(grads[9], ("dp", "seq"), scatter_dimension=0, tiled=True),
        lax.psum_scatter(grads[10], ("dp", "seq"), scatter_dimension=0, tiled=True),
        lax.psum_scatter(grads[11], ("dp", "seq"), scatter_dimension=0, tiled=True),
        lax.psum_scatter(grads[12], ("dp", "seq"), scatter_dimension=0, tiled=True),
        lax.psum_scatter(grads[13], ("dp", "seq"), scatter_dimension=0, tiled=True),
        lax.psum_scatter(grads[14], ("dp", "seq"), scatter_dimension=0, tiled=True),
    )
    return (
        layer_out,
        grad_inputs,
        owned[0],
        owned[6],
        owned[1],
        owned[2],
        owned[7],
        owned[3],
        owned[8],
        owned[9],
        owned[10],
        owned[4],
        owned[11],
        owned[5],
        owned[12],
        owned[13],
        owned[14],
    )


F32=jnp.float32; BF=jnp.bfloat16
NT=(((1,),(1,)),((),()))
NN=(((1,),(0,)),((),()))


def mm(a,b,dims=NN):
    return lax.dot_general(a,b,dims,preferred_element_type=F32)


GROUP=16


def half_mask(shape, head, dim):
    lanes=lax.broadcasted_iota(jnp.int32,shape,dim)
    return (lanes<64) if head==0 else (lanes>=64)


def only(x, head):
    return jnp.where(half_mask(x.shape,head,1),x,jnp.zeros_like(x))


def take_rows(ref, pos_ref, first):
    width=ref.shape[1]
    out=jnp.zeros((GROUP,width),F32)
    rows=lax.broadcasted_iota(jnp.int32,(GROUP,width),0)
    for m in range(MEM):
        pos=pos_ref[first+m]
        start=pl.multiple_of((pos//GROUP)*GROUP,GROUP)
        part=ref[pl.ds(start,GROUP),:].astype(F32)
        row=jnp.sum(jnp.where(rows==pos-start,part,0.0),0,keepdims=True)
        out=jnp.where(rows==m,row,out)
    return out.astype(BF)


def put_rows(ref, pos_ref, first, values, add):
    width=ref.shape[1]
    rows=lax.broadcasted_iota(jnp.int32,(GROUP,width),0)
    for m in range(MEM):
        pos=pos_ref[first+m]
        start=pl.multiple_of((pos//GROUP)*GROUP,GROUP)
        old=ref[pl.ds(start,GROUP),:].astype(F32)
        row=values[m:m+1,:]
        new=jnp.where(rows==pos-start,old+row if add else row,old)
        ref[pl.ds(start,GROUP),:]=new.astype(ref.dtype)


def transposed(x):
    return jnp.transpose(x.astype(F32)).astype(BF)


def fwd_kernel(pos_ref, posv_ref, limit_ref, write_ref, qkv_ref, o_ref, lse_ref, vt_ref, qt_ref, acc_ref, *, bq, np_, qb0, qb1):
    rows_all=qkv_ref.shape[0]
    nq=rows_all//bq
    W=np_*128
    nh=2*np_
    cols=lambda part,p:slice(part*W+p*128,part*W+p*128+128)
    hr=lambda h:slice(80*h,80*h+80)
    mem=take_rows(qkv_ref,pos_ref,0)
    kr=[only(mem[:,cols(1,h//2)],h%2) for h in range(nh)]
    ones16=jnp.ones((16,GROUP),BF)
    vrt=[]
    for p in range(np_):
        vt=transposed(qkv_ref[:,cols(2,p)])
        mt=transposed(mem[:,cols(2,p)])
        qt_ref[p*128:p*128+128,:]=transposed(qkv_ref[:,cols(0,p)])
        for h in range(2):
            vt_ref[80*(2*p+h):80*(2*p+h)+64,:]=vt[64*h:64*h+64]
            vt_ref[80*(2*p+h)+64:80*(2*p+h)+80,:]=jnp.ones((16,rows_all),BF)
            vrt.append(jnp.concatenate([mt[64*h:64*h+64],ones16],0))
    read_pos=posv_ref[...]
    def q_step(qb, unused):
        q0=pl.multiple_of(qb*bq,bq)
        limit=limit_ref[:,pl.ds(q0,bq)][0:1]
        key_iota=lax.broadcasted_iota(jnp.int32,(bq,bq),0)
        zq=jnp.zeros((64,bq),BF)
        def qh(h):
            own=qt_ref[64*h:64*h+64,pl.ds(q0,bq)]
            return jnp.concatenate([own,zq] if h%2==0 else [zq,own],0)
        def soft(h,s,vt,m):
            m2=jnp.maximum(m,jnp.max(s,0,keepdims=True))
            fix=jnp.exp2(m-m2)
            p=jnp.exp2(s-m2)
            acc_ref[hr(h),:]=acc_ref[hr(h),:]*fix+mm(vt,p.astype(BF))
            return m2
        def block(kb,carry,mask):
            k0=pl.multiple_of(kb*bq,bq)
            ss=[mm(qkv_ref[pl.ds(k0,bq),cols(1,h//2)],qh(h)) for h in range(nh)]
            if mask:
                ss=[jnp.where(key_iota+k0<=limit,s,masked_score) for s in ss]
            return tuple(soft(h,ss[h],vt_ref[hr(h),pl.ds(k0,bq)],carry[h]) for h in range(nh))
        acc_ref[...]=jnp.zeros_like(acc_ref)
        carry=tuple(jnp.full((1,bq),masked_score,F32) for _ in range(nh))
        carry=block(qb,carry,True)
        carry=tuple(soft(h,jnp.where(read_pos>limit,mm(kr[h],qh(h)),masked_score),vrt[h],carry[h]) for h in range(nh))
        carry=lax.fori_loop(0,qb,lambda kb,c:block(kb,c,False),carry)
        far=jnp.max(limit)>=q0+bq
        carry=lax.cond(far,lambda c:block(jnp.minimum(qb+1,nq-1),c,True),lambda c:c,carry)
        wr=write_ref[:,pl.ds(q0,bq)][0:1]
        outs=[]
        for h in range(nh):
            l=acc_ref[80*h+64:80*h+65,:]
            outs.append(acc_ref[80*h:80*h+64,:]/l)
            lse=carry[h]+jnp.log2(l)
            lse_ref[h:h+1,pl.ds(q0,bq)]=jnp.where(wr>0,1e30,lse)
        o_ref[pl.ds(q0,bq),:]=jnp.transpose(jnp.concatenate(outs,0)).astype(BF)
        return unused
    lax.fori_loop(qb0,qb1,q_step,0)
    rows=take_rows(qkv_ref,pos_ref,MEM)
    out=[]
    for p in range(np_):
        total=jnp.zeros((GROUP,128),F32)
        qw=rows[:,cols(0,p)]
        for h in range(2):
            s=mm(only(qw,h),qkv_ref[:,cols(1,p)],NT)
            m=jnp.max(s,1,keepdims=True)
            e=jnp.exp2(s-m)
            l=jnp.sum(e,1,keepdims=True)
            ow=mm(e.astype(BF),qkv_ref[:,cols(2,p)])/l
            total=total+jnp.where(half_mask((GROUP,128),h,1),ow,0.0)
        out.append(total)
    put_rows(o_ref,pos_ref,MEM,jnp.concatenate(out,1),False)


LN2=0.6931471805599453


def bwd_kernel(pos_ref, posv_ref, limit_ref, qkv_ref, do_ref, o_ref, lse_ref,
               dqkv_ref, bias_ref, qt_ref, kt_ref, dot_ref, dk_acc, dv_acc, dq_acc, dr_acc, *, bq, scale, np_):
    rows_all=qkv_ref.shape[0]
    nq=rows_all//bq
    W=np_*128
    nh=2*np_
    cols=lambda part,p:slice(part*W+p*128,part*W+p*128+128)
    pc=lambda p:slice(p*128,p*128+128)
    hr=lambda h:slice(64*h,64*h+64)
    for p in range(np_):
        qt_ref[pc(p),:]=transposed(qkv_ref[:,cols(0,p)])
        kt_ref[pc(p),:]=transposed(qkv_ref[:,cols(1,p)])
        dot_ref[pc(p),:]=transposed(do_ref[:,pc(p)])
    mem=take_rows(qkv_ref,pos_ref,0)
    kr=[mem[:,cols(1,p)] for p in range(np_)]
    vr=[mem[:,cols(2,p)] for p in range(np_)]
    krt=[transposed(kr[p]) for p in range(np_)]
    read_pos=posv_ref[...]
    rows=take_rows(qkv_ref,pos_ref,MEM)
    dow_all=take_rows(do_ref,pos_ref,MEM)
    valid=lax.broadcasted_iota(jnp.int32,(GROUP,1),0)<MEM
    dqw_all=[]
    for pr in range(np_):
        qw=rows[:,cols(0,pr)]
        dow=dow_all[:,pc(pr)]
        qwt=transposed(qw); dowt=transposed(dow)
        dqw=jnp.zeros((GROUP,128),F32)
        for h in range(2):
            s=mm(only(qw,h),qkv_ref[:,cols(1,pr)],NT)
            m=jnp.max(s,1,keepdims=True)
            p=jnp.exp2(s-m)
            p=p*jnp.where(valid,1.0/jnp.sum(p,1,keepdims=True),0.0)
            dp=mm(only(dow,h),qkv_ref[:,cols(2,pr)],NT)
            ds=(p*(dp-jnp.sum(p*dp,1,keepdims=True))).astype(BF)
            dqw=dqw+jnp.where(half_mask((GROUP,128),h,1),mm(ds,qkv_ref[:,cols(1,pr)]),0.0)
            dk_acc[hr(2*pr+h),:]=mm(qwt[64*h:64*h+64],ds)
            dv_acc[hr(2*pr+h),:]=mm(dowt[64*h:64*h+64],p.astype(BF))
        dqw_all.append(dqw)
    dr_acc[...]=jnp.zeros_like(dr_acc)
    def q_step(qb, unused):
        q0=pl.multiple_of(qb*bq,bq)
        limit=limit_ref[:,pl.ds(q0,bq)][0:1]
        zq=jnp.zeros((64,bq),BF)
        def padded(ref,h):
            own=ref[hr(h),pl.ds(q0,bq)]
            return jnp.concatenate([own,zq] if h%2==0 else [zq,own],0)
        prod=jnp.transpose(do_ref[pl.ds(q0,bq),:].astype(F32)*o_ref[pl.ds(q0,bq),:].astype(F32))
        delta=[jnp.sum(prod[hr(h)],0,keepdims=True) for h in range(nh)]
        lse=[lse_ref[h:h+1,pl.ds(q0,bq)] for h in range(nh)]
        key_iota=lax.broadcasted_iota(jnp.int32,(bq,bq),0)
        dq_acc[...]=jnp.zeros_like(dq_acc)
        def grads(h,s,v):
            p=jnp.exp2(s-lse[h])
            dp=mm(v,padded(dot_ref,h))
            return (p*(dp-delta[h])).astype(BF),p.astype(BF)
        def block(kb,mask):
            k0=pl.multiple_of(kb*bq,bq)
            ks=pl.ds(k0,bq)
            held={}
            def front(h):
                s=mm(qkv_ref[ks,cols(1,h//2)],padded(qt_ref,h))
                if mask:
                    s=jnp.where(key_iota+k0<=limit,s,masked_score)
                held[h]=(s,mm(qkv_ref[ks,cols(2,h//2)],padded(dot_ref,h)))
            def middle(h):
                s,dp=held[h]
                p=jnp.exp2(s-lse[h])
                held[h]=((p*(dp-delta[h])).astype(BF),p.astype(BF))
            def back(h):
                ds,p=held[h]
                dq_acc[hr(h),:]+=mm(kt_ref[hr(h),ks],ds)
                dk_acc[hr(h),ks]+=mm(qt_ref[hr(h),pl.ds(q0,bq)],ds,NT)
                dv_acc[hr(h),ks]+=mm(dot_ref[hr(h),pl.ds(q0,bq)],p,NT)
            for h in range(nh+2):
                if h<nh:
                    front(h)
                if 0<=h-1<nh:
                    middle(h-1)
                if h>=2:
                    back(h-2)
        block(qb,True)
        for h in range(nh):
            s=jnp.where(read_pos>limit,mm(kr[h//2],padded(qt_ref,h)),masked_score)
            ds,p=grads(h,s,vr[h//2])
            dr_acc[0,hr(h),:]+=mm(qt_ref[hr(h),pl.ds(q0,bq)],ds,NT)
            dr_acc[1,hr(h),:]+=mm(dot_ref[hr(h),pl.ds(q0,bq)],p,NT)
            dq_acc[hr(h),:]+=mm(krt[h//2][64*(h%2):64*(h%2)+64,:],ds)
        def step(kb,c):
            block(kb,False)
            return c
        lax.fori_loop(0,qb,step,0)
        @pl.when(jnp.max(limit)>=q0+bq)
        def _():
            block(jnp.minimum(qb+1,nq-1),True)
        dqkv_ref[pl.ds(q0,bq),0:W]=(jnp.transpose(dq_acc[...])*scale).astype(BF)
        return unused
    lax.fori_loop(0,nq,q_step,0)
    put_rows(dqkv_ref.at[:,0:W],pos_ref,MEM,jnp.concatenate(dqw_all,1)*scale,False)
    for p in range(np_):
        dqkv_ref[:,cols(1,p)]=(jnp.transpose(dk_acc[pc(p),:])*LN2).astype(BF)
        dqkv_ref[:,cols(2,p)]=jnp.transpose(dv_acc[pc(p),:]).astype(BF)
    put_rows(dqkv_ref.at[:,W:2*W],pos_ref,0,jnp.transpose(dr_acc[0])*LN2,True)
    put_rows(dqkv_ref.at[:,2*W:3*W],pos_ref,0,jnp.transpose(dr_acc[1]),True)
    rows8=lax.broadcasted_iota(jnp.int32,(8,W),0)
    bq_sum=jnp.sum(dqkv_ref[:,0:W].astype(F32),0,keepdims=True)
    bv_sum=jnp.sum(dqkv_ref[:,2*W:3*W].astype(F32),0,keepdims=True)
    bias_ref[...]=jnp.where(rows8==0,bq_sum,jnp.where(rows8==1,bv_sum,0.0))


ONCE=pl.Buffered(1)


def attn_fwd(qkv, pos, posv, limit, write, np_, bq=256, qb0=0, qb1=None):
    L=qkv.shape[0]; W=np_*128
    row8=pl.BlockSpec((8,L),lambda i:(0,0),pipeline_mode=ONCE)
    full=lambda w:pl.BlockSpec((L,w),lambda i:(0,0),pipeline_mode=ONCE)
    return pl.pallas_call(partial(fwd_kernel,bq=bq,np_=np_,qb0=qb0,qb1=L//bq if qb1 is None else qb1),
        grid=(1,),
        in_specs=[pl.BlockSpec(memory_space=pltpu.SMEM),pl.BlockSpec((GROUP,1),lambda i:(0,0)),row8,row8,full(3*W)],
        out_specs=[full(W),row8],
        out_shape=[jax.ShapeDtypeStruct((L,W),BF),jax.ShapeDtypeStruct((8,L),F32)],
        scratch_shapes=[pltpu.VMEM((np_*160,L),BF),pltpu.VMEM((W,L),BF),pltpu.VMEM((np_*160,bq),F32)],
        name="attn_fwd",
    )(pos,posv,limit,write,qkv)


def attn_bwd(qkv, pos, posv, limit, do, o, lse, np_, scale, bq=256):
    L=qkv.shape[0]; W=np_*128
    row8=pl.BlockSpec((8,L),lambda i:(0,0),pipeline_mode=ONCE)
    full=lambda w:pl.BlockSpec((L,w),lambda i:(0,0),pipeline_mode=ONCE)
    return pl.pallas_call(partial(bwd_kernel,bq=bq,scale=scale,np_=np_),
        grid=(1,),
        in_specs=[pl.BlockSpec(memory_space=pltpu.SMEM),pl.BlockSpec((GROUP,1),lambda i:(0,0)),row8,full(3*W),full(W),full(W),row8],
        out_specs=[full(3*W),pl.BlockSpec((8,W),lambda i:(0,0))],
        out_shape=[jax.ShapeDtypeStruct((L,3*W),BF),jax.ShapeDtypeStruct((8,W),F32)],
        scratch_shapes=[pltpu.VMEM((W,L),BF)]*3+[pltpu.VMEM((W,L),F32)]*2+[pltpu.VMEM((W,bq),F32),pltpu.VMEM((2,W,GROUP),F32)],
        name="attn_bwd",
    )(pos,posv,limit,qkv,do,o,lse)


LOG2E = 1.4426950408889634
ALL = ("dp", "seq")
RSQRT2 = 0.7071067811865476
RSQRT2PI = 0.3989422804014327


def bit_swap(x, axis, size, bit):
    return lax.ppermute(x, axis, [(i, i ^ bit) for i in range(size)])


def side(flag, own, peer, axis):
    low = jnp.where(flag, peer, own)
    high = jnp.where(flag, own, peer)
    return jnp.concatenate([low, high], axis)


def bits_of(size):
    out = []
    bit = 1
    while bit < size:
        out.append(bit)
        bit *= 2
    return out


def gather_dp(block, size):
    bits = bits_of(size)[::-1]
    index = lax.axis_index("dp")
    out = block
    for bit in bits:
        other = bit_swap(out, "dp", size, bit)
        up = (index & bit) != 0
        out = jnp.stack([jnp.where(up, other, out), jnp.where(up, out, other)])
    count = len(bits)
    out = out.transpose(tuple(range(count))[::-1] + tuple(range(count, out.ndim)))
    return out.reshape((size,) + block.shape)


def halve_dp(rest, size, bit):
    up = (lax.axis_index("dp") & bit) != 0
    rest = rest.reshape((rest.shape[0] // 2, 2) + rest.shape[1:])
    give = jnp.where(up, rest[:, 0], rest[:, 1]).astype(BF)
    keep = jnp.where(up, rest[:, 1], rest[:, 0])
    got = bit_swap(give, "dp", size, bit)
    return keep + got.astype(F32)


def norm_parts(values):
    centre = jnp.mean(values, -1, keepdims=True)
    centred = values - centre
    spread = jnp.mean(centred * centred, -1, keepdims=True)
    factor = lax.rsqrt(spread + norm_epsilon)
    return centred * factor, factor


def norm_back(gradient, unit, factor):
    return factor * (
        gradient
        - jnp.mean(gradient, -1, keepdims=True)
        - unit * jnp.mean(gradient * unit, -1, keepdims=True)
    )


def fast_body(
    inputs,
    query_weight,
    query_bias,
    key_weight,
    value_weight,
    value_bias,
    output_weight,
    output_bias,
    first_gain,
    first_shift,
    inner_weight,
    inner_bias,
    outer_weight,
    outer_bias,
    second_gain,
    second_shift,
    cotangent,
    piece_start,
    memory_pos,
    *,
    n_dp,
):
    rows, width = inputs.shape
    inner_width = inner_weight.shape[1]
    devices = 2 * n_dp
    part = width // devices
    inner_part = inner_width // devices
    ratio = inner_width // width
    half = width // 2
    seq = lax.axis_index("seq")
    upper = seq == 1

    def swap(x):
        return bit_swap(x, "seq", 2, 1)

    wide = inner_weight.reshape(part, ratio, width).transpose(1, 0, 2).reshape(ratio * part, width)
    packed = jnp.concatenate([output_weight, wide, outer_weight], 0)
    late = lax.all_gather(packed, ALL, axis=0, tiled=False)
    peer_inputs = swap(inputs)
    vectors = jnp.concatenate(
        [
            query_bias,
            value_bias,
            output_bias,
            first_gain,
            first_shift,
            outer_bias,
            second_gain,
            second_shift,
            inner_bias,
        ]
    )
    count = vectors.shape[0]
    three = jnp.stack([query_weight, key_weight, value_weight], 1)
    three = three.reshape(part, 3, 2, half)
    line = jnp.pad(vectors, (0, 3 * half - count))[None, :]
    line = jnp.pad(line, ((0, 7), (0, 0)))

    def columns(upper_half):
        kept = jnp.where(upper_half, three[:, :, 1], three[:, :, 0]).reshape(part, 3 * half)
        return jnp.concatenate([kept, line], 0)

    pair = side(upper, columns(upper)[None], swap(columns(jnp.logical_not(upper)))[None], 0)
    early = gather_dp(pair, n_dp).reshape(devices, part + 8, 3 * half)
    w_three = early[:, :part].reshape(width, 3 * half)
    lines = early[:, part, :count].astype(F32)
    vector = lambda k: lines[:, k * part : (k + 1) * part].reshape(width)
    b_query, b_value, b_output, g_first, s_first, b_outer, g_second, s_second = map(vector, range(8))
    b_inner = lines[:, 8 * part :].reshape(inner_width)
    own_half = lambda v: jnp.where(upper, v[half:], v[:half])
    features = side(upper, inputs, peer_inputs, 0)
    scale = HD ** (-0.5)
    shift = jnp.concatenate([own_half(b_query), jnp.zeros((half,), F32), own_half(b_value)])
    grow = jnp.concatenate([jnp.full((half,), scale * LOG2E, F32), jnp.ones((2 * half,), F32)])
    qkv = ((dense(features, w_three) + shift) * grow).astype(BF)
    positions = jnp.arange(2 * rows, dtype=jnp.int32)
    limit = positions
    for piece in range(NPIC):
        start = piece_start[0, piece]
        inside = (positions >= start) & (positions < start + PIC)
        limit = jnp.where(inside, start + PIC - 1, limit)
    memories = memory_pos[0]
    writes = jnp.any(positions[None, :] == memories[MEM:, None], 0).astype(jnp.int32)
    limit = jnp.broadcast_to(limit, (8, 2 * rows))
    writes = jnp.broadcast_to(writes, (8, 2 * rows))
    reads = jnp.pad(memories[:MEM], (0, GROUP - MEM), constant_values=-1)[:, None]
    pairs = half // (2 * HD)
    out_heads, totals = attn_fwd(qkv, memories, reads, limit, writes, pairs)
    other_rows = jnp.where(upper, out_heads[:rows], out_heads[rows:])
    own_rows = jnp.where(upper, out_heads[rows:], out_heads[:rows])
    attended = side(upper, own_rows, swap(other_rows), 1)
    w_output = late[:, :part].reshape(width, width)
    w_inner = jnp.concatenate(
        [
            late[:, part + k * part : 2 * part + k * part].reshape(width, width)
            for k in range(ratio)
        ],
        1,
    )
    w_outer = late[:, part + ratio * part :].reshape(inner_width, width)
    mixed = inputs.astype(F32) + dense(attended, w_output) + b_output
    first_unit, first_factor = norm_parts(mixed)
    hidden_norm = first_unit * g_first + s_first
    hidden_low = hidden_norm.astype(BF)
    inner = dense(hidden_low, w_inner) + b_inner
    chance = 0.5 * (1.0 + lax.erf(inner * RSQRT2))
    activated = (inner * chance).astype(BF)
    slope = (chance + inner * (RSQRT2PI * jnp.exp(-0.5 * inner * inner))).astype(BF)
    activated, slope = lax.optimization_barrier((activated, slope))
    second_in = hidden_norm + dense(activated, w_outer) + b_outer
    second_unit, second_factor = norm_parts(second_in)
    layer_out = (second_unit * g_second + s_second).astype(BF)
    cot = cotangent.astype(F32)
    grad_second_gain = jnp.sum(cot * second_unit, 0)
    grad_second_shift = jnp.sum(cot, 0)
    grad_second_in = norm_back(cot * g_second, second_unit, second_factor)
    grad_outer_bias = jnp.sum(grad_second_in, 0)
    second_low = grad_second_in.astype(BF)
    grad_inner = back_product(second_low, w_outer) * slope.astype(F32)
    grad_inner_bias = jnp.sum(grad_inner, 0)
    inner_low = grad_inner.astype(BF)
    column = lambda k: inner_low[:, k * width : (k + 1) * width]
    inner_blocks = [
        outer_product(hidden_low, column(k)).astype(BF).reshape(devices, part, width)
        for k in range(ratio)
    ]
    grad_outer_weight = outer_product(activated, second_low).astype(BF)
    bundle = jnp.concatenate(
        inner_blocks + [grad_outer_weight.reshape(devices, inner_part, width)], 1
    )
    bundle_rows = bundle.shape[1]
    bundle, inner_low = lax.optimization_barrier((bundle, inner_low))
    reduced = lax.psum_scatter(
        bundle.reshape(devices * bundle_rows, width), ALL, scatter_dimension=0, tiled=True
    )
    grad_hidden = grad_second_in + back_product(inner_low, w_inner)
    grad_first_gain = jnp.sum(grad_hidden * first_unit, 0)
    grad_first_shift = jnp.sum(grad_hidden, 0)
    grad_mixed = norm_back(grad_hidden * g_first, first_unit, first_factor)
    grad_output_bias = jnp.sum(grad_mixed, 0)
    mixed_low = grad_mixed.astype(BF)
    grad_attended = back_product(mixed_low, w_output).astype(BF)
    grad_other = jnp.where(upper, grad_attended[:, :half], grad_attended[:, half:])
    grad_own = jnp.where(upper, grad_attended[:, half:], grad_attended[:, :half])
    grad_heads = side(upper, grad_own, swap(grad_other), 0)
    grad_output_weight = outer_product(attended, mixed_low).reshape(devices, part, width)
    thin = [
        grad_output_bias,
        grad_first_gain,
        grad_first_shift,
        grad_outer_bias,
        grad_second_gain,
        grad_second_shift,
    ]
    thin = jnp.concatenate(
        [v.reshape(devices, part) for v in thin] + [grad_inner_bias.reshape(devices, inner_part)], 1
    )
    thin = jnp.pad(thin[:, None, :], ((0, 0), (0, 7), (0, width - thin.shape[1])))
    mid = jnp.concatenate([grad_output_weight, thin], 1).reshape(n_dp, 2, part + 8, width)
    bits = bits_of(n_dp)
    mid = halve_dp(mid, n_dp, bits[0])
    grads, bias_sums = attn_bwd(
        qkv, memories, reads, limit, grad_heads, out_heads, totals, pairs, scale
    )
    other_grads = jnp.where(upper, grads[:rows], grads[rows:])
    own_grads = jnp.where(upper, grads[rows:], grads[:rows])
    for_peer = back_product(other_grads, w_three).astype(BF)
    for_peer, grads = lax.optimization_barrier((for_peer, grads))
    sent = swap(for_peer)
    three_grad = outer_product(features, grads).reshape(devices, part, 3 * half)
    full = lambda v: side(upper, v, jnp.zeros_like(v), 0).reshape(devices, part)
    tails = jnp.concatenate([full(bias_sums[0]), full(bias_sums[1])], 1)
    tails = jnp.pad(tails[:, None, :], ((0, 0), (0, 7), (0, 3 * half - 2 * part)))
    blocks = jnp.concatenate([three_grad, tails], 1).reshape(n_dp, 2, part + 8, 3 * half)
    blocks = halve_dp(blocks, n_dp, bits[0])
    own_part = lax.optimization_barrier(grad_mixed + back_product(own_grads, w_three))
    mid = halve_dp(mid, n_dp, bits[1])
    blocks = halve_dp(blocks, n_dp, bits[1])
    blocks = jnp.concatenate([blocks, mid], 3)
    for bit in bits[2:]:
        blocks = halve_dp(blocks, n_dp, bit)
    mine = blocks[0]
    give = jnp.where(upper, mine[0], mine[1])
    keep = jnp.where(upper, mine[1], mine[0])
    got = swap(give.astype(BF)).astype(F32)
    grad_inputs = own_part + sent.astype(F32)
    total = keep[:, 3 * half :] + got[:, 3 * half :]
    tail_sum = keep[part, : 2 * part] + got[part, : 2 * part]
    keep = keep[:part, : 3 * half].reshape(part, 3, half)
    got = got[:part, : 3 * half].reshape(part, 3, half)
    matrices = side(upper, keep, got, 2)
    thin_part = lambda k: total[part, k * part : (k + 1) * part]
    reduced = reduced.astype(F32)
    own_inner = jnp.concatenate([reduced[k * part : (k + 1) * part] for k in range(ratio)], 1)
    own_outer = reduced[ratio * part :]
    return (
        layer_out,
        grad_inputs,
        matrices[:, 0],
        tail_sum[:part],
        matrices[:, 1],
        matrices[:, 2],
        tail_sum[part:],
        total[:part],
        thin_part(0),
        thin_part(1),
        thin_part(2),
        own_inner,
        total[part, 6 * part : 6 * part + inner_part],
        own_outer,
        thin_part(3),
        thin_part(4),
        thin_part(5),
    )


def solution(mesh):
    in_specs = (
        P(("dp", "seq"), None),
        P(("dp", "seq"), None),
        P(("dp", "seq")),
        P(("dp", "seq"), None),
        P(("dp", "seq"), None),
        P(("dp", "seq")),
        P(("dp", "seq"), None),
        P(("dp", "seq")),
        P(("dp", "seq")),
        P(("dp", "seq")),
        P(("dp", "seq"), None),
        P(("dp", "seq")),
        P(("dp", "seq"), None),
        P(("dp", "seq")),
        P(("dp", "seq")),
        P(("dp", "seq")),
        P(("dp", "seq"), None),
        P("dp", None),
        P("dp", None),
    )
    out_specs = (
        P(("dp", "seq"), None),
        P(("dp", "seq"), None),
        P(("dp", "seq"), None),
        P(("dp", "seq")),
        P(("dp", "seq"), None),
        P(("dp", "seq"), None),
        P(("dp", "seq")),
        P(("dp", "seq"), None),
        P(("dp", "seq")),
        P(("dp", "seq")),
        P(("dp", "seq")),
        P(("dp", "seq"), None),
        P(("dp", "seq")),
        P(("dp", "seq"), None),
        P(("dp", "seq")),
        P(("dp", "seq")),
        P(("dp", "seq")),
    )
    n_dp = mesh.shape["dp"]
    if mesh.shape["seq"] != 2 or n_dp & (n_dp - 1) != 0 or n_dp < 4:
        return jax.shard_map(
            body, mesh=mesh, in_specs=in_specs, out_specs=out_specs, check_vma=False
        )

    def chosen(*arrays):
        return fast_body(*arrays, n_dp=n_dp)

    return jax.shard_map(
        chosen, mesh=mesh, in_specs=in_specs, out_specs=out_specs, check_vma=False
    )
```

```python
from functools import partial

import jax
import jax.numpy as jnp
from jax import lax
from jax.experimental import pallas as pl
from jax.experimental.pallas import tpu as pltpu
from jax.sharding import PartitionSpec as P


H = 12
HD = 64
LEN = 2048
PIC = 256
NPIC = 2
MEM = 10


norm_epsilon = 1e-05
masked_score = -1e30


def normalize(values, gain, shift):
    centre = jnp.mean(values, -1, keepdims=True)
    centred = values - centre
    spread = jnp.mean(centred * centred, -1, keepdims=True)
    return centred * lax.rsqrt(spread + norm_epsilon) * gain + shift


def gelu_exact(values):
    return jax.nn.gelu(values, approximate=False)


def visible_cols(positions, columns, starts, memories):
    labels = jnp.arange(NPIC, dtype=jnp.int32)[:, None] + 1
    in_cols = (columns[None, :] >= starts[:, None]) & (columns[None, :] < starts[:, None] + PIC)
    in_rows = (positions[None, :] >= starts[:, None]) & (positions[None, :] < starts[:, None] + PIC)
    piece_cols = jnp.sum(jnp.where(in_cols, labels, 0), 0)
    piece_rows = jnp.sum(jnp.where(in_rows, labels, 0), 0)
    same_piece = (piece_rows[:, None] == piece_cols[None, :]) & (piece_rows[:, None] > 0)
    read_cols = jnp.any(columns[None, :] == memories[:MEM, None], 0)
    write_rows = jnp.any(positions[None, :] == memories[MEM:, None], 0)
    causal = columns[None, :] <= positions[:, None]
    return causal | same_piece | read_cols[None, :] | write_rows[:, None]


def visible(positions, starts, memories):
    return visible_cols(positions, jnp.arange(LEN, dtype=jnp.int32), starts, memories)


def dense(left, right):
    return jnp.dot(left, right, preferred_element_type=jnp.float32)


def outer_product(left, right):
    return jnp.einsum("ta,tb->ab", left, right, preferred_element_type=jnp.float32)


def back_product(gradient, weight):
    return jnp.einsum("tb,ab->ta", gradient, weight, preferred_element_type=jnp.float32)


def body(
    inputs,
    query_weight,
    query_bias,
    key_weight,
    value_weight,
    value_bias,
    output_weight,
    output_bias,
    first_gain,
    first_shift,
    inner_weight,
    inner_bias,
    outer_weight,
    outer_bias,
    second_gain,
    second_shift,
    cotangent,
    piece_start,
    memory_pos,
):
    shards = (
        query_weight,
        key_weight,
        value_weight,
        output_weight,
        inner_weight,
        outer_weight,
        query_bias,
        value_bias,
        output_bias,
        first_gain,
        first_shift,
        inner_bias,
        outer_bias,
        second_gain,
        second_shift,
    )
    gathered = (
        lax.all_gather(shards[0], ("dp", "seq"), axis=0, tiled=True),
        lax.all_gather(shards[1], ("dp", "seq"), axis=0, tiled=True),
        lax.all_gather(shards[2], ("dp", "seq"), axis=0, tiled=True),
        lax.all_gather(shards[3], ("dp", "seq"), axis=0, tiled=True),
        lax.all_gather(shards[4], ("dp", "seq"), axis=0, tiled=True),
        lax.all_gather(shards[5], ("dp", "seq"), axis=0, tiled=True),
        lax.all_gather(shards[6], ("dp", "seq"), axis=0, tiled=True),
        lax.all_gather(shards[7], ("dp", "seq"), axis=0, tiled=True),
        lax.all_gather(shards[8], ("dp", "seq"), axis=0, tiled=True),
        lax.all_gather(shards[9], ("dp", "seq"), axis=0, tiled=True),
        lax.all_gather(shards[10], ("dp", "seq"), axis=0, tiled=True),
        lax.all_gather(shards[11], ("dp", "seq"), axis=0, tiled=True),
        lax.all_gather(shards[12], ("dp", "seq"), axis=0, tiled=True),
        lax.all_gather(shards[13], ("dp", "seq"), axis=0, tiled=True),
        lax.all_gather(shards[14], ("dp", "seq"), axis=0, tiled=True),
    )
    w_query, w_key, w_value, w_output, w_inner, w_outer = gathered[:6]
    vectors = [vector.astype(jnp.float32) for vector in gathered[6:]]
    b_query, b_value, b_output, g_first, s_first, b_inner, b_outer, g_second, s_second = vectors
    local_rows = inputs.shape[0]
    model_width = inputs.shape[1]
    score_scale = HD ** (-0.5)
    pair_count = H // 2
    pair_width = 2 * HD
    block_rows = min(512, local_rows, LEN)
    block_count = local_rows // block_rows
    first_row = lax.axis_index("seq") * local_rows
    query_low = (dense(inputs, w_query) + b_query).astype(jnp.bfloat16)
    key_low = dense(inputs, w_key).astype(jnp.bfloat16)
    value_low = (dense(inputs, w_value) + b_value).astype(jnp.bfloat16)
    group_keys, group_values = (
        lax.all_gather(key_low, "seq", axis=0, tiled=True),
        lax.all_gather(value_low, "seq", axis=0, tiled=True),
    )
    group_rows = group_keys.shape[0]

    def context(block_index):
        row_start = first_row + block_index * block_rows
        seq_index = row_start // LEN
        positions = row_start - seq_index * LEN + jnp.arange(block_rows, dtype=jnp.int32)
        starts = piece_start[0]
        memories = memory_pos[0]
        allowed = visible(positions, starts, memories)
        return (seq_index, allowed, group_keys, group_values)

    def pair_part(matrix, pair_index, count):
        return lax.dynamic_slice_in_dim(matrix, pair_index * pair_width, pair_width, 1).reshape(
            count, 2, HD
        )

    def pair_scores(query_pair, key_pair, allowed):
        raw = (
            jnp.einsum("qhd,khd->hqk", query_pair, key_pair, preferred_element_type=jnp.float32)
            * score_scale
        )
        return jnp.where(allowed[None], raw, masked_score)

    def forward_block(block_index):
        _, allowed, seq_keys, seq_values = context(block_index)
        block_query = lax.dynamic_slice_in_dim(query_low, block_index * block_rows, block_rows, 0)

        def forward_pair_step(carry, pair_index):
            out_buffer, total_buffer = carry
            query_pair = pair_part(block_query, pair_index, block_rows)
            key_pair = pair_part(seq_keys, pair_index, LEN)
            value_pair = pair_part(seq_values, pair_index, LEN)
            scores = pair_scores(query_pair, key_pair, allowed)
            peak = jnp.max(scores, -1, keepdims=True)
            expo_terms = jnp.exp(scores - peak)
            row_sum = jnp.sum(expo_terms, -1, keepdims=True)
            chances_low = (expo_terms / row_sum).astype(jnp.bfloat16)
            blended = jnp.einsum(
                "hqk,khd->qhd", chances_low, value_pair, preferred_element_type=jnp.float32
            )
            blended = blended.reshape(block_rows, pair_width).astype(jnp.bfloat16)
            out_buffer = lax.dynamic_update_slice_in_dim(
                out_buffer, blended, pair_index * pair_width, 1
            )
            log_pair = (peak + jnp.log(row_sum))[:, :, 0]
            total_buffer = lax.dynamic_update_slice_in_dim(
                total_buffer, log_pair, pair_index * 2, 0
            )
            return ((out_buffer, total_buffer), None)

        initial = (
            jnp.zeros((block_rows, model_width), jnp.bfloat16),
            jnp.zeros((H, block_rows), jnp.float32),
        )
        (out_buffer, total_buffer), unused = lax.scan(
            forward_pair_step, initial, jnp.arange(pair_count)
        )
        return (out_buffer, total_buffer)

    attended_blocks, log_totals = lax.map(forward_block, jnp.arange(block_count))
    attended = attended_blocks.reshape(local_rows, model_width)
    mixed = inputs.astype(jnp.float32) + dense(attended, w_output) + b_output
    hidden_norm, first_pull = jax.vjp(normalize, mixed, g_first, s_first)
    hidden_low = hidden_norm.astype(jnp.bfloat16)
    inner = dense(hidden_low, w_inner) + b_inner
    activated_full, gelu_pull = jax.vjp(gelu_exact, inner)
    activated = activated_full.astype(jnp.bfloat16)
    second_in = hidden_norm + dense(activated, w_outer) + b_outer
    normed_out, second_pull = jax.vjp(normalize, second_in, g_second, s_second)
    layer_out = normed_out.astype(jnp.bfloat16)
    back_weights = (
        lax.all_gather(query_weight, ("dp", "seq"), axis=0, tiled=True),
        lax.all_gather(key_weight, ("dp", "seq"), axis=0, tiled=True),
        lax.all_gather(value_weight, ("dp", "seq"), axis=0, tiled=True),
        lax.all_gather(output_weight, ("dp", "seq"), axis=0, tiled=True),
        lax.all_gather(inner_weight, ("dp", "seq"), axis=0, tiled=True),
        lax.all_gather(outer_weight, ("dp", "seq"), axis=0, tiled=True),
    )
    v_query, v_key, v_value, v_output, v_inner, v_outer = back_weights
    grad_second_in, grad_second_gain, grad_second_shift = second_pull(cotangent.astype(jnp.float32))
    grad_outer_bias = jnp.sum(grad_second_in, 0)
    second_low = grad_second_in.astype(jnp.bfloat16)
    grad_outer_weight = outer_product(activated, second_low)
    (grad_inner,) = gelu_pull(back_product(second_low, v_outer))
    grad_inner_bias = jnp.sum(grad_inner, 0)
    inner_low = grad_inner.astype(jnp.bfloat16)
    grad_inner_weight = outer_product(hidden_low, inner_low)
    grad_hidden = grad_second_in + back_product(inner_low, v_inner)
    grad_mixed, grad_first_gain, grad_first_shift = first_pull(grad_hidden)
    grad_output_bias = jnp.sum(grad_mixed, 0)
    mixed_low = grad_mixed.astype(jnp.bfloat16)
    grad_output_weight = outer_product(attended, mixed_low)
    grad_attended = back_product(mixed_low, v_output).astype(jnp.bfloat16)

    def backward_block(carry, block_index):
        _, allowed, seq_keys, seq_values = context(block_index)
        block_query = lax.dynamic_slice_in_dim(query_low, block_index * block_rows, block_rows, 0)
        block_grad = lax.dynamic_slice_in_dim(
            grad_attended, block_index * block_rows, block_rows, 0
        )
        block_total = log_totals[block_index]

        def backward_pair_step(inner_carry, pair_index):
            query_grad, term_buffer = (inner_carry[0], inner_carry[1])
            query_pair = pair_part(block_query, pair_index, block_rows)
            key_pair = pair_part(seq_keys, pair_index, LEN)
            value_pair = pair_part(seq_values, pair_index, LEN)
            grad_pair = pair_part(block_grad, pair_index, block_rows)
            scores = pair_scores(query_pair, key_pair, allowed)
            total_pair = lax.dynamic_slice_in_dim(block_total, pair_index * 2, 2, 0)
            chances = jnp.exp(scores - total_pair[:, :, None])
            chance_grad = jnp.einsum(
                "qhd,khd->hqk", grad_pair, value_pair, preferred_element_type=jnp.float32
            )
            row_terms = jnp.sum(chances * chance_grad, -1, keepdims=True)
            score_grad = (chances * (chance_grad - row_terms)).astype(jnp.bfloat16)
            query_part = jnp.einsum(
                "hqk,khd->qhd", score_grad, key_pair, preferred_element_type=jnp.float32
            )
            query_part = query_part.reshape(block_rows, pair_width) * score_scale
            query_grad = lax.dynamic_update_slice_in_dim(
                query_grad, query_part, pair_index * pair_width, 1
            )
            term_buffer = lax.dynamic_update_slice_in_dim(
                term_buffer, row_terms[:, :, 0], pair_index * 2, 0
            )
            seq_key_grad, seq_value_grad = (inner_carry[2], inner_carry[3])
            chances_low = chances.astype(jnp.bfloat16)
            key_part = jnp.einsum(
                "hqk,qhd->khd", score_grad, query_pair, preferred_element_type=jnp.float32
            )
            value_part = jnp.einsum(
                "hqk,qhd->khd", chances_low, grad_pair, preferred_element_type=jnp.float32
            )
            key_part = key_part.reshape(LEN, pair_width) * score_scale
            value_part = value_part.reshape(LEN, pair_width)
            seq_key_grad = lax.dynamic_update_slice_in_dim(
                seq_key_grad, key_part, pair_index * pair_width, 1
            )
            seq_value_grad = lax.dynamic_update_slice_in_dim(
                seq_value_grad, value_part, pair_index * pair_width, 1
            )
            return ((query_grad, term_buffer, seq_key_grad, seq_value_grad), None)

        initial = (
            jnp.zeros((block_rows, model_width), jnp.float32),
            jnp.zeros((H, block_rows), jnp.float32),
        )
        initial = initial + (
            jnp.zeros((LEN, model_width), jnp.float32),
            jnp.zeros((LEN, model_width), jnp.float32),
        )
        finals, _ = lax.scan(backward_pair_step, initial, jnp.arange(pair_count))
        key_grads, value_grads = carry
        key_grads = key_grads + finals[2]
        value_grads = value_grads + finals[3]
        carry = (key_grads, value_grads)
        return (carry, (finals[0], finals[1]))

    group_zero = jnp.zeros((group_rows, model_width), jnp.float32)
    (key_grads, value_grads), (query_blocks, term_blocks) = lax.scan(
        backward_block, (group_zero, group_zero), jnp.arange(block_count)
    )
    key_sum, value_sum = (
        lax.psum_scatter(
            key_grads.astype(jnp.bfloat16), "seq", scatter_dimension=0, tiled=True
        ).astype(jnp.float32),
        lax.psum_scatter(
            value_grads.astype(jnp.bfloat16), "seq", scatter_dimension=0, tiled=True
        ).astype(jnp.float32),
    )
    query_sum = query_blocks.reshape(local_rows, model_width)
    grad_query_bias = jnp.sum(query_sum, 0)
    grad_value_bias = jnp.sum(value_sum, 0)
    query_grad_low = query_sum.astype(jnp.bfloat16)
    key_grad_low = key_sum.astype(jnp.bfloat16)
    value_grad_low = value_sum.astype(jnp.bfloat16)
    grad_query_weight = outer_product(inputs, query_grad_low)
    grad_key_weight = outer_product(inputs, key_grad_low)
    grad_value_weight = outer_product(inputs, value_grad_low)
    grad_inputs = (
        grad_mixed
        + back_product(query_grad_low, v_query)
        + back_product(key_grad_low, v_key)
        + back_product(value_grad_low, v_value)
    )
    grads = (
        grad_query_weight,
        grad_key_weight,
        grad_value_weight,
        grad_output_weight,
        grad_inner_weight,
        grad_outer_weight,
        grad_query_bias,
        grad_value_bias,
        grad_output_bias,
        grad_first_gain,
        grad_first_shift,
        grad_inner_bias,
        grad_outer_bias,
        grad_second_gain,
        grad_second_shift,
    )
    owned = (
        lax.psum_scatter(grads[0], ("dp", "seq"), scatter_dimension=0, tiled=True),
        lax.psum_scatter(grads[1], ("dp", "seq"), scatter_dimension=0, tiled=True),
        lax.psum_scatter(grads[2], ("dp", "seq"), scatter_dimension=0, tiled=True),
        lax.psum_scatter(grads[3], ("dp", "seq"), scatter_dimension=0, tiled=True),
        lax.psum_scatter(grads[4], ("dp", "seq"), scatter_dimension=0, tiled=True),
        lax.psum_scatter(grads[5], ("dp", "seq"), scatter_dimension=0, tiled=True),
        lax.psum_scatter(grads[6], ("dp", "seq"), scatter_dimension=0, tiled=True),
        lax.psum_scatter(grads[7], ("dp", "seq"), scatter_dimension=0, tiled=True),
        lax.psum_scatter(grads[8], ("dp", "seq"), scatter_dimension=0, tiled=True),
        lax.psum_scatter(grads[9], ("dp", "seq"), scatter_dimension=0, tiled=True),
        lax.psum_scatter(grads[10], ("dp", "seq"), scatter_dimension=0, tiled=True),
        lax.psum_scatter(grads[11], ("dp", "seq"), scatter_dimension=0, tiled=True),
        lax.psum_scatter(grads[12], ("dp", "seq"), scatter_dimension=0, tiled=True),
        lax.psum_scatter(grads[13], ("dp", "seq"), scatter_dimension=0, tiled=True),
        lax.psum_scatter(grads[14], ("dp", "seq"), scatter_dimension=0, tiled=True),
    )
    return (
        layer_out,
        grad_inputs,
        owned[0],
        owned[6],
        owned[1],
        owned[2],
        owned[7],
        owned[3],
        owned[8],
        owned[9],
        owned[10],
        owned[4],
        owned[11],
        owned[5],
        owned[12],
        owned[13],
        owned[14],
    )


F32=jnp.float32; BF=jnp.bfloat16
NT=(((1,),(1,)),((),()))
NN=(((1,),(0,)),((),()))


def mm(a,b,dims=NN):
    return lax.dot_general(a,b,dims,preferred_element_type=F32)


GROUP=16


def half_mask(shape, head, dim):
    lanes=lax.broadcasted_iota(jnp.int32,shape,dim)
    return (lanes<64) if head==0 else (lanes>=64)


def only(x, head):
    return jnp.where(half_mask(x.shape,head,1),x,jnp.zeros_like(x))


def take_rows(ref, pos_ref, first):
    width=ref.shape[1]
    out=jnp.zeros((GROUP,width),F32)
    rows=lax.broadcasted_iota(jnp.int32,(GROUP,width),0)
    for m in range(MEM):
        pos=pos_ref[first+m]
        start=pl.multiple_of((pos//GROUP)*GROUP,GROUP)
        part=ref[pl.ds(start,GROUP),:].astype(F32)
        row=jnp.sum(jnp.where(rows==pos-start,part,0.0),0,keepdims=True)
        out=jnp.where(rows==m,row,out)
    return out.astype(BF)


def put_rows(ref, pos_ref, first, values, add):
    width=ref.shape[1]
    rows=lax.broadcasted_iota(jnp.int32,(GROUP,width),0)
    for m in range(MEM):
        pos=pos_ref[first+m]
        start=pl.multiple_of((pos//GROUP)*GROUP,GROUP)
        old=ref[pl.ds(start,GROUP),:].astype(F32)
        row=values[m:m+1,:]
        new=jnp.where(rows==pos-start,old+row if add else row,old)
        ref[pl.ds(start,GROUP),:]=new.astype(ref.dtype)


def transposed(x):
    return jnp.transpose(x.astype(F32)).astype(BF)


def fwd_kernel(pos_ref, posv_ref, limit_ref, write_ref, qkv_ref, o_ref, lse_ref, vt_ref, qt_ref, acc_ref, *, bq, np_, qb0, qb1):
    rows_all=qkv_ref.shape[0]
    nq=rows_all//bq
    W=np_*128
    nh=2*np_
    cols=lambda part,p:slice(part*W+p*128,part*W+p*128+128)
    hr=lambda h:slice(80*h,80*h+80)
    mem=take_rows(qkv_ref,pos_ref,0)
    kr=[only(mem[:,cols(1,h//2)],h%2) for h in range(nh)]
    ones16=jnp.ones((16,GROUP),BF)
    vrt=[]
    for p in range(np_):
        vt=transposed(qkv_ref[:,cols(2,p)])
        mt=transposed(mem[:,cols(2,p)])
        qt_ref[p*128:p*128+128,:]=transposed(qkv_ref[:,cols(0,p)])
        for h in range(2):
            vt_ref[80*(2*p+h):80*(2*p+h)+64,:]=vt[64*h:64*h+64]
            vt_ref[80*(2*p+h)+64:80*(2*p+h)+80,:]=jnp.ones((16,rows_all),BF)
            vrt.append(jnp.concatenate([mt[64*h:64*h+64],ones16],0))
    read_pos=posv_ref[...]
    def q_step(qb, unused):
        q0=pl.multiple_of(qb*bq,bq)
        limit=limit_ref[:,pl.ds(q0,bq)][0:1]
        key_iota=lax.broadcasted_iota(jnp.int32,(bq,bq),0)
        zq=jnp.zeros((64,bq),BF)
        def qh(h):
            own=qt_ref[64*h:64*h+64,pl.ds(q0,bq)]
            return jnp.concatenate([own,zq] if h%2==0 else [zq,own],0)
        def soft(h,s,vt,m):
            m2=jnp.maximum(m,jnp.max(s,0,keepdims=True))
            fix=jnp.exp2(m-m2)
            p=jnp.exp2(s-m2)
            acc_ref[hr(h),:]=acc_ref[hr(h),:]*fix+mm(vt,p.astype(BF))
            return m2
        def block(kb,carry,mask):
            k0=pl.multiple_of(kb*bq,bq)
            ss=[mm(qkv_ref[pl.ds(k0,bq),cols(1,h//2)],qh(h)) for h in range(nh)]
            if mask:
                ss=[jnp.where(key_iota+k0<=limit,s,masked_score) for s in ss]
            return tuple(soft(h,ss[h],vt_ref[hr(h),pl.ds(k0,bq)],carry[h]) for h in range(nh))
        acc_ref[...]=jnp.zeros_like(acc_ref)
        carry=tuple(jnp.full((1,bq),masked_score,F32) for _ in range(nh))
        carry=block(qb,carry,True)
        carry=tuple(soft(h,jnp.where(read_pos>limit,mm(kr[h],qh(h)),masked_score),vrt[h],carry[h]) for h in range(nh))
        carry=lax.fori_loop(0,qb,lambda kb,c:block(kb,c,False),carry)
        far=jnp.max(limit)>=q0+bq
        carry=lax.cond(far,lambda c:block(jnp.minimum(qb+1,nq-1),c,True),lambda c:c,carry)
        wr=write_ref[:,pl.ds(q0,bq)][0:1]
        outs=[]
        for h in range(nh):
            l=acc_ref[80*h+64:80*h+65,:]
            outs.append(acc_ref[80*h:80*h+64,:]/l)
            lse=carry[h]+jnp.log2(l)
            lse_ref[h:h+1,pl.ds(q0,bq)]=jnp.where(wr>0,1e30,lse)
        o_ref[pl.ds(q0,bq),:]=jnp.transpose(jnp.concatenate(outs,0)).astype(BF)
        return unused
    lax.fori_loop(qb0,qb1,q_step,0)
    rows=take_rows(qkv_ref,pos_ref,MEM)
    out=[]
    for p in range(np_):
        total=jnp.zeros((GROUP,128),F32)
        qw=rows[:,cols(0,p)]
        for h in range(2):
            s=mm(only(qw,h),qkv_ref[:,cols(1,p)],NT)
            m=jnp.max(s,1,keepdims=True)
            e=jnp.exp2(s-m)
            l=jnp.sum(e,1,keepdims=True)
            ow=mm(e.astype(BF),qkv_ref[:,cols(2,p)])/l
            total=total+jnp.where(half_mask((GROUP,128),h,1),ow,0.0)
        out.append(total)
    put_rows(o_ref,pos_ref,MEM,jnp.concatenate(out,1),False)


LN2=0.6931471805599453


def bwd_kernel(pos_ref, posv_ref, limit_ref, qkv_ref, do_ref, o_ref, lse_ref,
               dqkv_ref, bias_ref, qt_ref, kt_ref, dot_ref, dk_acc, dv_acc, dq_acc, dr_acc, *, bq, scale, np_):
    rows_all=qkv_ref.shape[0]
    nq=rows_all//bq
    W=np_*128
    nh=2*np_
    cols=lambda part,p:slice(part*W+p*128,part*W+p*128+128)
    pc=lambda p:slice(p*128,p*128+128)
    hr=lambda h:slice(64*h,64*h+64)
    for p in range(np_):
        qt_ref[pc(p),:]=transposed(qkv_ref[:,cols(0,p)])
        kt_ref[pc(p),:]=transposed(qkv_ref[:,cols(1,p)])
        dot_ref[pc(p),:]=transposed(do_ref[:,pc(p)])
    mem=take_rows(qkv_ref,pos_ref,0)
    kr=[mem[:,cols(1,p)] for p in range(np_)]
    vr=[mem[:,cols(2,p)] for p in range(np_)]
    krt=[transposed(kr[p]) for p in range(np_)]
    read_pos=posv_ref[...]
    rows=take_rows(qkv_ref,pos_ref,MEM)
    dow_all=take_rows(do_ref,pos_ref,MEM)
    valid=lax.broadcasted_iota(jnp.int32,(GROUP,1),0)<MEM
    dqw_all=[]
    for pr in range(np_):
        qw=rows[:,cols(0,pr)]
        dow=dow_all[:,pc(pr)]
        qwt=transposed(qw); dowt=transposed(dow)
        dqw=jnp.zeros((GROUP,128),F32)
        for h in range(2):
            s=mm(only(qw,h),qkv_ref[:,cols(1,pr)],NT)
            m=jnp.max(s,1,keepdims=True)
            p=jnp.exp2(s-m)
            p=p*jnp.where(valid,1.0/jnp.sum(p,1,keepdims=True),0.0)
            dp=mm(only(dow,h),qkv_ref[:,cols(2,pr)],NT)
            ds=(p*(dp-jnp.sum(p*dp,1,keepdims=True))).astype(BF)
            dqw=dqw+jnp.where(half_mask((GROUP,128),h,1),mm(ds,qkv_ref[:,cols(1,pr)]),0.0)
            dk_acc[hr(2*pr+h),:]=mm(qwt[64*h:64*h+64],ds)
            dv_acc[hr(2*pr+h),:]=mm(dowt[64*h:64*h+64],p.astype(BF))
        dqw_all.append(dqw)
    dr_acc[...]=jnp.zeros_like(dr_acc)
    def q_step(qb, unused):
        q0=pl.multiple_of(qb*bq,bq)
        limit=limit_ref[:,pl.ds(q0,bq)][0:1]
        zq=jnp.zeros((64,bq),BF)
        def padded(ref,h):
            own=ref[hr(h),pl.ds(q0,bq)]
            return jnp.concatenate([own,zq] if h%2==0 else [zq,own],0)
        prod=jnp.transpose(do_ref[pl.ds(q0,bq),:].astype(F32)*o_ref[pl.ds(q0,bq),:].astype(F32))
        delta=[jnp.sum(prod[hr(h)],0,keepdims=True) for h in range(nh)]
        lse=[lse_ref[h:h+1,pl.ds(q0,bq)] for h in range(nh)]
        key_iota=lax.broadcasted_iota(jnp.int32,(bq,bq),0)
        dq_acc[...]=jnp.zeros_like(dq_acc)
        def grads(h,s,v):
            p=jnp.exp2(s-lse[h])
            dp=mm(v,padded(dot_ref,h))
            return (p*(dp-delta[h])).astype(BF),p.astype(BF)
        def block(kb,mask):
            k0=pl.multiple_of(kb*bq,bq)
            ks=pl.ds(k0,bq)
            held={}
            def front(h):
                s=mm(qkv_ref[ks,cols(1,h//2)],padded(qt_ref,h))
                if mask:
                    s=jnp.where(key_iota+k0<=limit,s,masked_score)
                held[h]=(s,mm(qkv_ref[ks,cols(2,h//2)],padded(dot_ref,h)))
            def middle(h):
                s,dp=held[h]
                p=jnp.exp2(s-lse[h])
                held[h]=((p*(dp-delta[h])).astype(BF),p.astype(BF))
            def back(h):
                ds,p=held[h]
                dq_acc[hr(h),:]+=mm(kt_ref[hr(h),ks],ds)
                dk_acc[hr(h),ks]+=mm(qt_ref[hr(h),pl.ds(q0,bq)],ds,NT)
                dv_acc[hr(h),ks]+=mm(dot_ref[hr(h),pl.ds(q0,bq)],p,NT)
            for h in range(nh+2):
                if h<nh:
                    front(h)
                if 0<=h-1<nh:
                    middle(h-1)
                if h>=2:
                    back(h-2)
        block(qb,True)
        for h in range(nh):
            s=jnp.where(read_pos>limit,mm(kr[h//2],padded(qt_ref,h)),masked_score)
            ds,p=grads(h,s,vr[h//2])
            dr_acc[0,hr(h),:]+=mm(qt_ref[hr(h),pl.ds(q0,bq)],ds,NT)
            dr_acc[1,hr(h),:]+=mm(dot_ref[hr(h),pl.ds(q0,bq)],p,NT)
            dq_acc[hr(h),:]+=mm(krt[h//2][64*(h%2):64*(h%2)+64,:],ds)
        def step(kb,c):
            block(kb,False)
            return c
        lax.fori_loop(0,qb,step,0)
        @pl.when(jnp.max(limit)>=q0+bq)
        def _():
            block(jnp.minimum(qb+1,nq-1),True)
        dqkv_ref[pl.ds(q0,bq),0:W]=(jnp.transpose(dq_acc[...])*scale).astype(BF)
        return unused
    lax.fori_loop(0,nq,q_step,0)
    put_rows(dqkv_ref.at[:,0:W],pos_ref,MEM,jnp.concatenate(dqw_all,1)*scale,False)
    for p in range(np_):
        dqkv_ref[:,cols(1,p)]=(jnp.transpose(dk_acc[pc(p),:])*LN2).astype(BF)
        dqkv_ref[:,cols(2,p)]=jnp.transpose(dv_acc[pc(p),:]).astype(BF)
    put_rows(dqkv_ref.at[:,W:2*W],pos_ref,0,jnp.transpose(dr_acc[0])*LN2,True)
    put_rows(dqkv_ref.at[:,2*W:3*W],pos_ref,0,jnp.transpose(dr_acc[1]),True)
    rows8=lax.broadcasted_iota(jnp.int32,(8,W),0)
    bq_sum=jnp.sum(dqkv_ref[:,0:W].astype(F32),0,keepdims=True)
    bv_sum=jnp.sum(dqkv_ref[:,2*W:3*W].astype(F32),0,keepdims=True)
    bias_ref[...]=jnp.where(rows8==0,bq_sum,jnp.where(rows8==1,bv_sum,0.0))


ONCE=pl.Buffered(1)


def attn_fwd(qkv, pos, posv, limit, write, np_, bq=256, qb0=0, qb1=None):
    L=qkv.shape[0]; W=np_*128
    row8=pl.BlockSpec((8,L),lambda i:(0,0),pipeline_mode=ONCE)
    full=lambda w:pl.BlockSpec((L,w),lambda i:(0,0),pipeline_mode=ONCE)
    return pl.pallas_call(partial(fwd_kernel,bq=bq,np_=np_,qb0=qb0,qb1=L//bq if qb1 is None else qb1),
        grid=(1,),
        in_specs=[pl.BlockSpec(memory_space=pltpu.SMEM),pl.BlockSpec((GROUP,1),lambda i:(0,0)),row8,row8,full(3*W)],
        out_specs=[full(W),row8],
        out_shape=[jax.ShapeDtypeStruct((L,W),BF),jax.ShapeDtypeStruct((8,L),F32)],
        scratch_shapes=[pltpu.VMEM((np_*160,L),BF),pltpu.VMEM((W,L),BF),pltpu.VMEM((np_*160,bq),F32)],
        name="attn_fwd",
    )(pos,posv,limit,write,qkv)


def attn_bwd(qkv, pos, posv, limit, do, o, lse, np_, scale, bq=256):
    L=qkv.shape[0]; W=np_*128
    row8=pl.BlockSpec((8,L),lambda i:(0,0),pipeline_mode=ONCE)
    full=lambda w:pl.BlockSpec((L,w),lambda i:(0,0),pipeline_mode=ONCE)
    return pl.pallas_call(partial(bwd_kernel,bq=bq,scale=scale,np_=np_),
        grid=(1,),
        in_specs=[pl.BlockSpec(memory_space=pltpu.SMEM),pl.BlockSpec((GROUP,1),lambda i:(0,0)),row8,full(3*W),full(W),full(W),row8],
        out_specs=[full(3*W),pl.BlockSpec((8,W),lambda i:(0,0))],
        out_shape=[jax.ShapeDtypeStruct((L,3*W),BF),jax.ShapeDtypeStruct((8,W),F32)],
        scratch_shapes=[pltpu.VMEM((W,L),BF)]*3+[pltpu.VMEM((W,L),F32)]*2+[pltpu.VMEM((W,bq),F32),pltpu.VMEM((2,W,GROUP),F32)],
        name="attn_bwd",
    )(pos,posv,limit,qkv,do,o,lse)


LANES = 128
LOG2E = 1.4426950408889634
ALL = ("dp", "seq")
RSQRT2 = 0.7071067811865476
RSQRT2PI = 0.3989422804014327


def bit_swap(x, axis, size, bit):
    return lax.ppermute(x, axis, [(i, i ^ bit) for i in range(size)])


def side(flag, own, peer, axis):
    low = jnp.where(flag, peer, own)
    high = jnp.where(flag, own, peer)
    return jnp.concatenate([low, high], axis)


def bits_of(size):
    out = []
    bit = 1
    while bit < size:
        out.append(bit)
        bit *= 2
    return out


def gather_dp(block, size):
    bits = bits_of(size)[::-1]
    index = lax.axis_index("dp")
    out = block
    for bit in bits:
        other = bit_swap(out, "dp", size, bit)
        up = (index & bit) != 0
        out = jnp.stack([jnp.where(up, other, out), jnp.where(up, out, other)])
    count = len(bits)
    out = out.transpose(tuple(range(count))[::-1] + tuple(range(count, out.ndim)))
    return out.reshape((size,) + block.shape)


def halve_dp(rest, size, bit):
    up = (lax.axis_index("dp") & bit) != 0
    rest = rest.reshape((rest.shape[0] // 2, 2) + rest.shape[1:])
    give = jnp.where(up, rest[:, 0], rest[:, 1]).astype(BF)
    keep = jnp.where(up, rest[:, 1], rest[:, 0])
    got = bit_swap(give, "dp", size, bit)
    return keep + got.astype(F32)


def spread_lanes(rows, part):
    rows = jnp.pad(rows, ((0, 0), (0, part * LANES - rows.shape[1])))
    return rows.reshape(rows.shape[0], part, LANES)


def norm_parts(values):
    centre = jnp.mean(values, -1, keepdims=True)
    centred = values - centre
    spread = jnp.mean(centred * centred, -1, keepdims=True)
    factor = lax.rsqrt(spread + norm_epsilon)
    return centred * factor, factor


def norm_back(gradient, unit, factor):
    return factor * (
        gradient
        - jnp.mean(gradient, -1, keepdims=True)
        - unit * jnp.mean(gradient * unit, -1, keepdims=True)
    )


def fast_body(
    inputs,
    query_weight,
    query_bias,
    key_weight,
    value_weight,
    value_bias,
    output_weight,
    output_bias,
    first_gain,
    first_shift,
    inner_weight,
    inner_bias,
    outer_weight,
    outer_bias,
    second_gain,
    second_shift,
    cotangent,
    piece_start,
    memory_pos,
    *,
    n_dp,
):
    rows, width = inputs.shape
    inner_width = inner_weight.shape[1]
    devices = 2 * n_dp
    part = width // devices
    inner_part = inner_width // devices
    ratio = inner_width // width
    half = width // 2
    seq = lax.axis_index("seq")
    upper = seq == 1

    def swap(x):
        return bit_swap(x, "seq", 2, 1)

    wide = inner_weight.reshape(part, ratio, width).transpose(1, 0, 2).reshape(ratio * part, width)
    packed = jnp.concatenate([output_weight, wide, outer_weight], 0)
    late = lax.all_gather(packed, ALL, axis=0, tiled=False)
    peer_inputs = swap(inputs)
    vectors = jnp.concatenate(
        [
            query_bias,
            value_bias,
            output_bias,
            first_gain,
            first_shift,
            outer_bias,
            second_gain,
            second_shift,
            inner_bias,
        ]
    )
    count = vectors.shape[0]
    three = jnp.stack([query_weight, key_weight, value_weight], 1)
    three = three.reshape(part, 3, 2, half)
    line = jnp.pad(vectors, (0, part * LANES - count)).reshape(part, LANES)

    def columns(upper_half):
        kept = jnp.where(upper_half, three[:, :, 1], three[:, :, 0]).reshape(part, 3 * half)
        return jnp.concatenate([kept, line], 1)

    pair = side(upper, columns(upper)[None], swap(columns(jnp.logical_not(upper)))[None], 0)
    early = gather_dp(pair, n_dp).reshape(width, 3 * half + LANES)
    w_three = early[:, : 3 * half]
    lines = early[:, 3 * half :].astype(F32).reshape(devices, part * LANES)
    vector = lambda k: lines[:, k * part : (k + 1) * part].reshape(width)
    b_query, b_value, b_output, g_first, s_first, b_outer, g_second, s_second = map(vector, range(8))
    b_inner = lines[:, 8 * part : count].reshape(inner_width)
    own_half = lambda v: jnp.where(upper, v[half:], v[:half])
    features = side(upper, inputs, peer_inputs, 0)
    scale = HD ** (-0.5)
    shift = jnp.concatenate([own_half(b_query), jnp.zeros((half,), F32), own_half(b_value)])
    grow = jnp.concatenate([jnp.full((half,), scale * LOG2E, F32), jnp.ones((2 * half,), F32)])
    qkv = ((dense(features, w_three) + shift) * grow).astype(BF)
    positions = jnp.arange(2 * rows, dtype=jnp.int32)
    limit = positions
    for piece in range(NPIC):
        start = piece_start[0, piece]
        inside = (positions >= start) & (positions < start + PIC)
        limit = jnp.where(inside, start + PIC - 1, limit)
    memories = memory_pos[0]
    writes = jnp.any(positions[None, :] == memories[MEM:, None], 0).astype(jnp.int32)
    limit = jnp.broadcast_to(limit, (8, 2 * rows))
    writes = jnp.broadcast_to(writes, (8, 2 * rows))
    reads = jnp.pad(memories[:MEM], (0, GROUP - MEM), constant_values=-1)[:, None]
    pairs = half // (2 * HD)
    out_heads, totals = attn_fwd(qkv, memories, reads, limit, writes, pairs)
    other_rows = jnp.where(upper, out_heads[:rows], out_heads[rows:])
    own_rows = jnp.where(upper, out_heads[rows:], out_heads[:rows])
    attended = side(upper, own_rows, swap(other_rows), 1)
    w_output = late[:, :part].reshape(width, width)
    w_inner = jnp.concatenate(
        [
            late[:, part + k * part : 2 * part + k * part].reshape(width, width)
            for k in range(ratio)
        ],
        1,
    )
    w_outer = late[:, part + ratio * part :].reshape(inner_width, width)
    mixed = inputs.astype(F32) + dense(attended, w_output) + b_output
    first_unit, first_factor = norm_parts(mixed)
    hidden_norm = first_unit * g_first + s_first
    hidden_low = hidden_norm.astype(BF)
    inner = dense(hidden_low, w_inner) + b_inner
    chance = 0.5 * (1.0 + lax.erf(inner * RSQRT2))
    activated = (inner * chance).astype(BF)
    slope = (chance + inner * (RSQRT2PI * jnp.exp(-0.5 * inner * inner))).astype(BF)
    activated, slope = lax.optimization_barrier((activated, slope))
    second_in = hidden_norm + dense(activated, w_outer) + b_outer
    second_unit, second_factor = norm_parts(second_in)
    layer_out = (second_unit * g_second + s_second).astype(BF)
    cot = cotangent.astype(F32)
    grad_second_gain = jnp.sum(cot * second_unit, 0)
    grad_second_shift = jnp.sum(cot, 0)
    grad_second_in = norm_back(cot * g_second, second_unit, second_factor)
    grad_outer_bias = jnp.sum(grad_second_in, 0)
    second_low = grad_second_in.astype(BF)
    grad_inner = back_product(second_low, w_outer) * slope.astype(F32)
    grad_inner_bias = jnp.sum(grad_inner, 0)
    inner_low = grad_inner.astype(BF)
    column = lambda k: inner_low[:, k * width : (k + 1) * width]
    inner_blocks = [
        outer_product(hidden_low, column(k)).astype(BF).reshape(devices, part, width)
        for k in range(ratio)
    ]
    grad_outer_weight = outer_product(activated, second_low).astype(BF)
    bundle = jnp.concatenate(
        inner_blocks + [grad_outer_weight.reshape(devices, inner_part, width)], 1
    )
    bundle_rows = bundle.shape[1]
    bundle, inner_low = lax.optimization_barrier((bundle, inner_low))
    reduced = lax.psum_scatter(
        bundle.reshape(devices * bundle_rows, width), ALL, scatter_dimension=0, tiled=True
    )
    grad_hidden = grad_second_in + back_product(inner_low, w_inner)
    grad_first_gain = jnp.sum(grad_hidden * first_unit, 0)
    grad_first_shift = jnp.sum(grad_hidden, 0)
    grad_mixed = norm_back(grad_hidden * g_first, first_unit, first_factor)
    grad_output_bias = jnp.sum(grad_mixed, 0)
    mixed_low = grad_mixed.astype(BF)
    grad_attended = back_product(mixed_low, w_output).astype(BF)
    grad_other = jnp.where(upper, grad_attended[:, :half], grad_attended[:, half:])
    grad_own = jnp.where(upper, grad_attended[:, half:], grad_attended[:, :half])
    grad_heads = side(upper, grad_own, swap(grad_other), 0)
    grad_output_weight = outer_product(attended, mixed_low).reshape(devices, part, width)
    thin = [
        grad_output_bias,
        grad_first_gain,
        grad_first_shift,
        grad_outer_bias,
        grad_second_gain,
        grad_second_shift,
    ]
    thin = jnp.concatenate(
        [v.reshape(devices, part) for v in thin] + [grad_inner_bias.reshape(devices, inner_part)], 1
    )
    mid = jnp.concatenate([grad_output_weight, spread_lanes(thin, part)], 2)
    mid = mid.reshape(n_dp, 2, part, width + LANES)
    bits = bits_of(n_dp)
    mid = halve_dp(mid, n_dp, bits[0])
    mid = halve_dp(mid, n_dp, bits[1])
    grads, bias_sums = attn_bwd(
        qkv, memories, reads, limit, grad_heads, out_heads, totals, pairs, scale
    )
    other_grads = jnp.where(upper, grads[:rows], grads[rows:])
    own_grads = jnp.where(upper, grads[rows:], grads[:rows])
    for_peer = back_product(other_grads, w_three).astype(BF)
    for_peer, grads = lax.optimization_barrier((for_peer, grads))
    sent = swap(for_peer)
    three_grad = outer_product(features, grads).reshape(devices, part, 3 * half)
    full = lambda v: side(upper, v, jnp.zeros_like(v), 0).reshape(devices, part)
    tails = jnp.concatenate([full(bias_sums[0]), full(bias_sums[1])], 1)
    blocks = jnp.concatenate([three_grad, spread_lanes(tails, part)], 2)
    wide_half = 3 * half + LANES
    blocks = blocks.reshape(n_dp, 2, part, wide_half)
    blocks = halve_dp(blocks, n_dp, bits[0])
    own_part = lax.optimization_barrier(grad_mixed + back_product(own_grads, w_three))
    blocks = halve_dp(blocks, n_dp, bits[1])
    blocks = jnp.concatenate([blocks, mid], 3)
    for bit in bits[2:]:
        blocks = halve_dp(blocks, n_dp, bit)
    mine = blocks[0]
    give = jnp.where(upper, mine[0], mine[1])
    keep = jnp.where(upper, mine[1], mine[0])
    got = swap(give.astype(BF)).astype(F32)
    grad_inputs = own_part + sent.astype(F32)
    total = keep[:, wide_half : wide_half + width] + got[:, wide_half : wide_half + width]
    ends = lambda x: x[:, wide_half + width :].reshape(-1)
    thin_sum = ends(keep) + ends(got)
    ends = lambda x: x[:, 3 * half : wide_half].reshape(-1)
    tail_sum = ends(keep) + ends(got)
    keep = keep[:, : 3 * half].reshape(part, 3, half)
    got = got[:, : 3 * half].reshape(part, 3, half)
    matrices = side(upper, keep, got, 2)
    thin_part = lambda k: thin_sum[k * part : (k + 1) * part]
    reduced = reduced.astype(F32)
    own_inner = jnp.concatenate([reduced[k * part : (k + 1) * part] for k in range(ratio)], 1)
    own_outer = reduced[ratio * part :]
    return (
        layer_out,
        grad_inputs,
        matrices[:, 0],
        tail_sum[:part],
        matrices[:, 1],
        matrices[:, 2],
        tail_sum[part : 2 * part],
        total,
        thin_part(0),
        thin_part(1),
        thin_part(2),
        own_inner,
        thin_sum[6 * part : 6 * part + inner_part],
        own_outer,
        thin_part(3),
        thin_part(4),
        thin_part(5),
    )


def solution(mesh):
    in_specs = (
        P(("dp", "seq"), None),
        P(("dp", "seq"), None),
        P(("dp", "seq")),
        P(("dp", "seq"), None),
        P(("dp", "seq"), None),
        P(("dp", "seq")),
        P(("dp", "seq"), None),
        P(("dp", "seq")),
        P(("dp", "seq")),
        P(("dp", "seq")),
        P(("dp", "seq"), None),
        P(("dp", "seq")),
        P(("dp", "seq"), None),
        P(("dp", "seq")),
        P(("dp", "seq")),
        P(("dp", "seq")),
        P(("dp", "seq"), None),
        P("dp", None),
        P("dp", None),
    )
    out_specs = (
        P(("dp", "seq"), None),
        P(("dp", "seq"), None),
        P(("dp", "seq"), None),
        P(("dp", "seq")),
        P(("dp", "seq"), None),
        P(("dp", "seq"), None),
        P(("dp", "seq")),
        P(("dp", "seq"), None),
        P(("dp", "seq")),
        P(("dp", "seq")),
        P(("dp", "seq")),
        P(("dp", "seq"), None),
        P(("dp", "seq")),
        P(("dp", "seq"), None),
        P(("dp", "seq")),
        P(("dp", "seq")),
        P(("dp", "seq")),
    )
    n_dp = mesh.shape["dp"]
    if mesh.shape["seq"] != 2 or n_dp & (n_dp - 1) != 0 or n_dp < 4:
        return jax.shard_map(
            body, mesh=mesh, in_specs=in_specs, out_specs=out_specs, check_vma=False
        )

    def chosen(*arrays):
        return fast_body(*arrays, n_dp=n_dp)

    return jax.shard_map(
        chosen, mesh=mesh, in_specs=in_specs, out_specs=out_specs, check_vma=False
    )
```

```python
from functools import partial

import jax
import jax.numpy as jnp
from jax import lax
from jax.experimental import pallas as pl
from jax.experimental.pallas import tpu as pltpu
from jax.sharding import PartitionSpec as P


H = 12
HD = 64
LEN = 2048
PIC = 256
NPIC = 2
MEM = 10


norm_epsilon = 1e-05
masked_score = -1e30


def normalize(values, gain, shift):
    centre = jnp.mean(values, -1, keepdims=True)
    centred = values - centre
    spread = jnp.mean(centred * centred, -1, keepdims=True)
    return centred * lax.rsqrt(spread + norm_epsilon) * gain + shift


def gelu_exact(values):
    return jax.nn.gelu(values, approximate=False)


def visible_cols(positions, columns, starts, memories):
    labels = jnp.arange(NPIC, dtype=jnp.int32)[:, None] + 1
    in_cols = (columns[None, :] >= starts[:, None]) & (columns[None, :] < starts[:, None] + PIC)
    in_rows = (positions[None, :] >= starts[:, None]) & (positions[None, :] < starts[:, None] + PIC)
    piece_cols = jnp.sum(jnp.where(in_cols, labels, 0), 0)
    piece_rows = jnp.sum(jnp.where(in_rows, labels, 0), 0)
    same_piece = (piece_rows[:, None] == piece_cols[None, :]) & (piece_rows[:, None] > 0)
    read_cols = jnp.any(columns[None, :] == memories[:MEM, None], 0)
    write_rows = jnp.any(positions[None, :] == memories[MEM:, None], 0)
    causal = columns[None, :] <= positions[:, None]
    return causal | same_piece | read_cols[None, :] | write_rows[:, None]


def visible(positions, starts, memories):
    return visible_cols(positions, jnp.arange(LEN, dtype=jnp.int32), starts, memories)


def dense(left, right):
    return jnp.dot(left, right, preferred_element_type=jnp.float32)


def outer_product(left, right):
    return jnp.einsum("ta,tb->ab", left, right, preferred_element_type=jnp.float32)


def back_product(gradient, weight):
    return jnp.einsum("tb,ab->ta", gradient, weight, preferred_element_type=jnp.float32)


def body(
    inputs,
    query_weight,
    query_bias,
    key_weight,
    value_weight,
    value_bias,
    output_weight,
    output_bias,
    first_gain,
    first_shift,
    inner_weight,
    inner_bias,
    outer_weight,
    outer_bias,
    second_gain,
    second_shift,
    cotangent,
    piece_start,
    memory_pos,
):
    shards = (
        query_weight,
        key_weight,
        value_weight,
        output_weight,
        inner_weight,
        outer_weight,
        query_bias,
        value_bias,
        output_bias,
        first_gain,
        first_shift,
        inner_bias,
        outer_bias,
        second_gain,
        second_shift,
    )
    gathered = (
        lax.all_gather(shards[0], ("dp", "seq"), axis=0, tiled=True),
        lax.all_gather(shards[1], ("dp", "seq"), axis=0, tiled=True),
        lax.all_gather(shards[2], ("dp", "seq"), axis=0, tiled=True),
        lax.all_gather(shards[3], ("dp", "seq"), axis=0, tiled=True),
        lax.all_gather(shards[4], ("dp", "seq"), axis=0, tiled=True),
        lax.all_gather(shards[5], ("dp", "seq"), axis=0, tiled=True),
        lax.all_gather(shards[6], ("dp", "seq"), axis=0, tiled=True),
        lax.all_gather(shards[7], ("dp", "seq"), axis=0, tiled=True),
        lax.all_gather(shards[8], ("dp", "seq"), axis=0, tiled=True),
        lax.all_gather(shards[9], ("dp", "seq"), axis=0, tiled=True),
        lax.all_gather(shards[10], ("dp", "seq"), axis=0, tiled=True),
        lax.all_gather(shards[11], ("dp", "seq"), axis=0, tiled=True),
        lax.all_gather(shards[12], ("dp", "seq"), axis=0, tiled=True),
        lax.all_gather(shards[13], ("dp", "seq"), axis=0, tiled=True),
        lax.all_gather(shards[14], ("dp", "seq"), axis=0, tiled=True),
    )
    w_query, w_key, w_value, w_output, w_inner, w_outer = gathered[:6]
    vectors = [vector.astype(jnp.float32) for vector in gathered[6:]]
    b_query, b_value, b_output, g_first, s_first, b_inner, b_outer, g_second, s_second = vectors
    local_rows = inputs.shape[0]
    model_width = inputs.shape[1]
    score_scale = HD ** (-0.5)
    pair_count = H // 2
    pair_width = 2 * HD
    block_rows = min(512, local_rows, LEN)
    block_count = local_rows // block_rows
    first_row = lax.axis_index("seq") * local_rows
    query_low = (dense(inputs, w_query) + b_query).astype(jnp.bfloat16)
    key_low = dense(inputs, w_key).astype(jnp.bfloat16)
    value_low = (dense(inputs, w_value) + b_value).astype(jnp.bfloat16)
    group_keys, group_values = (
        lax.all_gather(key_low, "seq", axis=0, tiled=True),
        lax.all_gather(value_low, "seq", axis=0, tiled=True),
    )
    group_rows = group_keys.shape[0]

    def context(block_index):
        row_start = first_row + block_index * block_rows
        seq_index = row_start // LEN
        positions = row_start - seq_index * LEN + jnp.arange(block_rows, dtype=jnp.int32)
        starts = piece_start[0]
        memories = memory_pos[0]
        allowed = visible(positions, starts, memories)
        return (seq_index, allowed, group_keys, group_values)

    def pair_part(matrix, pair_index, count):
        return lax.dynamic_slice_in_dim(matrix, pair_index * pair_width, pair_width, 1).reshape(
            count, 2, HD
        )

    def pair_scores(query_pair, key_pair, allowed):
        raw = (
            jnp.einsum("qhd,khd->hqk", query_pair, key_pair, preferred_element_type=jnp.float32)
            * score_scale
        )
        return jnp.where(allowed[None], raw, masked_score)

    def forward_block(block_index):
        _, allowed, seq_keys, seq_values = context(block_index)
        block_query = lax.dynamic_slice_in_dim(query_low, block_index * block_rows, block_rows, 0)

        def forward_pair_step(carry, pair_index):
            out_buffer, total_buffer = carry
            query_pair = pair_part(block_query, pair_index, block_rows)
            key_pair = pair_part(seq_keys, pair_index, LEN)
            value_pair = pair_part(seq_values, pair_index, LEN)
            scores = pair_scores(query_pair, key_pair, allowed)
            peak = jnp.max(scores, -1, keepdims=True)
            expo_terms = jnp.exp(scores - peak)
            row_sum = jnp.sum(expo_terms, -1, keepdims=True)
            chances_low = (expo_terms / row_sum).astype(jnp.bfloat16)
            blended = jnp.einsum(
                "hqk,khd->qhd", chances_low, value_pair, preferred_element_type=jnp.float32
            )
            blended = blended.reshape(block_rows, pair_width).astype(jnp.bfloat16)
            out_buffer = lax.dynamic_update_slice_in_dim(
                out_buffer, blended, pair_index * pair_width, 1
            )
            log_pair = (peak + jnp.log(row_sum))[:, :, 0]
            total_buffer = lax.dynamic_update_slice_in_dim(
                total_buffer, log_pair, pair_index * 2, 0
            )
            return ((out_buffer, total_buffer), None)

        initial = (
            jnp.zeros((block_rows, model_width), jnp.bfloat16),
            jnp.zeros((H, block_rows), jnp.float32),
        )
        (out_buffer, total_buffer), unused = lax.scan(
            forward_pair_step, initial, jnp.arange(pair_count)
        )
        return (out_buffer, total_buffer)

    attended_blocks, log_totals = lax.map(forward_block, jnp.arange(block_count))
    attended = attended_blocks.reshape(local_rows, model_width)
    mixed = inputs.astype(jnp.float32) + dense(attended, w_output) + b_output
    hidden_norm, first_pull = jax.vjp(normalize, mixed, g_first, s_first)
    hidden_low = hidden_norm.astype(jnp.bfloat16)
    inner = dense(hidden_low, w_inner) + b_inner
    activated_full, gelu_pull = jax.vjp(gelu_exact, inner)
    activated = activated_full.astype(jnp.bfloat16)
    second_in = hidden_norm + dense(activated, w_outer) + b_outer
    normed_out, second_pull = jax.vjp(normalize, second_in, g_second, s_second)
    layer_out = normed_out.astype(jnp.bfloat16)
    back_weights = (
        lax.all_gather(query_weight, ("dp", "seq"), axis=0, tiled=True),
        lax.all_gather(key_weight, ("dp", "seq"), axis=0, tiled=True),
        lax.all_gather(value_weight, ("dp", "seq"), axis=0, tiled=True),
        lax.all_gather(output_weight, ("dp", "seq"), axis=0, tiled=True),
        lax.all_gather(inner_weight, ("dp", "seq"), axis=0, tiled=True),
        lax.all_gather(outer_weight, ("dp", "seq"), axis=0, tiled=True),
    )
    v_query, v_key, v_value, v_output, v_inner, v_outer = back_weights
    grad_second_in, grad_second_gain, grad_second_shift = second_pull(cotangent.astype(jnp.float32))
    grad_outer_bias = jnp.sum(grad_second_in, 0)
    second_low = grad_second_in.astype(jnp.bfloat16)
    grad_outer_weight = outer_product(activated, second_low)
    (grad_inner,) = gelu_pull(back_product(second_low, v_outer))
    grad_inner_bias = jnp.sum(grad_inner, 0)
    inner_low = grad_inner.astype(jnp.bfloat16)
    grad_inner_weight = outer_product(hidden_low, inner_low)
    grad_hidden = grad_second_in + back_product(inner_low, v_inner)
    grad_mixed, grad_first_gain, grad_first_shift = first_pull(grad_hidden)
    grad_output_bias = jnp.sum(grad_mixed, 0)
    mixed_low = grad_mixed.astype(jnp.bfloat16)
    grad_output_weight = outer_product(attended, mixed_low)
    grad_attended = back_product(mixed_low, v_output).astype(jnp.bfloat16)

    def backward_block(carry, block_index):
        _, allowed, seq_keys, seq_values = context(block_index)
        block_query = lax.dynamic_slice_in_dim(query_low, block_index * block_rows, block_rows, 0)
        block_grad = lax.dynamic_slice_in_dim(
            grad_attended, block_index * block_rows, block_rows, 0
        )
        block_total = log_totals[block_index]

        def backward_pair_step(inner_carry, pair_index):
            query_grad, term_buffer = (inner_carry[0], inner_carry[1])
            query_pair = pair_part(block_query, pair_index, block_rows)
            key_pair = pair_part(seq_keys, pair_index, LEN)
            value_pair = pair_part(seq_values, pair_index, LEN)
            grad_pair = pair_part(block_grad, pair_index, block_rows)
            scores = pair_scores(query_pair, key_pair, allowed)
            total_pair = lax.dynamic_slice_in_dim(block_total, pair_index * 2, 2, 0)
            chances = jnp.exp(scores - total_pair[:, :, None])
            chance_grad = jnp.einsum(
                "qhd,khd->hqk", grad_pair, value_pair, preferred_element_type=jnp.float32
            )
            row_terms = jnp.sum(chances * chance_grad, -1, keepdims=True)
            score_grad = (chances * (chance_grad - row_terms)).astype(jnp.bfloat16)
            query_part = jnp.einsum(
                "hqk,khd->qhd", score_grad, key_pair, preferred_element_type=jnp.float32
            )
            query_part = query_part.reshape(block_rows, pair_width) * score_scale
            query_grad = lax.dynamic_update_slice_in_dim(
                query_grad, query_part, pair_index * pair_width, 1
            )
            term_buffer = lax.dynamic_update_slice_in_dim(
                term_buffer, row_terms[:, :, 0], pair_index * 2, 0
            )
            seq_key_grad, seq_value_grad = (inner_carry[2], inner_carry[3])
            chances_low = chances.astype(jnp.bfloat16)
            key_part = jnp.einsum(
                "hqk,qhd->khd", score_grad, query_pair, preferred_element_type=jnp.float32
            )
            value_part = jnp.einsum(
                "hqk,qhd->khd", chances_low, grad_pair, preferred_element_type=jnp.float32
            )
            key_part = key_part.reshape(LEN, pair_width) * score_scale
            value_part = value_part.reshape(LEN, pair_width)
            seq_key_grad = lax.dynamic_update_slice_in_dim(
                seq_key_grad, key_part, pair_index * pair_width, 1
            )
            seq_value_grad = lax.dynamic_update_slice_in_dim(
                seq_value_grad, value_part, pair_index * pair_width, 1
            )
            return ((query_grad, term_buffer, seq_key_grad, seq_value_grad), None)

        initial = (
            jnp.zeros((block_rows, model_width), jnp.float32),
            jnp.zeros((H, block_rows), jnp.float32),
        )
        initial = initial + (
            jnp.zeros((LEN, model_width), jnp.float32),
            jnp.zeros((LEN, model_width), jnp.float32),
        )
        finals, _ = lax.scan(backward_pair_step, initial, jnp.arange(pair_count))
        key_grads, value_grads = carry
        key_grads = key_grads + finals[2]
        value_grads = value_grads + finals[3]
        carry = (key_grads, value_grads)
        return (carry, (finals[0], finals[1]))

    group_zero = jnp.zeros((group_rows, model_width), jnp.float32)
    (key_grads, value_grads), (query_blocks, term_blocks) = lax.scan(
        backward_block, (group_zero, group_zero), jnp.arange(block_count)
    )
    key_sum, value_sum = (
        lax.psum_scatter(
            key_grads.astype(jnp.bfloat16), "seq", scatter_dimension=0, tiled=True
        ).astype(jnp.float32),
        lax.psum_scatter(
            value_grads.astype(jnp.bfloat16), "seq", scatter_dimension=0, tiled=True
        ).astype(jnp.float32),
    )
    query_sum = query_blocks.reshape(local_rows, model_width)
    grad_query_bias = jnp.sum(query_sum, 0)
    grad_value_bias = jnp.sum(value_sum, 0)
    query_grad_low = query_sum.astype(jnp.bfloat16)
    key_grad_low = key_sum.astype(jnp.bfloat16)
    value_grad_low = value_sum.astype(jnp.bfloat16)
    grad_query_weight = outer_product(inputs, query_grad_low)
    grad_key_weight = outer_product(inputs, key_grad_low)
    grad_value_weight = outer_product(inputs, value_grad_low)
    grad_inputs = (
        grad_mixed
        + back_product(query_grad_low, v_query)
        + back_product(key_grad_low, v_key)
        + back_product(value_grad_low, v_value)
    )
    grads = (
        grad_query_weight,
        grad_key_weight,
        grad_value_weight,
        grad_output_weight,
        grad_inner_weight,
        grad_outer_weight,
        grad_query_bias,
        grad_value_bias,
        grad_output_bias,
        grad_first_gain,
        grad_first_shift,
        grad_inner_bias,
        grad_outer_bias,
        grad_second_gain,
        grad_second_shift,
    )
    owned = (
        lax.psum_scatter(grads[0], ("dp", "seq"), scatter_dimension=0, tiled=True),
        lax.psum_scatter(grads[1], ("dp", "seq"), scatter_dimension=0, tiled=True),
        lax.psum_scatter(grads[2], ("dp", "seq"), scatter_dimension=0, tiled=True),
        lax.psum_scatter(grads[3], ("dp", "seq"), scatter_dimension=0, tiled=True),
        lax.psum_scatter(grads[4], ("dp", "seq"), scatter_dimension=0, tiled=True),
        lax.psum_scatter(grads[5], ("dp", "seq"), scatter_dimension=0, tiled=True),
        lax.psum_scatter(grads[6], ("dp", "seq"), scatter_dimension=0, tiled=True),
        lax.psum_scatter(grads[7], ("dp", "seq"), scatter_dimension=0, tiled=True),
        lax.psum_scatter(grads[8], ("dp", "seq"), scatter_dimension=0, tiled=True),
        lax.psum_scatter(grads[9], ("dp", "seq"), scatter_dimension=0, tiled=True),
        lax.psum_scatter(grads[10], ("dp", "seq"), scatter_dimension=0, tiled=True),
        lax.psum_scatter(grads[11], ("dp", "seq"), scatter_dimension=0, tiled=True),
        lax.psum_scatter(grads[12], ("dp", "seq"), scatter_dimension=0, tiled=True),
        lax.psum_scatter(grads[13], ("dp", "seq"), scatter_dimension=0, tiled=True),
        lax.psum_scatter(grads[14], ("dp", "seq"), scatter_dimension=0, tiled=True),
    )
    return (
        layer_out,
        grad_inputs,
        owned[0],
        owned[6],
        owned[1],
        owned[2],
        owned[7],
        owned[3],
        owned[8],
        owned[9],
        owned[10],
        owned[4],
        owned[11],
        owned[5],
        owned[12],
        owned[13],
        owned[14],
    )


F32=jnp.float32; BF=jnp.bfloat16
NT=(((1,),(1,)),((),()))
NN=(((1,),(0,)),((),()))


def mm(a,b,dims=NN):
    return lax.dot_general(a,b,dims,preferred_element_type=F32)


GROUP=16


def half_mask(shape, head, dim):
    lanes=lax.broadcasted_iota(jnp.int32,shape,dim)
    return (lanes<64) if head==0 else (lanes>=64)


def only(x, head):
    return jnp.where(half_mask(x.shape,head,1),x,jnp.zeros_like(x))


def take_rows(ref, pos_ref, first):
    width=ref.shape[1]
    out=jnp.zeros((GROUP,width),F32)
    rows=lax.broadcasted_iota(jnp.int32,(GROUP,width),0)
    for m in range(MEM):
        pos=pos_ref[first+m]
        start=pl.multiple_of((pos//GROUP)*GROUP,GROUP)
        part=ref[pl.ds(start,GROUP),:].astype(F32)
        row=jnp.sum(jnp.where(rows==pos-start,part,0.0),0,keepdims=True)
        out=jnp.where(rows==m,row,out)
    return out.astype(BF)


def put_rows(ref, pos_ref, first, values, add):
    width=ref.shape[1]
    rows=lax.broadcasted_iota(jnp.int32,(GROUP,width),0)
    for m in range(MEM):
        pos=pos_ref[first+m]
        start=pl.multiple_of((pos//GROUP)*GROUP,GROUP)
        old=ref[pl.ds(start,GROUP),:].astype(F32)
        row=values[m:m+1,:]
        new=jnp.where(rows==pos-start,old+row if add else row,old)
        ref[pl.ds(start,GROUP),:]=new.astype(ref.dtype)


def transposed(x):
    return jnp.transpose(x.astype(F32)).astype(BF)


def fwd_kernel(pos_ref, posv_ref, limit_ref, write_ref, qkv_ref, o_ref, lse_ref, vt_ref, qt_ref, acc_ref, *, bq, np_, qb0, qb1):
    rows_all=qkv_ref.shape[0]
    nq=rows_all//bq
    W=np_*128
    nh=2*np_
    cols=lambda part,p:slice(part*W+p*128,part*W+p*128+128)
    hr=lambda h:slice(80*h,80*h+80)
    mem=take_rows(qkv_ref,pos_ref,0)
    kr=[only(mem[:,cols(1,h//2)],h%2) for h in range(nh)]
    ones16=jnp.ones((16,GROUP),BF)
    vrt=[]
    for p in range(np_):
        vt=transposed(qkv_ref[:,cols(2,p)])
        mt=transposed(mem[:,cols(2,p)])
        qt_ref[p*128:p*128+128,:]=transposed(qkv_ref[:,cols(0,p)])
        for h in range(2):
            vt_ref[80*(2*p+h):80*(2*p+h)+64,:]=vt[64*h:64*h+64]
            vt_ref[80*(2*p+h)+64:80*(2*p+h)+80,:]=jnp.ones((16,rows_all),BF)
            vrt.append(jnp.concatenate([mt[64*h:64*h+64],ones16],0))
    read_pos=posv_ref[...]
    def q_step(qb, unused):
        q0=pl.multiple_of(qb*bq,bq)
        limit=limit_ref[:,pl.ds(q0,bq)][0:1]
        key_iota=lax.broadcasted_iota(jnp.int32,(bq,bq),0)
        zq=jnp.zeros((64,bq),BF)
        def qh(h):
            own=qt_ref[64*h:64*h+64,pl.ds(q0,bq)]
            return jnp.concatenate([own,zq] if h%2==0 else [zq,own],0)
        def soft(h,s,vt,m):
            m2=jnp.maximum(m,jnp.max(s,0,keepdims=True))
            fix=jnp.exp2(m-m2)
            p=jnp.exp2(s-m2)
            acc_ref[hr(h),:]=acc_ref[hr(h),:]*fix+mm(vt,p.astype(BF))
            return m2
        def block(kb,carry,mask):
            k0=pl.multiple_of(kb*bq,bq)
            ss=[mm(qkv_ref[pl.ds(k0,bq),cols(1,h//2)],qh(h)) for h in range(nh)]
            if mask:
                ss=[jnp.where(key_iota+k0<=limit,s,masked_score) for s in ss]
            return tuple(soft(h,ss[h],vt_ref[hr(h),pl.ds(k0,bq)],carry[h]) for h in range(nh))
        acc_ref[...]=jnp.zeros_like(acc_ref)
        carry=tuple(jnp.full((1,bq),masked_score,F32) for _ in range(nh))
        carry=block(qb,carry,True)
        carry=tuple(soft(h,jnp.where(read_pos>limit,mm(kr[h],qh(h)),masked_score),vrt[h],carry[h]) for h in range(nh))
        carry=lax.fori_loop(0,qb,lambda kb,c:block(kb,c,False),carry)
        far=jnp.max(limit)>=q0+bq
        carry=lax.cond(far,lambda c:block(jnp.minimum(qb+1,nq-1),c,True),lambda c:c,carry)
        wr=write_ref[:,pl.ds(q0,bq)][0:1]
        outs=[]
        for h in range(nh):
            l=acc_ref[80*h+64:80*h+65,:]
            outs.append(acc_ref[80*h:80*h+64,:]/l)
            lse=carry[h]+jnp.log2(l)
            lse_ref[h:h+1,pl.ds(q0,bq)]=jnp.where(wr>0,1e30,lse)
        o_ref[pl.ds(q0,bq),:]=jnp.transpose(jnp.concatenate(outs,0)).astype(BF)
        return unused
    lax.fori_loop(qb0,qb1,q_step,0)
    rows=take_rows(qkv_ref,pos_ref,MEM)
    out=[]
    for p in range(np_):
        total=jnp.zeros((GROUP,128),F32)
        qw=rows[:,cols(0,p)]
        for h in range(2):
            s=mm(only(qw,h),qkv_ref[:,cols(1,p)],NT)
            m=jnp.max(s,1,keepdims=True)
            e=jnp.exp2(s-m)
            l=jnp.sum(e,1,keepdims=True)
            ow=mm(e.astype(BF),qkv_ref[:,cols(2,p)])/l
            total=total+jnp.where(half_mask((GROUP,128),h,1),ow,0.0)
        out.append(total)
    put_rows(o_ref,pos_ref,MEM,jnp.concatenate(out,1),False)


LN2=0.6931471805599453


def bwd_kernel(pos_ref, posv_ref, limit_ref, qkv_ref, do_ref, o_ref, lse_ref,
               dqkv_ref, bias_ref, qt_ref, kt_ref, dot_ref, dk_acc, dv_acc, dq_acc, dr_acc, *, bq, scale, np_):
    rows_all=qkv_ref.shape[0]
    nq=rows_all//bq
    W=np_*128
    nh=2*np_
    cols=lambda part,p:slice(part*W+p*128,part*W+p*128+128)
    pc=lambda p:slice(p*128,p*128+128)
    hr=lambda h:slice(64*h,64*h+64)
    for p in range(np_):
        qt_ref[pc(p),:]=transposed(qkv_ref[:,cols(0,p)])
        kt_ref[pc(p),:]=transposed(qkv_ref[:,cols(1,p)])
        dot_ref[pc(p),:]=transposed(do_ref[:,pc(p)])
    mem=take_rows(qkv_ref,pos_ref,0)
    kr=[mem[:,cols(1,p)] for p in range(np_)]
    vr=[mem[:,cols(2,p)] for p in range(np_)]
    krt=[transposed(kr[p]) for p in range(np_)]
    read_pos=posv_ref[...]
    rows=take_rows(qkv_ref,pos_ref,MEM)
    dow_all=take_rows(do_ref,pos_ref,MEM)
    valid=lax.broadcasted_iota(jnp.int32,(GROUP,1),0)<MEM
    dqw_all=[]
    for pr in range(np_):
        qw=rows[:,cols(0,pr)]
        dow=dow_all[:,pc(pr)]
        qwt=transposed(qw); dowt=transposed(dow)
        dqw=jnp.zeros((GROUP,128),F32)
        for h in range(2):
            s=mm(only(qw,h),qkv_ref[:,cols(1,pr)],NT)
            m=jnp.max(s,1,keepdims=True)
            p=jnp.exp2(s-m)
            p=p*jnp.where(valid,1.0/jnp.sum(p,1,keepdims=True),0.0)
            dp=mm(only(dow,h),qkv_ref[:,cols(2,pr)],NT)
            ds=(p*(dp-jnp.sum(p*dp,1,keepdims=True))).astype(BF)
            dqw=dqw+jnp.where(half_mask((GROUP,128),h,1),mm(ds,qkv_ref[:,cols(1,pr)]),0.0)
            dk_acc[hr(2*pr+h),:]=mm(qwt[64*h:64*h+64],ds)
            dv_acc[hr(2*pr+h),:]=mm(dowt[64*h:64*h+64],p.astype(BF))
        dqw_all.append(dqw)
    dr_acc[...]=jnp.zeros_like(dr_acc)
    def q_step(qb, unused):
        q0=pl.multiple_of(qb*bq,bq)
        limit=limit_ref[:,pl.ds(q0,bq)][0:1]
        zq=jnp.zeros((64,bq),BF)
        def padded(ref,h):
            own=ref[hr(h),pl.ds(q0,bq)]
            return jnp.concatenate([own,zq] if h%2==0 else [zq,own],0)
        prod=jnp.transpose(do_ref[pl.ds(q0,bq),:].astype(F32)*o_ref[pl.ds(q0,bq),:].astype(F32))
        delta=[jnp.sum(prod[hr(h)],0,keepdims=True) for h in range(nh)]
        lse=[lse_ref[h:h+1,pl.ds(q0,bq)] for h in range(nh)]
        key_iota=lax.broadcasted_iota(jnp.int32,(bq,bq),0)
        dq_acc[...]=jnp.zeros_like(dq_acc)
        def grads(h,s,v):
            p=jnp.exp2(s-lse[h])
            dp=mm(v,padded(dot_ref,h))
            return (p*(dp-delta[h])).astype(BF),p.astype(BF)
        def block(kb,mask):
            k0=pl.multiple_of(kb*bq,bq)
            ks=pl.ds(k0,bq)
            held={}
            def front(h):
                s=mm(qkv_ref[ks,cols(1,h//2)],padded(qt_ref,h))
                if mask:
                    s=jnp.where(key_iota+k0<=limit,s,masked_score)
                held[h]=(s,mm(qkv_ref[ks,cols(2,h//2)],padded(dot_ref,h)))
            def middle(h):
                s,dp=held[h]
                p=jnp.exp2(s-lse[h])
                held[h]=((p*(dp-delta[h])).astype(BF),p.astype(BF))
            def back(h):
                ds,p=held[h]
                dq_acc[hr(h),:]+=mm(kt_ref[hr(h),ks],ds)
                dk_acc[hr(h),ks]+=mm(qt_ref[hr(h),pl.ds(q0,bq)],ds,NT)
                dv_acc[hr(h),ks]+=mm(dot_ref[hr(h),pl.ds(q0,bq)],p,NT)
            for h in range(nh+2):
                if h<nh:
                    front(h)
                if 0<=h-1<nh:
                    middle(h-1)
                if h>=2:
                    back(h-2)
        block(qb,True)
        for h in range(nh):
            s=jnp.where(read_pos>limit,mm(kr[h//2],padded(qt_ref,h)),masked_score)
            ds,p=grads(h,s,vr[h//2])
            dr_acc[0,hr(h),:]+=mm(qt_ref[hr(h),pl.ds(q0,bq)],ds,NT)
            dr_acc[1,hr(h),:]+=mm(dot_ref[hr(h),pl.ds(q0,bq)],p,NT)
            dq_acc[hr(h),:]+=mm(krt[h//2][64*(h%2):64*(h%2)+64,:],ds)
        def step(kb,c):
            block(kb,False)
            return c
        lax.fori_loop(0,qb,step,0)
        @pl.when(jnp.max(limit)>=q0+bq)
        def _():
            block(jnp.minimum(qb+1,nq-1),True)
        dqkv_ref[pl.ds(q0,bq),0:W]=(jnp.transpose(dq_acc[...])*scale).astype(BF)
        return unused
    lax.fori_loop(0,nq,q_step,0)
    put_rows(dqkv_ref.at[:,0:W],pos_ref,MEM,jnp.concatenate(dqw_all,1)*scale,False)
    for p in range(np_):
        dqkv_ref[:,cols(1,p)]=(jnp.transpose(dk_acc[pc(p),:])*LN2).astype(BF)
        dqkv_ref[:,cols(2,p)]=jnp.transpose(dv_acc[pc(p),:]).astype(BF)
    put_rows(dqkv_ref.at[:,W:2*W],pos_ref,0,jnp.transpose(dr_acc[0])*LN2,True)
    put_rows(dqkv_ref.at[:,2*W:3*W],pos_ref,0,jnp.transpose(dr_acc[1]),True)
    rows8=lax.broadcasted_iota(jnp.int32,(8,W),0)
    bq_sum=jnp.sum(dqkv_ref[:,0:W].astype(F32),0,keepdims=True)
    bv_sum=jnp.sum(dqkv_ref[:,2*W:3*W].astype(F32),0,keepdims=True)
    bias_ref[...]=jnp.where(rows8==0,bq_sum,jnp.where(rows8==1,bv_sum,0.0))


ONCE=pl.Buffered(1)


def attn_fwd(qkv, pos, posv, limit, write, np_, bq=256, qb0=0, qb1=None):
    L=qkv.shape[0]; W=np_*128
    row8=pl.BlockSpec((8,L),lambda i:(0,0),pipeline_mode=ONCE)
    full=lambda w:pl.BlockSpec((L,w),lambda i:(0,0),pipeline_mode=ONCE)
    return pl.pallas_call(partial(fwd_kernel,bq=bq,np_=np_,qb0=qb0,qb1=L//bq if qb1 is None else qb1),
        grid=(1,),
        in_specs=[pl.BlockSpec(memory_space=pltpu.SMEM),pl.BlockSpec((GROUP,1),lambda i:(0,0)),row8,row8,full(3*W)],
        out_specs=[full(W),row8],
        out_shape=[jax.ShapeDtypeStruct((L,W),BF),jax.ShapeDtypeStruct((8,L),F32)],
        scratch_shapes=[pltpu.VMEM((np_*160,L),BF),pltpu.VMEM((W,L),BF),pltpu.VMEM((np_*160,bq),F32)],
        name="attn_fwd",
    )(pos,posv,limit,write,qkv)


def attn_bwd(qkv, pos, posv, limit, do, o, lse, np_, scale, bq=256):
    L=qkv.shape[0]; W=np_*128
    row8=pl.BlockSpec((8,L),lambda i:(0,0),pipeline_mode=ONCE)
    full=lambda w:pl.BlockSpec((L,w),lambda i:(0,0),pipeline_mode=ONCE)
    return pl.pallas_call(partial(bwd_kernel,bq=bq,scale=scale,np_=np_),
        grid=(1,),
        in_specs=[pl.BlockSpec(memory_space=pltpu.SMEM),pl.BlockSpec((GROUP,1),lambda i:(0,0)),row8,full(3*W),full(W),full(W),row8],
        out_specs=[full(3*W),pl.BlockSpec((8,W),lambda i:(0,0))],
        out_shape=[jax.ShapeDtypeStruct((L,3*W),BF),jax.ShapeDtypeStruct((8,W),F32)],
        scratch_shapes=[pltpu.VMEM((W,L),BF)]*3+[pltpu.VMEM((W,L),F32)]*2+[pltpu.VMEM((W,bq),F32),pltpu.VMEM((2,W,GROUP),F32)],
        name="attn_bwd",
    )(pos,posv,limit,qkv,do,o,lse)


LANES = 128
LOG2E = 1.4426950408889634
ALL = ("dp", "seq")
RSQRT2 = 0.7071067811865476
RSQRT2PI = 0.3989422804014327


def bit_swap(x, axis, size, bit):
    return lax.ppermute(x, axis, [(i, i ^ bit) for i in range(size)])


def side(flag, own, peer, axis):
    low = jnp.where(flag, peer, own)
    high = jnp.where(flag, own, peer)
    return jnp.concatenate([low, high], axis)


def bits_of(size):
    out = []
    bit = 1
    while bit < size:
        out.append(bit)
        bit *= 2
    return out


def double_dp(out, size, bit):
    other = bit_swap(out, "dp", size, bit)
    up = (lax.axis_index("dp") & bit) != 0
    return jnp.stack([jnp.where(up, other, out), jnp.where(up, out, other)])


def halve_dp(rest, size, bit):
    up = (lax.axis_index("dp") & bit) != 0
    rest = rest.reshape((rest.shape[0] // 2, 2) + rest.shape[1:])
    give = jnp.where(up, rest[:, 0], rest[:, 1]).astype(BF)
    keep = jnp.where(up, rest[:, 1], rest[:, 0])
    got = bit_swap(give, "dp", size, bit)
    return keep + got.astype(F32)


def spread_lanes(rows, part):
    rows = jnp.pad(rows, ((0, 0), (0, part * LANES - rows.shape[1])))
    return rows.reshape(rows.shape[0], part, LANES)


def norm_parts(values):
    centre = jnp.mean(values, -1, keepdims=True)
    centred = values - centre
    spread = jnp.mean(centred * centred, -1, keepdims=True)
    factor = lax.rsqrt(spread + norm_epsilon)
    return centred * factor, factor


def norm_back(gradient, unit, factor):
    return factor * (
        gradient
        - jnp.mean(gradient, -1, keepdims=True)
        - unit * jnp.mean(gradient * unit, -1, keepdims=True)
    )


def fast_body(
    inputs,
    query_weight,
    query_bias,
    key_weight,
    value_weight,
    value_bias,
    output_weight,
    output_bias,
    first_gain,
    first_shift,
    inner_weight,
    inner_bias,
    outer_weight,
    outer_bias,
    second_gain,
    second_shift,
    cotangent,
    piece_start,
    memory_pos,
    *,
    n_dp,
):
    rows, width = inputs.shape
    inner_width = inner_weight.shape[1]
    devices = 2 * n_dp
    part = width // devices
    inner_part = inner_width // devices
    ratio = inner_width // width
    half = width // 2
    seq = lax.axis_index("seq")
    upper = seq == 1

    def swap(x):
        return bit_swap(x, "seq", 2, 1)

    wide = inner_weight.reshape(part, ratio, width).transpose(1, 0, 2).reshape(ratio * part, width)
    packed = jnp.concatenate([output_weight, wide, outer_weight], 0)
    columns_of = [
        query_bias,
        value_bias,
        output_bias,
        first_gain,
        first_shift,
        outer_bias,
        second_gain,
        second_shift,
    ] + [inner_bias[k * part : (k + 1) * part] for k in range(ratio)]
    line = jnp.pad(jnp.stack(columns_of, 1), ((0, 0), (0, LANES - len(columns_of))))

    def columns(upper_half):
        pick = lambda w: jnp.where(upper_half, w[:, half:], w[:, :half])
        return jnp.concatenate([pick(query_weight), pick(key_weight), pick(value_weight), line], 1)

    own_columns = columns(upper)
    peer_columns = swap(columns(jnp.logical_not(upper)))
    peer_inputs = swap(inputs)
    early = side(upper, own_columns[None], peer_columns[None], 0)
    bits = bits_of(n_dp)
    for bit in bits[::-1]:
        early = double_dp(early, n_dp, bit)
        if bit == bits[-1]:
            early, packed = lax.optimization_barrier((early, packed))
            late = lax.all_gather(packed, ALL, axis=0, tiled=False)
    count = len(bits)
    early = early.transpose(tuple(range(count))[::-1] + tuple(range(count, early.ndim)))
    early = early.reshape(width, 3 * half + LANES)
    w_three = early[:, : 3 * half]
    table = early[:, 3 * half :].T.astype(F32)
    b_query, b_value, b_output, g_first, s_first, b_outer, g_second, s_second = (
        table[k] for k in range(8)
    )
    b_inner = table[8 : 8 + ratio].reshape(ratio, devices, part).transpose(1, 0, 2)
    b_inner = b_inner.reshape(inner_width)
    own_half = lambda v: lax.dynamic_slice_in_dim(v, seq * half, half, 0)
    features = side(upper, inputs, peer_inputs, 0)
    scale = HD ** (-0.5)
    shift = jnp.concatenate([own_half(b_query), jnp.zeros((half,), F32), own_half(b_value)])
    grow = jnp.concatenate([jnp.full((half,), scale * LOG2E, F32), jnp.ones((2 * half,), F32)])
    qkv = ((dense(features, w_three) + shift) * grow).astype(BF)
    positions = jnp.arange(2 * rows, dtype=jnp.int32)
    limit = positions
    for piece in range(NPIC):
        start = piece_start[0, piece]
        inside = (positions >= start) & (positions < start + PIC)
        limit = jnp.where(inside, start + PIC - 1, limit)
    memories = memory_pos[0]
    writes = jnp.any(positions[None, :] == memories[MEM:, None], 0).astype(jnp.int32)
    limit = jnp.broadcast_to(limit, (8, 2 * rows))
    writes = jnp.broadcast_to(writes, (8, 2 * rows))
    reads = jnp.pad(memories[:MEM], (0, GROUP - MEM), constant_values=-1)[:, None]
    pairs = half // (2 * HD)
    out_heads, totals = attn_fwd(qkv, memories, reads, limit, writes, pairs)
    own_of = lambda v: lax.dynamic_slice_in_dim(v, seq * rows, rows, 0)
    peer_of = lambda v: lax.dynamic_slice_in_dim(v, (1 - seq) * rows, rows, 0)
    other_rows = peer_of(out_heads)
    own_rows = own_of(out_heads)
    attended = side(upper, own_rows, swap(other_rows), 1)
    w_output = late[:, :part].reshape(width, width)
    w_inner = jnp.concatenate(
        [
            late[:, part + k * part : 2 * part + k * part].reshape(width, width)
            for k in range(ratio)
        ],
        1,
    )
    w_outer = late[:, part + ratio * part :].reshape(inner_width, width)
    mixed = inputs.astype(F32) + dense(attended, w_output) + b_output
    first_unit, first_factor = norm_parts(mixed)
    hidden_norm = first_unit * g_first + s_first
    hidden_low = hidden_norm.astype(BF)
    inner = dense(hidden_low, w_inner) + b_inner
    chance = 0.5 * (1.0 + lax.erf(inner * RSQRT2))
    activated = (inner * chance).astype(BF)
    slope = (chance + inner * (RSQRT2PI * jnp.exp(-0.5 * inner * inner))).astype(BF)
    activated, slope = lax.optimization_barrier((activated, slope))
    second_in = hidden_norm + dense(activated, w_outer) + b_outer
    second_unit, second_factor = norm_parts(second_in)
    layer_out = (second_unit * g_second + s_second).astype(BF)
    cot = cotangent.astype(F32)
    grad_second_gain = jnp.sum(cot * second_unit, 0)
    grad_second_shift = jnp.sum(cot, 0)
    grad_second_in = norm_back(cot * g_second, second_unit, second_factor)
    grad_outer_bias = jnp.sum(grad_second_in, 0)
    second_low = grad_second_in.astype(BF)
    grad_inner = back_product(second_low, w_outer) * slope.astype(F32)
    grad_inner_bias = jnp.sum(grad_inner, 0)
    inner_low = grad_inner.astype(BF)
    column = lambda k: inner_low[:, k * width : (k + 1) * width]
    inner_blocks = [
        outer_product(hidden_low, column(k)).astype(BF).reshape(devices, part, width)
        for k in range(ratio)
    ]
    grad_outer_weight = outer_product(activated, second_low).astype(BF)
    bundle = jnp.concatenate(
        inner_blocks + [grad_outer_weight.reshape(devices, inner_part, width)], 1
    )
    bundle_rows = bundle.shape[1]
    bundle, inner_low = lax.optimization_barrier((bundle, inner_low))
    reduced = lax.psum_scatter(
        bundle.reshape(devices * bundle_rows, width), ALL, scatter_dimension=0, tiled=True
    )
    grad_hidden = grad_second_in + back_product(inner_low, w_inner)
    grad_first_gain = jnp.sum(grad_hidden * first_unit, 0)
    grad_first_shift = jnp.sum(grad_hidden, 0)
    grad_mixed = norm_back(grad_hidden * g_first, first_unit, first_factor)
    grad_output_bias = jnp.sum(grad_mixed, 0)
    mixed_low = grad_mixed.astype(BF)
    grad_attended = back_product(mixed_low, w_output).astype(BF)
    grad_other = lax.dynamic_slice_in_dim(grad_attended, (1 - seq) * half, half, 1)
    grad_own = lax.dynamic_slice_in_dim(grad_attended, seq * half, half, 1)
    grad_heads = side(upper, grad_own, swap(grad_other), 0)
    grad_output_weight = outer_product(attended, mixed_low).reshape(devices, part, width)
    thin = [
        grad_output_bias,
        grad_first_gain,
        grad_first_shift,
        grad_outer_bias,
        grad_second_gain,
        grad_second_shift,
    ]
    thin = jnp.concatenate(
        [v.reshape(devices, part) for v in thin] + [grad_inner_bias.reshape(devices, inner_part)], 1
    )
    mid = jnp.concatenate([grad_output_weight, spread_lanes(thin, part)], 2)
    mid = mid.reshape(n_dp, 2, part, width + LANES)
    mid = halve_dp(mid, n_dp, bits[0])
    mid = halve_dp(mid, n_dp, bits[1])
    grads, bias_sums = attn_bwd(
        qkv, memories, reads, limit, grad_heads, out_heads, totals, pairs, scale
    )
    other_grads = peer_of(grads)
    own_grads = own_of(grads)
    for_peer = back_product(other_grads, w_three).astype(BF)
    for_peer, grads = lax.optimization_barrier((for_peer, grads))
    sent = swap(for_peer)
    three_grad = outer_product(features, grads).reshape(devices, part, 3 * half)
    full = lambda v: side(upper, v, jnp.zeros_like(v), 0).reshape(devices, part)
    tails = jnp.concatenate([full(bias_sums[0]), full(bias_sums[1])], 1)
    blocks = jnp.concatenate([three_grad, spread_lanes(tails, part)], 2)
    wide_half = 3 * half + LANES
    blocks = blocks.reshape(n_dp, 2, part, wide_half)
    blocks = halve_dp(blocks, n_dp, bits[0])
    own_part = lax.optimization_barrier(grad_mixed + back_product(own_grads, w_three))
    blocks = halve_dp(blocks, n_dp, bits[1])
    blocks = jnp.concatenate([blocks, mid], 3)
    for bit in bits[2:]:
        blocks = halve_dp(blocks, n_dp, bit)
    mine = blocks[0]
    give = jnp.where(upper, mine[0], mine[1]).astype(BF)
    keep = jnp.where(upper, mine[1], mine[0])
    own_inner = jnp.concatenate([reduced[k * part : (k + 1) * part] for k in range(ratio)], 1)
    own_inner = own_inner.astype(F32)
    own_outer = reduced[ratio * part :].astype(F32)
    give, own_inner, own_outer = lax.optimization_barrier((give, own_inner, own_outer))
    got = swap(give).astype(F32)
    grad_inputs = own_part + sent.astype(F32)
    span = lambda x, k, n: x[:, k : k + n]
    both = lambda k, n: span(keep, k, n) + span(got, k, n)
    matrix = lambda k: side(upper, span(keep, k * half, half), span(got, k * half, half), 1)
    grad_output = both(wide_half, width)
    thin_sum = both(wide_half + width, LANES).reshape(-1)
    tail_sum = both(3 * half, LANES).reshape(-1)
    thin_part = lambda k: thin_sum[k * part : (k + 1) * part]
    return (
        layer_out,
        grad_inputs,
        matrix(0),
        tail_sum[:part],
        matrix(1),
        matrix(2),
        tail_sum[part : 2 * part],
        grad_output,
        thin_part(0),
        thin_part(1),
        thin_part(2),
        own_inner,
        thin_sum[6 * part : 6 * part + inner_part],
        own_outer,
        thin_part(3),
        thin_part(4),
        thin_part(5),
    )


def solution(mesh):
    in_specs = (
        P(("dp", "seq"), None),
        P(("dp", "seq"), None),
        P(("dp", "seq")),
        P(("dp", "seq"), None),
        P(("dp", "seq"), None),
        P(("dp", "seq")),
        P(("dp", "seq"), None),
        P(("dp", "seq")),
        P(("dp", "seq")),
        P(("dp", "seq")),
        P(("dp", "seq"), None),
        P(("dp", "seq")),
        P(("dp", "seq"), None),
        P(("dp", "seq")),
        P(("dp", "seq")),
        P(("dp", "seq")),
        P(("dp", "seq"), None),
        P("dp", None),
        P("dp", None),
    )
    out_specs = (
        P(("dp", "seq"), None),
        P(("dp", "seq"), None),
        P(("dp", "seq"), None),
        P(("dp", "seq")),
        P(("dp", "seq"), None),
        P(("dp", "seq"), None),
        P(("dp", "seq")),
        P(("dp", "seq"), None),
        P(("dp", "seq")),
        P(("dp", "seq")),
        P(("dp", "seq")),
        P(("dp", "seq"), None),
        P(("dp", "seq")),
        P(("dp", "seq"), None),
        P(("dp", "seq")),
        P(("dp", "seq")),
        P(("dp", "seq")),
    )
    n_dp = mesh.shape["dp"]
    if mesh.shape["seq"] != 2 or n_dp & (n_dp - 1) != 0 or n_dp < 4:
        return jax.shard_map(
            body, mesh=mesh, in_specs=in_specs, out_specs=out_specs, check_vma=False
        )

    def chosen(*arrays):
        return fast_body(*arrays, n_dp=n_dp)

    return jax.shard_map(
        chosen, mesh=mesh, in_specs=in_specs, out_specs=out_specs, check_vma=False
    )
```

```python
from functools import partial

import jax
import jax.numpy as jnp
from jax import lax
from jax.experimental import pallas as pl
from jax.experimental.pallas import tpu as pltpu
from jax.sharding import PartitionSpec as P


H = 12
HD = 64
LEN = 2048
PIC = 256
NPIC = 2
MEM = 10


norm_epsilon = 1e-05
masked_score = -1e30


def normalize(values, gain, shift):
    centre = jnp.mean(values, -1, keepdims=True)
    centred = values - centre
    spread = jnp.mean(centred * centred, -1, keepdims=True)
    return centred * lax.rsqrt(spread + norm_epsilon) * gain + shift


def gelu_exact(values):
    return jax.nn.gelu(values, approximate=False)


def visible_cols(positions, columns, starts, memories):
    labels = jnp.arange(NPIC, dtype=jnp.int32)[:, None] + 1
    in_cols = (columns[None, :] >= starts[:, None]) & (columns[None, :] < starts[:, None] + PIC)
    in_rows = (positions[None, :] >= starts[:, None]) & (positions[None, :] < starts[:, None] + PIC)
    piece_cols = jnp.sum(jnp.where(in_cols, labels, 0), 0)
    piece_rows = jnp.sum(jnp.where(in_rows, labels, 0), 0)
    same_piece = (piece_rows[:, None] == piece_cols[None, :]) & (piece_rows[:, None] > 0)
    read_cols = jnp.any(columns[None, :] == memories[:MEM, None], 0)
    write_rows = jnp.any(positions[None, :] == memories[MEM:, None], 0)
    causal = columns[None, :] <= positions[:, None]
    return causal | same_piece | read_cols[None, :] | write_rows[:, None]


def visible(positions, starts, memories):
    return visible_cols(positions, jnp.arange(LEN, dtype=jnp.int32), starts, memories)


def dense(left, right):
    return jnp.dot(left, right, preferred_element_type=jnp.float32)


def outer_product(left, right):
    return jnp.einsum("ta,tb->ab", left, right, preferred_element_type=jnp.float32)


def back_product(gradient, weight):
    return jnp.einsum("tb,ab->ta", gradient, weight, preferred_element_type=jnp.float32)


def body(
    inputs,
    query_weight,
    query_bias,
    key_weight,
    value_weight,
    value_bias,
    output_weight,
    output_bias,
    first_gain,
    first_shift,
    inner_weight,
    inner_bias,
    outer_weight,
    outer_bias,
    second_gain,
    second_shift,
    cotangent,
    piece_start,
    memory_pos,
):
    shards = (
        query_weight,
        key_weight,
        value_weight,
        output_weight,
        inner_weight,
        outer_weight,
        query_bias,
        value_bias,
        output_bias,
        first_gain,
        first_shift,
        inner_bias,
        outer_bias,
        second_gain,
        second_shift,
    )
    gathered = (
        lax.all_gather(shards[0], ("dp", "seq"), axis=0, tiled=True),
        lax.all_gather(shards[1], ("dp", "seq"), axis=0, tiled=True),
        lax.all_gather(shards[2], ("dp", "seq"), axis=0, tiled=True),
        lax.all_gather(shards[3], ("dp", "seq"), axis=0, tiled=True),
        lax.all_gather(shards[4], ("dp", "seq"), axis=0, tiled=True),
        lax.all_gather(shards[5], ("dp", "seq"), axis=0, tiled=True),
        lax.all_gather(shards[6], ("dp", "seq"), axis=0, tiled=True),
        lax.all_gather(shards[7], ("dp", "seq"), axis=0, tiled=True),
        lax.all_gather(shards[8], ("dp", "seq"), axis=0, tiled=True),
        lax.all_gather(shards[9], ("dp", "seq"), axis=0, tiled=True),
        lax.all_gather(shards[10], ("dp", "seq"), axis=0, tiled=True),
        lax.all_gather(shards[11], ("dp", "seq"), axis=0, tiled=True),
        lax.all_gather(shards[12], ("dp", "seq"), axis=0, tiled=True),
        lax.all_gather(shards[13], ("dp", "seq"), axis=0, tiled=True),
        lax.all_gather(shards[14], ("dp", "seq"), axis=0, tiled=True),
    )
    w_query, w_key, w_value, w_output, w_inner, w_outer = gathered[:6]
    vectors = [vector.astype(jnp.float32) for vector in gathered[6:]]
    b_query, b_value, b_output, g_first, s_first, b_inner, b_outer, g_second, s_second = vectors
    local_rows = inputs.shape[0]
    model_width = inputs.shape[1]
    score_scale = HD ** (-0.5)
    pair_count = H // 2
    pair_width = 2 * HD
    block_rows = min(512, local_rows, LEN)
    block_count = local_rows // block_rows
    first_row = lax.axis_index("seq") * local_rows
    query_low = (dense(inputs, w_query) + b_query).astype(jnp.bfloat16)
    key_low = dense(inputs, w_key).astype(jnp.bfloat16)
    value_low = (dense(inputs, w_value) + b_value).astype(jnp.bfloat16)
    group_keys, group_values = (
        lax.all_gather(key_low, "seq", axis=0, tiled=True),
        lax.all_gather(value_low, "seq", axis=0, tiled=True),
    )
    group_rows = group_keys.shape[0]

    def context(block_index):
        row_start = first_row + block_index * block_rows
        seq_index = row_start // LEN
        positions = row_start - seq_index * LEN + jnp.arange(block_rows, dtype=jnp.int32)
        starts = piece_start[0]
        memories = memory_pos[0]
        allowed = visible(positions, starts, memories)
        return (seq_index, allowed, group_keys, group_values)

    def pair_part(matrix, pair_index, count):
        return lax.dynamic_slice_in_dim(matrix, pair_index * pair_width, pair_width, 1).reshape(
            count, 2, HD
        )

    def pair_scores(query_pair, key_pair, allowed):
        raw = (
            jnp.einsum("qhd,khd->hqk", query_pair, key_pair, preferred_element_type=jnp.float32)
            * score_scale
        )
        return jnp.where(allowed[None], raw, masked_score)

    def forward_block(block_index):
        _, allowed, seq_keys, seq_values = context(block_index)
        block_query = lax.dynamic_slice_in_dim(query_low, block_index * block_rows, block_rows, 0)

        def forward_pair_step(carry, pair_index):
            out_buffer, total_buffer = carry
            query_pair = pair_part(block_query, pair_index, block_rows)
            key_pair = pair_part(seq_keys, pair_index, LEN)
            value_pair = pair_part(seq_values, pair_index, LEN)
            scores = pair_scores(query_pair, key_pair, allowed)
            peak = jnp.max(scores, -1, keepdims=True)
            expo_terms = jnp.exp(scores - peak)
            row_sum = jnp.sum(expo_terms, -1, keepdims=True)
            chances_low = (expo_terms / row_sum).astype(jnp.bfloat16)
            blended = jnp.einsum(
                "hqk,khd->qhd", chances_low, value_pair, preferred_element_type=jnp.float32
            )
            blended = blended.reshape(block_rows, pair_width).astype(jnp.bfloat16)
            out_buffer = lax.dynamic_update_slice_in_dim(
                out_buffer, blended, pair_index * pair_width, 1
            )
            log_pair = (peak + jnp.log(row_sum))[:, :, 0]
            total_buffer = lax.dynamic_update_slice_in_dim(
                total_buffer, log_pair, pair_index * 2, 0
            )
            return ((out_buffer, total_buffer), None)

        initial = (
            jnp.zeros((block_rows, model_width), jnp.bfloat16),
            jnp.zeros((H, block_rows), jnp.float32),
        )
        (out_buffer, total_buffer), unused = lax.scan(
            forward_pair_step, initial, jnp.arange(pair_count)
        )
        return (out_buffer, total_buffer)

    attended_blocks, log_totals = lax.map(forward_block, jnp.arange(block_count))
    attended = attended_blocks.reshape(local_rows, model_width)
    mixed = inputs.astype(jnp.float32) + dense(attended, w_output) + b_output
    hidden_norm, first_pull = jax.vjp(normalize, mixed, g_first, s_first)
    hidden_low = hidden_norm.astype(jnp.bfloat16)
    inner = dense(hidden_low, w_inner) + b_inner
    activated_full, gelu_pull = jax.vjp(gelu_exact, inner)
    activated = activated_full.astype(jnp.bfloat16)
    second_in = hidden_norm + dense(activated, w_outer) + b_outer
    normed_out, second_pull = jax.vjp(normalize, second_in, g_second, s_second)
    layer_out = normed_out.astype(jnp.bfloat16)
    back_weights = (
        lax.all_gather(query_weight, ("dp", "seq"), axis=0, tiled=True),
        lax.all_gather(key_weight, ("dp", "seq"), axis=0, tiled=True),
        lax.all_gather(value_weight, ("dp", "seq"), axis=0, tiled=True),
        lax.all_gather(output_weight, ("dp", "seq"), axis=0, tiled=True),
        lax.all_gather(inner_weight, ("dp", "seq"), axis=0, tiled=True),
        lax.all_gather(outer_weight, ("dp", "seq"), axis=0, tiled=True),
    )
    v_query, v_key, v_value, v_output, v_inner, v_outer = back_weights
    grad_second_in, grad_second_gain, grad_second_shift = second_pull(cotangent.astype(jnp.float32))
    grad_outer_bias = jnp.sum(grad_second_in, 0)
    second_low = grad_second_in.astype(jnp.bfloat16)
    grad_outer_weight = outer_product(activated, second_low)
    (grad_inner,) = gelu_pull(back_product(second_low, v_outer))
    grad_inner_bias = jnp.sum(grad_inner, 0)
    inner_low = grad_inner.astype(jnp.bfloat16)
    grad_inner_weight = outer_product(hidden_low, inner_low)
    grad_hidden = grad_second_in + back_product(inner_low, v_inner)
    grad_mixed, grad_first_gain, grad_first_shift = first_pull(grad_hidden)
    grad_output_bias = jnp.sum(grad_mixed, 0)
    mixed_low = grad_mixed.astype(jnp.bfloat16)
    grad_output_weight = outer_product(attended, mixed_low)
    grad_attended = back_product(mixed_low, v_output).astype(jnp.bfloat16)

    def backward_block(carry, block_index):
        _, allowed, seq_keys, seq_values = context(block_index)
        block_query = lax.dynamic_slice_in_dim(query_low, block_index * block_rows, block_rows, 0)
        block_grad = lax.dynamic_slice_in_dim(
            grad_attended, block_index * block_rows, block_rows, 0
        )
        block_total = log_totals[block_index]

        def backward_pair_step(inner_carry, pair_index):
            query_grad, term_buffer = (inner_carry[0], inner_carry[1])
            query_pair = pair_part(block_query, pair_index, block_rows)
            key_pair = pair_part(seq_keys, pair_index, LEN)
            value_pair = pair_part(seq_values, pair_index, LEN)
            grad_pair = pair_part(block_grad, pair_index, block_rows)
            scores = pair_scores(query_pair, key_pair, allowed)
            total_pair = lax.dynamic_slice_in_dim(block_total, pair_index * 2, 2, 0)
            chances = jnp.exp(scores - total_pair[:, :, None])
            chance_grad = jnp.einsum(
                "qhd,khd->hqk", grad_pair, value_pair, preferred_element_type=jnp.float32
            )
            row_terms = jnp.sum(chances * chance_grad, -1, keepdims=True)
            score_grad = (chances * (chance_grad - row_terms)).astype(jnp.bfloat16)
            query_part = jnp.einsum(
                "hqk,khd->qhd", score_grad, key_pair, preferred_element_type=jnp.float32
            )
            query_part = query_part.reshape(block_rows, pair_width) * score_scale
            query_grad = lax.dynamic_update_slice_in_dim(
                query_grad, query_part, pair_index * pair_width, 1
            )
            term_buffer = lax.dynamic_update_slice_in_dim(
                term_buffer, row_terms[:, :, 0], pair_index * 2, 0
            )
            seq_key_grad, seq_value_grad = (inner_carry[2], inner_carry[3])
            chances_low = chances.astype(jnp.bfloat16)
            key_part = jnp.einsum(
                "hqk,qhd->khd", score_grad, query_pair, preferred_element_type=jnp.float32
            )
            value_part = jnp.einsum(
                "hqk,qhd->khd", chances_low, grad_pair, preferred_element_type=jnp.float32
            )
            key_part = key_part.reshape(LEN, pair_width) * score_scale
            value_part = value_part.reshape(LEN, pair_width)
            seq_key_grad = lax.dynamic_update_slice_in_dim(
                seq_key_grad, key_part, pair_index * pair_width, 1
            )
            seq_value_grad = lax.dynamic_update_slice_in_dim(
                seq_value_grad, value_part, pair_index * pair_width, 1
            )
            return ((query_grad, term_buffer, seq_key_grad, seq_value_grad), None)

        initial = (
            jnp.zeros((block_rows, model_width), jnp.float32),
            jnp.zeros((H, block_rows), jnp.float32),
        )
        initial = initial + (
            jnp.zeros((LEN, model_width), jnp.float32),
            jnp.zeros((LEN, model_width), jnp.float32),
        )
        finals, _ = lax.scan(backward_pair_step, initial, jnp.arange(pair_count))
        key_grads, value_grads = carry
        key_grads = key_grads + finals[2]
        value_grads = value_grads + finals[3]
        carry = (key_grads, value_grads)
        return (carry, (finals[0], finals[1]))

    group_zero = jnp.zeros((group_rows, model_width), jnp.float32)
    (key_grads, value_grads), (query_blocks, term_blocks) = lax.scan(
        backward_block, (group_zero, group_zero), jnp.arange(block_count)
    )
    key_sum, value_sum = (
        lax.psum_scatter(
            key_grads.astype(jnp.bfloat16), "seq", scatter_dimension=0, tiled=True
        ).astype(jnp.float32),
        lax.psum_scatter(
            value_grads.astype(jnp.bfloat16), "seq", scatter_dimension=0, tiled=True
        ).astype(jnp.float32),
    )
    query_sum = query_blocks.reshape(local_rows, model_width)
    grad_query_bias = jnp.sum(query_sum, 0)
    grad_value_bias = jnp.sum(value_sum, 0)
    query_grad_low = query_sum.astype(jnp.bfloat16)
    key_grad_low = key_sum.astype(jnp.bfloat16)
    value_grad_low = value_sum.astype(jnp.bfloat16)
    grad_query_weight = outer_product(inputs, query_grad_low)
    grad_key_weight = outer_product(inputs, key_grad_low)
    grad_value_weight = outer_product(inputs, value_grad_low)
    grad_inputs = (
        grad_mixed
        + back_product(query_grad_low, v_query)
        + back_product(key_grad_low, v_key)
        + back_product(value_grad_low, v_value)
    )
    grads = (
        grad_query_weight,
        grad_key_weight,
        grad_value_weight,
        grad_output_weight,
        grad_inner_weight,
        grad_outer_weight,
        grad_query_bias,
        grad_value_bias,
        grad_output_bias,
        grad_first_gain,
        grad_first_shift,
        grad_inner_bias,
        grad_outer_bias,
        grad_second_gain,
        grad_second_shift,
    )
    owned = (
        lax.psum_scatter(grads[0], ("dp", "seq"), scatter_dimension=0, tiled=True),
        lax.psum_scatter(grads[1], ("dp", "seq"), scatter_dimension=0, tiled=True),
        lax.psum_scatter(grads[2], ("dp", "seq"), scatter_dimension=0, tiled=True),
        lax.psum_scatter(grads[3], ("dp", "seq"), scatter_dimension=0, tiled=True),
        lax.psum_scatter(grads[4], ("dp", "seq"), scatter_dimension=0, tiled=True),
        lax.psum_scatter(grads[5], ("dp", "seq"), scatter_dimension=0, tiled=True),
        lax.psum_scatter(grads[6], ("dp", "seq"), scatter_dimension=0, tiled=True),
        lax.psum_scatter(grads[7], ("dp", "seq"), scatter_dimension=0, tiled=True),
        lax.psum_scatter(grads[8], ("dp", "seq"), scatter_dimension=0, tiled=True),
        lax.psum_scatter(grads[9], ("dp", "seq"), scatter_dimension=0, tiled=True),
        lax.psum_scatter(grads[10], ("dp", "seq"), scatter_dimension=0, tiled=True),
        lax.psum_scatter(grads[11], ("dp", "seq"), scatter_dimension=0, tiled=True),
        lax.psum_scatter(grads[12], ("dp", "seq"), scatter_dimension=0, tiled=True),
        lax.psum_scatter(grads[13], ("dp", "seq"), scatter_dimension=0, tiled=True),
        lax.psum_scatter(grads[14], ("dp", "seq"), scatter_dimension=0, tiled=True),
    )
    return (
        layer_out,
        grad_inputs,
        owned[0],
        owned[6],
        owned[1],
        owned[2],
        owned[7],
        owned[3],
        owned[8],
        owned[9],
        owned[10],
        owned[4],
        owned[11],
        owned[5],
        owned[12],
        owned[13],
        owned[14],
    )


F32=jnp.float32; BF=jnp.bfloat16
NT=(((1,),(1,)),((),()))
NN=(((1,),(0,)),((),()))


def mm(a,b,dims=NN):
    return lax.dot_general(a,b,dims,preferred_element_type=F32)


GROUP=16
LEAD,LAG=6,7


def half_mask(shape, head, dim):
    lanes=lax.broadcasted_iota(jnp.int32,shape,dim)
    return (lanes<64) if head==0 else (lanes>=64)


def only(x, head):
    return jnp.where(half_mask(x.shape,head,1),x,jnp.zeros_like(x))


def take_rows(ref, pos_ref, first):
    width=ref.shape[1]
    out=jnp.zeros((GROUP,width),F32)
    rows=lax.broadcasted_iota(jnp.int32,(GROUP,width),0)
    for m in range(MEM):
        pos=pos_ref[first+m]
        start=pl.multiple_of((pos//GROUP)*GROUP,GROUP)
        part=ref[pl.ds(start,GROUP),:].astype(F32)
        row=jnp.sum(jnp.where(rows==pos-start,part,0.0),0,keepdims=True)
        out=jnp.where(rows==m,row,out)
    return out.astype(BF)


def put_rows(ref, pos_ref, first, values, add):
    width=ref.shape[1]
    rows=lax.broadcasted_iota(jnp.int32,(GROUP,width),0)
    for m in range(MEM):
        pos=pos_ref[first+m]
        start=pl.multiple_of((pos//GROUP)*GROUP,GROUP)
        old=ref[pl.ds(start,GROUP),:].astype(F32)
        row=values[m:m+1,:]
        new=jnp.where(rows==pos-start,old+row if add else row,old)
        ref[pl.ds(start,GROUP),:]=new.astype(ref.dtype)


def transposed(x):
    return jnp.transpose(x)


def fwd_kernel(pos_ref, posv_ref, limit_ref, write_ref, qkv_ref, o_ref, lse_ref, vt_ref, qt_ref, acc_ref, *, bq, np_, qb0, qb1):
    rows_all=qkv_ref.shape[0]
    nq=rows_all//bq
    W=np_*128
    nh=2*np_
    cols=lambda part,p:slice(part*W+p*128,part*W+p*128+128)
    hr=lambda h:slice(80*h,80*h+80)
    mem=take_rows(qkv_ref,pos_ref,0)
    kr=[only(mem[:,cols(1,h//2)],h%2) for h in range(nh)]
    ones16=jnp.ones((16,GROUP),BF)
    vrt=[]
    for p in range(np_):
        vt=transposed(qkv_ref[:,cols(2,p)])
        mt=transposed(mem[:,cols(2,p)])
        qt_ref[p*128:p*128+128,:]=transposed(qkv_ref[:,cols(0,p)])
        for h in range(2):
            vt_ref[80*(2*p+h):80*(2*p+h)+64,:]=vt[64*h:64*h+64]
            vt_ref[80*(2*p+h)+64:80*(2*p+h)+80,:]=jnp.ones((16,rows_all),BF)
            vrt.append(jnp.concatenate([mt[64*h:64*h+64],ones16],0))
    read_pos=posv_ref[...]
    def q_step(qb, unused):
        q0=pl.multiple_of(qb*bq,bq)
        limit=limit_ref[:,pl.ds(q0,bq)][0:1]
        key_iota=lax.broadcasted_iota(jnp.int32,(bq,bq),0)
        zq=jnp.zeros((64,bq),BF)
        def qh(h):
            own=qt_ref[64*h:64*h+64,pl.ds(q0,bq)]
            return jnp.concatenate([own,zq] if h%2==0 else [zq,own],0)
        def soft(h,s,vt,m):
            m2=jnp.maximum(m,jnp.max(s,0,keepdims=True))
            fix=jnp.exp2(m-m2)
            p=jnp.exp2(s-m2)
            acc_ref[hr(h),:]=acc_ref[hr(h),:]*fix+mm(vt,p.astype(BF))
            return m2
        def block(kb,carry,mask):
            k0=pl.multiple_of(kb*bq,bq)
            held={}
            peaks=[None]*nh
            def front(h):
                s=mm(qkv_ref[pl.ds(k0,bq),cols(1,h//2)],qh(h))
                held[h]=jnp.where(key_iota+k0<=limit,s,masked_score) if mask else s
            def middle(h):
                s=held[h]
                peaks[h]=jnp.maximum(carry[h],jnp.max(s,0,keepdims=True))
                held[h]=jnp.exp2(s-peaks[h]).astype(BF)
            def back(h):
                fix=jnp.exp2(carry[h]-peaks[h])
                acc_ref[hr(h),:]=acc_ref[hr(h),:]*fix+mm(vt_ref[hr(h),pl.ds(k0,bq)],held[h])
            for h in range(nh+LAG):
                if h<nh:
                    front(h)
                if 0<=h-LEAD<nh:
                    middle(h-LEAD)
                if h>=LAG:
                    back(h-LAG)
            return tuple(peaks)
        acc_ref[...]=jnp.zeros_like(acc_ref)
        carry=tuple(jnp.full((1,bq),masked_score,F32) for _ in range(nh))
        carry=block(qb,carry,True)
        carry=tuple(soft(h,jnp.where(read_pos>limit,mm(kr[h],qh(h)),masked_score),vrt[h],carry[h]) for h in range(nh))
        carry=lax.fori_loop(0,qb,lambda kb,c:block(kb,c,False),carry)
        far=jnp.max(limit)>=q0+bq
        carry=lax.cond(far,lambda c:block(jnp.minimum(qb+1,nq-1),c,True),lambda c:c,carry)
        wr=write_ref[:,pl.ds(q0,bq)][0:1]
        outs=[]
        for h in range(nh):
            l=acc_ref[80*h+64:80*h+65,:]
            outs.append(acc_ref[80*h:80*h+64,:]/l)
            lse=carry[h]+jnp.log2(l)
            lse_ref[h:h+1,pl.ds(q0,bq)]=jnp.where(wr>0,1e30,lse)
        o_ref[pl.ds(q0,bq),:]=transposed(jnp.concatenate(outs,0).astype(BF))
        return unused
    lax.fori_loop(qb0,qb1,q_step,0)
    rows=take_rows(qkv_ref,pos_ref,MEM)
    out=[]
    for p in range(np_):
        total=jnp.zeros((GROUP,128),F32)
        qw=rows[:,cols(0,p)]
        for h in range(2):
            s=mm(only(qw,h),qkv_ref[:,cols(1,p)],NT)
            m=jnp.max(s,1,keepdims=True)
            e=jnp.exp2(s-m)
            l=jnp.sum(e,1,keepdims=True)
            ow=mm(e.astype(BF),qkv_ref[:,cols(2,p)])/l
            total=total+jnp.where(half_mask((GROUP,128),h,1),ow,0.0)
        out.append(total)
    put_rows(o_ref,pos_ref,MEM,jnp.concatenate(out,1),False)


LN2=0.6931471805599453


def bwd_kernel(pos_ref, posv_ref, limit_ref, qkv_ref, do_ref, o_ref, lse_ref,
               dqkv_ref, bias_ref, qt_ref, kt_ref, dot_ref, dk_acc, dv_acc, dq_acc, dr_acc, *, bq, scale, np_):
    rows_all=qkv_ref.shape[0]
    nq=rows_all//bq
    W=np_*128
    nh=2*np_
    cols=lambda part,p:slice(part*W+p*128,part*W+p*128+128)
    pc=lambda p:slice(p*128,p*128+128)
    hr=lambda h:slice(64*h,64*h+64)
    for p in range(np_):
        qt_ref[pc(p),:]=transposed(qkv_ref[:,cols(0,p)])
        kt_ref[pc(p),:]=transposed(qkv_ref[:,cols(1,p)])
        dot_ref[pc(p),:]=transposed(do_ref[:,pc(p)])
    mem=take_rows(qkv_ref,pos_ref,0)
    kr=[mem[:,cols(1,p)] for p in range(np_)]
    vr=[mem[:,cols(2,p)] for p in range(np_)]
    krt=[transposed(kr[p]) for p in range(np_)]
    read_pos=posv_ref[...]
    rows=take_rows(qkv_ref,pos_ref,MEM)
    dow_all=take_rows(do_ref,pos_ref,MEM)
    valid=lax.broadcasted_iota(jnp.int32,(GROUP,1),0)<MEM
    dqw_all=[]
    for pr in range(np_):
        qw=rows[:,cols(0,pr)]
        dow=dow_all[:,pc(pr)]
        qwt=transposed(qw); dowt=transposed(dow)
        dqw=jnp.zeros((GROUP,128),F32)
        for h in range(2):
            s=mm(only(qw,h),qkv_ref[:,cols(1,pr)],NT)
            m=jnp.max(s,1,keepdims=True)
            p=jnp.exp2(s-m)
            p=p*jnp.where(valid,1.0/jnp.sum(p,1,keepdims=True),0.0)
            dp=mm(only(dow,h),qkv_ref[:,cols(2,pr)],NT)
            ds=(p*(dp-jnp.sum(p*dp,1,keepdims=True))).astype(BF)
            dqw=dqw+jnp.where(half_mask((GROUP,128),h,1),mm(ds,qkv_ref[:,cols(1,pr)]),0.0)
            dk_acc[hr(2*pr+h),:]=mm(qwt[64*h:64*h+64],ds)
            dv_acc[hr(2*pr+h),:]=mm(dowt[64*h:64*h+64],p.astype(BF))
        dqw_all.append(dqw)
    dr_acc[...]=jnp.zeros_like(dr_acc)
    def q_step(qb, unused):
        q0=pl.multiple_of(qb*bq,bq)
        limit=limit_ref[:,pl.ds(q0,bq)][0:1]
        zq=jnp.zeros((64,bq),BF)
        def padded(ref,h):
            own=ref[hr(h),pl.ds(q0,bq)]
            return jnp.concatenate([own,zq] if h%2==0 else [zq,own],0)
        prod=jnp.transpose(do_ref[pl.ds(q0,bq),:].astype(F32)*o_ref[pl.ds(q0,bq),:].astype(F32))
        delta=[jnp.sum(prod[hr(h)],0,keepdims=True) for h in range(nh)]
        lse=[lse_ref[h:h+1,pl.ds(q0,bq)] for h in range(nh)]
        key_iota=lax.broadcasted_iota(jnp.int32,(bq,bq),0)
        dq_acc[...]=jnp.zeros_like(dq_acc)
        def grads(h,s,v):
            p=jnp.exp2(s-lse[h])
            dp=mm(v,padded(dot_ref,h))
            return (p*(dp-delta[h])).astype(BF),p.astype(BF)
        def block(kb,mask):
            k0=pl.multiple_of(kb*bq,bq)
            ks=pl.ds(k0,bq)
            held={}
            def front(h):
                s=mm(qkv_ref[ks,cols(1,h//2)],padded(qt_ref,h))
                if mask:
                    s=jnp.where(key_iota+k0<=limit,s,masked_score)
                held[h]=(s,mm(qkv_ref[ks,cols(2,h//2)],padded(dot_ref,h)))
            def middle(h):
                s,dp=held[h]
                p=jnp.exp2(s-lse[h])
                held[h]=((p*(dp-delta[h])).astype(BF),p.astype(BF))
            def back(h):
                ds,p=held[h]
                dq_acc[hr(h),:]+=mm(kt_ref[hr(h),ks],ds)
                dk_acc[hr(h),ks]+=mm(qt_ref[hr(h),pl.ds(q0,bq)],ds,NT)
                dv_acc[hr(h),ks]+=mm(dot_ref[hr(h),pl.ds(q0,bq)],p,NT)
            for h in range(nh+2):
                if h<nh:
                    front(h)
                if 0<=h-1<nh:
                    middle(h-1)
                if h>=2:
                    back(h-2)
        block(qb,True)
        for h in range(nh):
            s=jnp.where(read_pos>limit,mm(kr[h//2],padded(qt_ref,h)),masked_score)
            ds,p=grads(h,s,vr[h//2])
            dr_acc[0,hr(h),:]+=mm(qt_ref[hr(h),pl.ds(q0,bq)],ds,NT)
            dr_acc[1,hr(h),:]+=mm(dot_ref[hr(h),pl.ds(q0,bq)],p,NT)
            dq_acc[hr(h),:]+=mm(krt[h//2][64*(h%2):64*(h%2)+64,:],ds)
        def step(kb,c):
            block(kb,False)
            return c
        lax.fori_loop(0,qb,step,0)
        @pl.when(jnp.max(limit)>=q0+bq)
        def _():
            block(jnp.minimum(qb+1,nq-1),True)
        dqkv_ref[pl.ds(q0,bq),0:W]=transposed((dq_acc[...]*scale).astype(BF))
        return unused
    lax.fori_loop(0,nq,q_step,0)
    put_rows(dqkv_ref.at[:,0:W],pos_ref,MEM,jnp.concatenate(dqw_all,1)*scale,False)
    for p in range(np_):
        dqkv_ref[:,cols(1,p)]=transposed((dk_acc[pc(p),:]*LN2).astype(BF))
        dqkv_ref[:,cols(2,p)]=transposed(dv_acc[pc(p),:].astype(BF))
    put_rows(dqkv_ref.at[:,W:2*W],pos_ref,0,jnp.transpose(dr_acc[0])*LN2,True)
    put_rows(dqkv_ref.at[:,2*W:3*W],pos_ref,0,jnp.transpose(dr_acc[1]),True)
    rows8=lax.broadcasted_iota(jnp.int32,(8,W),0)
    bq_sum=jnp.sum(dqkv_ref[:,0:W].astype(F32),0,keepdims=True)
    bv_sum=jnp.sum(dqkv_ref[:,2*W:3*W].astype(F32),0,keepdims=True)
    bias_ref[...]=jnp.where(rows8==0,bq_sum,jnp.where(rows8==1,bv_sum,0.0))


ONCE=pl.Buffered(1)


def attn_fwd(qkv, pos, posv, limit, write, np_, bq=256, qb0=0, qb1=None):
    L=qkv.shape[0]; W=np_*128
    row8=pl.BlockSpec((8,L),lambda i:(0,0),pipeline_mode=ONCE)
    full=lambda w:pl.BlockSpec((L,w),lambda i:(0,0),pipeline_mode=ONCE)
    return pl.pallas_call(partial(fwd_kernel,bq=bq,np_=np_,qb0=qb0,qb1=L//bq if qb1 is None else qb1),
        grid=(1,),
        in_specs=[pl.BlockSpec(memory_space=pltpu.SMEM),pl.BlockSpec((GROUP,1),lambda i:(0,0)),row8,row8,full(3*W)],
        out_specs=[full(W),row8],
        out_shape=[jax.ShapeDtypeStruct((L,W),BF),jax.ShapeDtypeStruct((8,L),F32)],
        scratch_shapes=[pltpu.VMEM((np_*160,L),BF),pltpu.VMEM((W,L),BF),pltpu.VMEM((np_*160,bq),F32)],
        name="attn_fwd",
    )(pos,posv,limit,write,qkv)


def attn_bwd(qkv, pos, posv, limit, do, o, lse, np_, scale, bq=256):
    L=qkv.shape[0]; W=np_*128
    row8=pl.BlockSpec((8,L),lambda i:(0,0),pipeline_mode=ONCE)
    full=lambda w:pl.BlockSpec((L,w),lambda i:(0,0),pipeline_mode=ONCE)
    return pl.pallas_call(partial(bwd_kernel,bq=bq,scale=scale,np_=np_),
        grid=(1,),
        in_specs=[pl.BlockSpec(memory_space=pltpu.SMEM),pl.BlockSpec((GROUP,1),lambda i:(0,0)),row8,full(3*W),full(W),full(W),row8],
        out_specs=[full(3*W),pl.BlockSpec((8,W),lambda i:(0,0))],
        out_shape=[jax.ShapeDtypeStruct((L,3*W),BF),jax.ShapeDtypeStruct((8,W),F32)],
        scratch_shapes=[pltpu.VMEM((W,L),BF)]*3+[pltpu.VMEM((W,L),F32)]*2+[pltpu.VMEM((W,bq),F32),pltpu.VMEM((2,W,GROUP),F32)],
        name="attn_bwd",
    )(pos,posv,limit,qkv,do,o,lse)


LANES = 128
LOG2E = 1.4426950408889634
ALL = ("dp", "seq")
RSQRT2 = 0.7071067811865476
RSQRT2PI = 0.3989422804014327


def bit_swap(x, axis, size, bit):
    return lax.ppermute(x, axis, [(i, i ^ bit) for i in range(size)])


def side(flag, own, peer, axis):
    low = jnp.where(flag, peer, own)
    high = jnp.where(flag, own, peer)
    return jnp.concatenate([low, high], axis)


def bits_of(size):
    out = []
    bit = 1
    while bit < size:
        out.append(bit)
        bit *= 2
    return out


def double_dp(out, size, bit):
    other = bit_swap(out, "dp", size, bit)
    up = (lax.axis_index("dp") & bit) != 0
    return jnp.stack([jnp.where(up, other, out), jnp.where(up, out, other)])


def halve_dp(rest, size, bit):
    up = (lax.axis_index("dp") & bit) != 0
    rest = rest.reshape((rest.shape[0] // 2, 2) + rest.shape[1:])
    give = jnp.where(up, rest[:, 0], rest[:, 1]).astype(BF)
    keep = jnp.where(up, rest[:, 1], rest[:, 0])
    got = bit_swap(give, "dp", size, bit)
    return keep + got.astype(F32)


def spread_lanes(rows, part):
    rows = jnp.pad(rows, ((0, 0), (0, part * LANES - rows.shape[1])))
    return rows.reshape(rows.shape[0], part, LANES)


def norm_parts(values):
    centre = jnp.mean(values, -1, keepdims=True)
    centred = values - centre
    spread = jnp.mean(centred * centred, -1, keepdims=True)
    factor = lax.rsqrt(spread + norm_epsilon)
    return centred * factor, factor


def norm_back(gradient, unit, factor):
    return factor * (
        gradient
        - jnp.mean(gradient, -1, keepdims=True)
        - unit * jnp.mean(gradient * unit, -1, keepdims=True)
    )


def fast_body(
    inputs,
    query_weight,
    query_bias,
    key_weight,
    value_weight,
    value_bias,
    output_weight,
    output_bias,
    first_gain,
    first_shift,
    inner_weight,
    inner_bias,
    outer_weight,
    outer_bias,
    second_gain,
    second_shift,
    cotangent,
    piece_start,
    memory_pos,
    *,
    n_dp,
):
    rows, width = inputs.shape
    inner_width = inner_weight.shape[1]
    devices = 2 * n_dp
    part = width // devices
    inner_part = inner_width // devices
    ratio = inner_width // width
    half = width // 2
    seq = lax.axis_index("seq")
    upper = seq == 1

    def swap(x):
        return bit_swap(x, "seq", 2, 1)

    wide = inner_weight.reshape(part, ratio, width).transpose(1, 0, 2).reshape(ratio * part, width)
    packed = jnp.concatenate([output_weight, wide, outer_weight], 0)
    columns_of = [
        query_bias,
        value_bias,
        output_bias,
        first_gain,
        first_shift,
        outer_bias,
        second_gain,
        second_shift,
    ] + [inner_bias[k * part : (k + 1) * part] for k in range(ratio)]
    line = jnp.pad(jnp.stack(columns_of, 1), ((0, 0), (0, LANES - len(columns_of))))

    def columns(upper_half):
        pick = lambda w: jnp.where(upper_half, w[:, half:], w[:, :half])
        return jnp.concatenate([pick(query_weight), pick(key_weight), pick(value_weight), line], 1)

    own_columns = columns(upper)
    peer_columns = swap(columns(jnp.logical_not(upper)))
    peer_inputs = swap(inputs)
    early = side(upper, own_columns[None], peer_columns[None], 0)
    bits = bits_of(n_dp)
    for bit in bits[::-1]:
        early = double_dp(early, n_dp, bit)
        if bit == bits[-1]:
            early, packed = lax.optimization_barrier((early, packed))
            late = lax.all_gather(packed, ALL, axis=0, tiled=False)
    count = len(bits)
    early = early.transpose(tuple(range(count))[::-1] + tuple(range(count, early.ndim)))
    early = early.reshape(width, 3 * half + LANES)
    w_three = early[:, : 3 * half]
    table = early[:, 3 * half :].T.astype(F32)
    b_query, b_value, b_output, g_first, s_first, b_outer, g_second, s_second = (
        table[k] for k in range(8)
    )
    b_inner = table[8 : 8 + ratio].reshape(ratio, devices, part).transpose(1, 0, 2)
    b_inner = b_inner.reshape(inner_width)
    own_half = lambda v: lax.dynamic_slice_in_dim(v, seq * half, half, 0)
    features = side(upper, inputs, peer_inputs, 0)
    scale = HD ** (-0.5)
    shift = jnp.concatenate([own_half(b_query), jnp.zeros((half,), F32), own_half(b_value)])
    grow = jnp.concatenate([jnp.full((half,), scale * LOG2E, F32), jnp.ones((2 * half,), F32)])
    qkv = ((dense(features, w_three) + shift) * grow).astype(BF)
    positions = jnp.arange(2 * rows, dtype=jnp.int32)
    limit = positions
    for piece in range(NPIC):
        start = piece_start[0, piece]
        inside = (positions >= start) & (positions < start + PIC)
        limit = jnp.where(inside, start + PIC - 1, limit)
    memories = memory_pos[0]
    writes = jnp.any(positions[None, :] == memories[MEM:, None], 0).astype(jnp.int32)
    limit = jnp.broadcast_to(limit, (8, 2 * rows))
    writes = jnp.broadcast_to(writes, (8, 2 * rows))
    reads = jnp.pad(memories[:MEM], (0, GROUP - MEM), constant_values=-1)[:, None]
    pairs = half // (2 * HD)
    out_heads, totals = attn_fwd(qkv, memories, reads, limit, writes, pairs)
    own_of = lambda v: lax.dynamic_slice_in_dim(v, seq * rows, rows, 0)
    peer_of = lambda v: lax.dynamic_slice_in_dim(v, (1 - seq) * rows, rows, 0)
    other_rows = peer_of(out_heads)
    own_rows = own_of(out_heads)
    attended = side(upper, own_rows, swap(other_rows), 1)
    w_output = late[:, :part].reshape(width, width)
    w_inner = jnp.concatenate(
        [
            late[:, part + k * part : 2 * part + k * part].reshape(width, width)
            for k in range(ratio)
        ],
        1,
    )
    w_outer = late[:, part + ratio * part :].reshape(inner_width, width)
    mixed = inputs.astype(F32) + dense(attended, w_output) + b_output
    first_unit, first_factor = norm_parts(mixed)
    hidden_norm = first_unit * g_first + s_first
    hidden_low = hidden_norm.astype(BF)
    inner = dense(hidden_low, w_inner) + b_inner
    chance = 0.5 * (1.0 + lax.erf(inner * RSQRT2))
    activated = (inner * chance).astype(BF)
    slope = (chance + inner * (RSQRT2PI * jnp.exp(-0.5 * inner * inner))).astype(BF)
    activated, slope = lax.optimization_barrier((activated, slope))
    second_in = hidden_norm + dense(activated, w_outer) + b_outer
    second_unit, second_factor = norm_parts(second_in)
    layer_out = (second_unit * g_second + s_second).astype(BF)
    cot = cotangent.astype(F32)
    grad_second_gain = jnp.sum(cot * second_unit, 0)
    grad_second_shift = jnp.sum(cot, 0)
    grad_second_in = norm_back(cot * g_second, second_unit, second_factor)
    grad_outer_bias = jnp.sum(grad_second_in, 0)
    second_low = grad_second_in.astype(BF)
    grad_inner = back_product(second_low, w_outer) * slope.astype(F32)
    grad_inner_bias = jnp.sum(grad_inner, 0)
    inner_low = grad_inner.astype(BF)
    column = lambda k: inner_low[:, k * width : (k + 1) * width]
    inner_blocks = [
        outer_product(hidden_low, column(k)).astype(BF).reshape(devices, part, width)
        for k in range(ratio)
    ]
    grad_outer_weight = outer_product(activated, second_low).astype(BF)
    bundle = jnp.concatenate(
        inner_blocks + [grad_outer_weight.reshape(devices, inner_part, width)], 1
    )
    bundle_rows = bundle.shape[1]
    bundle, inner_low = lax.optimization_barrier((bundle, inner_low))
    reduced = lax.psum_scatter(
        bundle.reshape(devices * bundle_rows, width), ALL, scatter_dimension=0, tiled=True
    )
    grad_hidden = grad_second_in + back_product(inner_low, w_inner)
    grad_first_gain = jnp.sum(grad_hidden * first_unit, 0)
    grad_first_shift = jnp.sum(grad_hidden, 0)
    grad_mixed = norm_back(grad_hidden * g_first, first_unit, first_factor)
    grad_output_bias = jnp.sum(grad_mixed, 0)
    mixed_low = grad_mixed.astype(BF)
    grad_attended = back_product(mixed_low, w_output).astype(BF)
    grad_other = lax.dynamic_slice_in_dim(grad_attended, (1 - seq) * half, half, 1)
    grad_own = lax.dynamic_slice_in_dim(grad_attended, seq * half, half, 1)
    grad_heads = side(upper, grad_own, swap(grad_other), 0)
    grad_output_weight = outer_product(attended, mixed_low).reshape(devices, part, width)
    thin = [
        grad_output_bias,
        grad_first_gain,
        grad_first_shift,
        grad_outer_bias,
        grad_second_gain,
        grad_second_shift,
    ]
    thin = jnp.concatenate(
        [v.reshape(devices, part) for v in thin] + [grad_inner_bias.reshape(devices, inner_part)], 1
    )
    mid = jnp.concatenate([grad_output_weight, spread_lanes(thin, part)], 2)
    mid = mid.reshape(n_dp, 2, part, width + LANES)
    mid = halve_dp(mid, n_dp, bits[0])
    mid = halve_dp(mid, n_dp, bits[1])
    grads, bias_sums = attn_bwd(
        qkv, memories, reads, limit, grad_heads, out_heads, totals, pairs, scale
    )
    other_grads = peer_of(grads)
    own_grads = own_of(grads)
    for_peer = back_product(other_grads, w_three).astype(BF)
    sent = swap(for_peer)
    three_grad = outer_product(features, grads).reshape(devices, part, 3 * half)
    full = lambda v: side(upper, v, jnp.zeros_like(v), 0).reshape(devices, part)
    tails = jnp.concatenate([full(bias_sums[0]), full(bias_sums[1])], 1)
    blocks = jnp.concatenate([three_grad, spread_lanes(tails, part)], 2)
    wide_half = 3 * half + LANES
    blocks = blocks.reshape(n_dp, 2, part, wide_half)
    blocks = halve_dp(blocks, n_dp, bits[0])
    own_part = lax.optimization_barrier(grad_mixed + back_product(own_grads, w_three))
    blocks = halve_dp(blocks, n_dp, bits[1])
    for bit in bits[2:]:
        mid = halve_dp(mid, n_dp, bit)
        blocks = halve_dp(blocks, n_dp, bit)
    mine = jnp.concatenate([blocks[0], mid[0]], 2)
    give = jnp.where(upper, mine[0], mine[1]).astype(BF)
    keep = jnp.where(upper, mine[1], mine[0])
    own_inner = jnp.concatenate(
        [reduced[k * part : (k + 1) * part] for k in range(ratio)], 1
    ).astype(F32)
    own_outer = reduced[ratio * part :].astype(F32)
    give, own_inner, own_outer = lax.optimization_barrier((give, own_inner, own_outer))
    got = swap(give).astype(F32)
    grad_inputs = own_part + sent.astype(F32)
    span = lambda x, k, n: x[:, k : k + n]
    both = lambda k, n: span(keep, k, n) + span(got, k, n)
    matrix = lambda k: side(upper, span(keep, k * half, half), span(got, k * half, half), 1)
    grad_output = both(wide_half, width)
    thin_sum = both(wide_half + width, LANES).reshape(-1)
    tail_sum = both(3 * half, LANES).reshape(-1)
    thin_part = lambda k: thin_sum[k * part : (k + 1) * part]
    return (
        layer_out,
        grad_inputs,
        matrix(0),
        tail_sum[:part],
        matrix(1),
        matrix(2),
        tail_sum[part : 2 * part],
        grad_output,
        thin_part(0),
        thin_part(1),
        thin_part(2),
        own_inner,
        thin_sum[6 * part : 6 * part + inner_part],
        own_outer,
        thin_part(3),
        thin_part(4),
        thin_part(5),
    )


def solution(mesh):
    in_specs = (
        P(("dp", "seq"), None),
        P(("dp", "seq"), None),
        P(("dp", "seq")),
        P(("dp", "seq"), None),
        P(("dp", "seq"), None),
        P(("dp", "seq")),
        P(("dp", "seq"), None),
        P(("dp", "seq")),
        P(("dp", "seq")),
        P(("dp", "seq")),
        P(("dp", "seq"), None),
        P(("dp", "seq")),
        P(("dp", "seq"), None),
        P(("dp", "seq")),
        P(("dp", "seq")),
        P(("dp", "seq")),
        P(("dp", "seq"), None),
        P("dp", None),
        P("dp", None),
    )
    out_specs = (
        P(("dp", "seq"), None),
        P(("dp", "seq"), None),
        P(("dp", "seq"), None),
        P(("dp", "seq")),
        P(("dp", "seq"), None),
        P(("dp", "seq"), None),
        P(("dp", "seq")),
        P(("dp", "seq"), None),
        P(("dp", "seq")),
        P(("dp", "seq")),
        P(("dp", "seq")),
        P(("dp", "seq"), None),
        P(("dp", "seq")),
        P(("dp", "seq"), None),
        P(("dp", "seq")),
        P(("dp", "seq")),
        P(("dp", "seq")),
    )
    n_dp = mesh.shape["dp"]
    if mesh.shape["seq"] != 2 or n_dp & (n_dp - 1) != 0 or n_dp < 4:
        return jax.shard_map(
            body, mesh=mesh, in_specs=in_specs, out_specs=out_specs, check_vma=False
        )

    def chosen(*arrays):
        return fast_body(*arrays, n_dp=n_dp)

    return jax.shard_map(
        chosen, mesh=mesh, in_specs=in_specs, out_specs=out_specs, check_vma=False
    )
```

```python
from functools import partial

import jax
import jax.numpy as jnp
from jax import lax
from jax.experimental import pallas as pl
from jax.experimental.pallas import tpu as pltpu
from jax.sharding import PartitionSpec as P


H = 12
HD = 64
LEN = 2048
PIC = 256
NPIC = 2
MEM = 10


norm_epsilon = 1e-05
masked_score = -1e30


def normalize(values, gain, shift):
    centre = jnp.mean(values, -1, keepdims=True)
    centred = values - centre
    spread = jnp.mean(centred * centred, -1, keepdims=True)
    return centred * lax.rsqrt(spread + norm_epsilon) * gain + shift


def gelu_exact(values):
    return jax.nn.gelu(values, approximate=False)


def visible_cols(positions, columns, starts, memories):
    labels = jnp.arange(NPIC, dtype=jnp.int32)[:, None] + 1
    in_cols = (columns[None, :] >= starts[:, None]) & (columns[None, :] < starts[:, None] + PIC)
    in_rows = (positions[None, :] >= starts[:, None]) & (positions[None, :] < starts[:, None] + PIC)
    piece_cols = jnp.sum(jnp.where(in_cols, labels, 0), 0)
    piece_rows = jnp.sum(jnp.where(in_rows, labels, 0), 0)
    same_piece = (piece_rows[:, None] == piece_cols[None, :]) & (piece_rows[:, None] > 0)
    read_cols = jnp.any(columns[None, :] == memories[:MEM, None], 0)
    write_rows = jnp.any(positions[None, :] == memories[MEM:, None], 0)
    causal = columns[None, :] <= positions[:, None]
    return causal | same_piece | read_cols[None, :] | write_rows[:, None]


def visible(positions, starts, memories):
    return visible_cols(positions, jnp.arange(LEN, dtype=jnp.int32), starts, memories)


def dense(left, right):
    return jnp.dot(left, right, preferred_element_type=jnp.float32)


def outer_product(left, right):
    return jnp.einsum("ta,tb->ab", left, right, preferred_element_type=jnp.float32)


def back_product(gradient, weight):
    return jnp.einsum("tb,ab->ta", gradient, weight, preferred_element_type=jnp.float32)


def body(
    inputs,
    query_weight,
    query_bias,
    key_weight,
    value_weight,
    value_bias,
    output_weight,
    output_bias,
    first_gain,
    first_shift,
    inner_weight,
    inner_bias,
    outer_weight,
    outer_bias,
    second_gain,
    second_shift,
    cotangent,
    piece_start,
    memory_pos,
):
    shards = (
        query_weight,
        key_weight,
        value_weight,
        output_weight,
        inner_weight,
        outer_weight,
        query_bias,
        value_bias,
        output_bias,
        first_gain,
        first_shift,
        inner_bias,
        outer_bias,
        second_gain,
        second_shift,
    )
    gathered = (
        lax.all_gather(shards[0], ("dp", "seq"), axis=0, tiled=True),
        lax.all_gather(shards[1], ("dp", "seq"), axis=0, tiled=True),
        lax.all_gather(shards[2], ("dp", "seq"), axis=0, tiled=True),
        lax.all_gather(shards[3], ("dp", "seq"), axis=0, tiled=True),
        lax.all_gather(shards[4], ("dp", "seq"), axis=0, tiled=True),
        lax.all_gather(shards[5], ("dp", "seq"), axis=0, tiled=True),
        lax.all_gather(shards[6], ("dp", "seq"), axis=0, tiled=True),
        lax.all_gather(shards[7], ("dp", "seq"), axis=0, tiled=True),
        lax.all_gather(shards[8], ("dp", "seq"), axis=0, tiled=True),
        lax.all_gather(shards[9], ("dp", "seq"), axis=0, tiled=True),
        lax.all_gather(shards[10], ("dp", "seq"), axis=0, tiled=True),
        lax.all_gather(shards[11], ("dp", "seq"), axis=0, tiled=True),
        lax.all_gather(shards[12], ("dp", "seq"), axis=0, tiled=True),
        lax.all_gather(shards[13], ("dp", "seq"), axis=0, tiled=True),
        lax.all_gather(shards[14], ("dp", "seq"), axis=0, tiled=True),
    )
    w_query, w_key, w_value, w_output, w_inner, w_outer = gathered[:6]
    vectors = [vector.astype(jnp.float32) for vector in gathered[6:]]
    b_query, b_value, b_output, g_first, s_first, b_inner, b_outer, g_second, s_second = vectors
    local_rows = inputs.shape[0]
    model_width = inputs.shape[1]
    score_scale = HD ** (-0.5)
    pair_count = H // 2
    pair_width = 2 * HD
    block_rows = min(512, local_rows, LEN)
    block_count = local_rows // block_rows
    first_row = lax.axis_index("seq") * local_rows
    query_low = (dense(inputs, w_query) + b_query).astype(jnp.bfloat16)
    key_low = dense(inputs, w_key).astype(jnp.bfloat16)
    value_low = (dense(inputs, w_value) + b_value).astype(jnp.bfloat16)
    group_keys, group_values = (
        lax.all_gather(key_low, "seq", axis=0, tiled=True),
        lax.all_gather(value_low, "seq", axis=0, tiled=True),
    )
    group_rows = group_keys.shape[0]

    def context(block_index):
        row_start = first_row + block_index * block_rows
        seq_index = row_start // LEN
        positions = row_start - seq_index * LEN + jnp.arange(block_rows, dtype=jnp.int32)
        starts = piece_start[0]
        memories = memory_pos[0]
        allowed = visible(positions, starts, memories)
        return (seq_index, allowed, group_keys, group_values)

    def pair_part(matrix, pair_index, count):
        return lax.dynamic_slice_in_dim(matrix, pair_index * pair_width, pair_width, 1).reshape(
            count, 2, HD
        )

    def pair_scores(query_pair, key_pair, allowed):
        raw = (
            jnp.einsum("qhd,khd->hqk", query_pair, key_pair, preferred_element_type=jnp.float32)
            * score_scale
        )
        return jnp.where(allowed[None], raw, masked_score)

    def forward_block(block_index):
        _, allowed, seq_keys, seq_values = context(block_index)
        block_query = lax.dynamic_slice_in_dim(query_low, block_index * block_rows, block_rows, 0)

        def forward_pair_step(carry, pair_index):
            out_buffer, total_buffer = carry
            query_pair = pair_part(block_query, pair_index, block_rows)
            key_pair = pair_part(seq_keys, pair_index, LEN)
            value_pair = pair_part(seq_values, pair_index, LEN)
            scores = pair_scores(query_pair, key_pair, allowed)
            peak = jnp.max(scores, -1, keepdims=True)
            expo_terms = jnp.exp(scores - peak)
            row_sum = jnp.sum(expo_terms, -1, keepdims=True)
            chances_low = (expo_terms / row_sum).astype(jnp.bfloat16)
            blended = jnp.einsum(
                "hqk,khd->qhd", chances_low, value_pair, preferred_element_type=jnp.float32
            )
            blended = blended.reshape(block_rows, pair_width).astype(jnp.bfloat16)
            out_buffer = lax.dynamic_update_slice_in_dim(
                out_buffer, blended, pair_index * pair_width, 1
            )
            log_pair = (peak + jnp.log(row_sum))[:, :, 0]
            total_buffer = lax.dynamic_update_slice_in_dim(
                total_buffer, log_pair, pair_index * 2, 0
            )
            return ((out_buffer, total_buffer), None)

        initial = (
            jnp.zeros((block_rows, model_width), jnp.bfloat16),
            jnp.zeros((H, block_rows), jnp.float32),
        )
        (out_buffer, total_buffer), unused = lax.scan(
            forward_pair_step, initial, jnp.arange(pair_count)
        )
        return (out_buffer, total_buffer)

    attended_blocks, log_totals = lax.map(forward_block, jnp.arange(block_count))
    attended = attended_blocks.reshape(local_rows, model_width)
    mixed = inputs.astype(jnp.float32) + dense(attended, w_output) + b_output
    hidden_norm, first_pull = jax.vjp(normalize, mixed, g_first, s_first)
    hidden_low = hidden_norm.astype(jnp.bfloat16)
    inner = dense(hidden_low, w_inner) + b_inner
    activated_full, gelu_pull = jax.vjp(gelu_exact, inner)
    activated = activated_full.astype(jnp.bfloat16)
    second_in = hidden_norm + dense(activated, w_outer) + b_outer
    normed_out, second_pull = jax.vjp(normalize, second_in, g_second, s_second)
    layer_out = normed_out.astype(jnp.bfloat16)
    back_weights = (
        lax.all_gather(query_weight, ("dp", "seq"), axis=0, tiled=True),
        lax.all_gather(key_weight, ("dp", "seq"), axis=0, tiled=True),
        lax.all_gather(value_weight, ("dp", "seq"), axis=0, tiled=True),
        lax.all_gather(output_weight, ("dp", "seq"), axis=0, tiled=True),
        lax.all_gather(inner_weight, ("dp", "seq"), axis=0, tiled=True),
        lax.all_gather(outer_weight, ("dp", "seq"), axis=0, tiled=True),
    )
    v_query, v_key, v_value, v_output, v_inner, v_outer = back_weights
    grad_second_in, grad_second_gain, grad_second_shift = second_pull(cotangent.astype(jnp.float32))
    grad_outer_bias = jnp.sum(grad_second_in, 0)
    second_low = grad_second_in.astype(jnp.bfloat16)
    grad_outer_weight = outer_product(activated, second_low)
    (grad_inner,) = gelu_pull(back_product(second_low, v_outer))
    grad_inner_bias = jnp.sum(grad_inner, 0)
    inner_low = grad_inner.astype(jnp.bfloat16)
    grad_inner_weight = outer_product(hidden_low, inner_low)
    grad_hidden = grad_second_in + back_product(inner_low, v_inner)
    grad_mixed, grad_first_gain, grad_first_shift = first_pull(grad_hidden)
    grad_output_bias = jnp.sum(grad_mixed, 0)
    mixed_low = grad_mixed.astype(jnp.bfloat16)
    grad_output_weight = outer_product(attended, mixed_low)
    grad_attended = back_product(mixed_low, v_output).astype(jnp.bfloat16)

    def backward_block(carry, block_index):
        _, allowed, seq_keys, seq_values = context(block_index)
        block_query = lax.dynamic_slice_in_dim(query_low, block_index * block_rows, block_rows, 0)
        block_grad = lax.dynamic_slice_in_dim(
            grad_attended, block_index * block_rows, block_rows, 0
        )
        block_total = log_totals[block_index]

        def backward_pair_step(inner_carry, pair_index):
            query_grad, term_buffer = (inner_carry[0], inner_carry[1])
            query_pair = pair_part(block_query, pair_index, block_rows)
            key_pair = pair_part(seq_keys, pair_index, LEN)
            value_pair = pair_part(seq_values, pair_index, LEN)
            grad_pair = pair_part(block_grad, pair_index, block_rows)
            scores = pair_scores(query_pair, key_pair, allowed)
            total_pair = lax.dynamic_slice_in_dim(block_total, pair_index * 2, 2, 0)
            chances = jnp.exp(scores - total_pair[:, :, None])
            chance_grad = jnp.einsum(
                "qhd,khd->hqk", grad_pair, value_pair, preferred_element_type=jnp.float32
            )
            row_terms = jnp.sum(chances * chance_grad, -1, keepdims=True)
            score_grad = (chances * (chance_grad - row_terms)).astype(jnp.bfloat16)
            query_part = jnp.einsum(
                "hqk,khd->qhd", score_grad, key_pair, preferred_element_type=jnp.float32
            )
            query_part = query_part.reshape(block_rows, pair_width) * score_scale
            query_grad = lax.dynamic_update_slice_in_dim(
                query_grad, query_part, pair_index * pair_width, 1
            )
            term_buffer = lax.dynamic_update_slice_in_dim(
                term_buffer, row_terms[:, :, 0], pair_index * 2, 0
            )
            seq_key_grad, seq_value_grad = (inner_carry[2], inner_carry[3])
            chances_low = chances.astype(jnp.bfloat16)
            key_part = jnp.einsum(
                "hqk,qhd->khd", score_grad, query_pair, preferred_element_type=jnp.float32
            )
            value_part = jnp.einsum(
                "hqk,qhd->khd", chances_low, grad_pair, preferred_element_type=jnp.float32
            )
            key_part = key_part.reshape(LEN, pair_width) * score_scale
            value_part = value_part.reshape(LEN, pair_width)
            seq_key_grad = lax.dynamic_update_slice_in_dim(
                seq_key_grad, key_part, pair_index * pair_width, 1
            )
            seq_value_grad = lax.dynamic_update_slice_in_dim(
                seq_value_grad, value_part, pair_index * pair_width, 1
            )
            return ((query_grad, term_buffer, seq_key_grad, seq_value_grad), None)

        initial = (
            jnp.zeros((block_rows, model_width), jnp.float32),
            jnp.zeros((H, block_rows), jnp.float32),
        )
        initial = initial + (
            jnp.zeros((LEN, model_width), jnp.float32),
            jnp.zeros((LEN, model_width), jnp.float32),
        )
        finals, _ = lax.scan(backward_pair_step, initial, jnp.arange(pair_count))
        key_grads, value_grads = carry
        key_grads = key_grads + finals[2]
        value_grads = value_grads + finals[3]
        carry = (key_grads, value_grads)
        return (carry, (finals[0], finals[1]))

    group_zero = jnp.zeros((group_rows, model_width), jnp.float32)
    (key_grads, value_grads), (query_blocks, term_blocks) = lax.scan(
        backward_block, (group_zero, group_zero), jnp.arange(block_count)
    )
    key_sum, value_sum = (
        lax.psum_scatter(
            key_grads.astype(jnp.bfloat16), "seq", scatter_dimension=0, tiled=True
        ).astype(jnp.float32),
        lax.psum_scatter(
            value_grads.astype(jnp.bfloat16), "seq", scatter_dimension=0, tiled=True
        ).astype(jnp.float32),
    )
    query_sum = query_blocks.reshape(local_rows, model_width)
    grad_query_bias = jnp.sum(query_sum, 0)
    grad_value_bias = jnp.sum(value_sum, 0)
    query_grad_low = query_sum.astype(jnp.bfloat16)
    key_grad_low = key_sum.astype(jnp.bfloat16)
    value_grad_low = value_sum.astype(jnp.bfloat16)
    grad_query_weight = outer_product(inputs, query_grad_low)
    grad_key_weight = outer_product(inputs, key_grad_low)
    grad_value_weight = outer_product(inputs, value_grad_low)
    grad_inputs = (
        grad_mixed
        + back_product(query_grad_low, v_query)
        + back_product(key_grad_low, v_key)
        + back_product(value_grad_low, v_value)
    )
    grads = (
        grad_query_weight,
        grad_key_weight,
        grad_value_weight,
        grad_output_weight,
        grad_inner_weight,
        grad_outer_weight,
        grad_query_bias,
        grad_value_bias,
        grad_output_bias,
        grad_first_gain,
        grad_first_shift,
        grad_inner_bias,
        grad_outer_bias,
        grad_second_gain,
        grad_second_shift,
    )
    owned = (
        lax.psum_scatter(grads[0], ("dp", "seq"), scatter_dimension=0, tiled=True),
        lax.psum_scatter(grads[1], ("dp", "seq"), scatter_dimension=0, tiled=True),
        lax.psum_scatter(grads[2], ("dp", "seq"), scatter_dimension=0, tiled=True),
        lax.psum_scatter(grads[3], ("dp", "seq"), scatter_dimension=0, tiled=True),
        lax.psum_scatter(grads[4], ("dp", "seq"), scatter_dimension=0, tiled=True),
        lax.psum_scatter(grads[5], ("dp", "seq"), scatter_dimension=0, tiled=True),
        lax.psum_scatter(grads[6], ("dp", "seq"), scatter_dimension=0, tiled=True),
        lax.psum_scatter(grads[7], ("dp", "seq"), scatter_dimension=0, tiled=True),
        lax.psum_scatter(grads[8], ("dp", "seq"), scatter_dimension=0, tiled=True),
        lax.psum_scatter(grads[9], ("dp", "seq"), scatter_dimension=0, tiled=True),
        lax.psum_scatter(grads[10], ("dp", "seq"), scatter_dimension=0, tiled=True),
        lax.psum_scatter(grads[11], ("dp", "seq"), scatter_dimension=0, tiled=True),
        lax.psum_scatter(grads[12], ("dp", "seq"), scatter_dimension=0, tiled=True),
        lax.psum_scatter(grads[13], ("dp", "seq"), scatter_dimension=0, tiled=True),
        lax.psum_scatter(grads[14], ("dp", "seq"), scatter_dimension=0, tiled=True),
    )
    return (
        layer_out,
        grad_inputs,
        owned[0],
        owned[6],
        owned[1],
        owned[2],
        owned[7],
        owned[3],
        owned[8],
        owned[9],
        owned[10],
        owned[4],
        owned[11],
        owned[5],
        owned[12],
        owned[13],
        owned[14],
    )


F32=jnp.float32; BF=jnp.bfloat16
NT=(((1,),(1,)),((),()))
NN=(((1,),(0,)),((),()))


def mm(a,b,dims=NN):
    return lax.dot_general(a,b,dims,preferred_element_type=F32)


GROUP=16


def half_mask(shape, head, dim):
    lanes=lax.broadcasted_iota(jnp.int32,shape,dim)
    return (lanes<64) if head==0 else (lanes>=64)


def only(x, head):
    return jnp.where(half_mask(x.shape,head,1),x,jnp.zeros_like(x))


def take_rows(ref, pos_ref, first):
    width=ref.shape[1]
    out=jnp.zeros((GROUP,width),F32)
    rows=lax.broadcasted_iota(jnp.int32,(GROUP,width),0)
    for m in range(MEM):
        pos=pos_ref[first+m]
        start=pl.multiple_of((pos//GROUP)*GROUP,GROUP)
        part=ref[pl.ds(start,GROUP),:].astype(F32)
        row=jnp.sum(jnp.where(rows==pos-start,part,0.0),0,keepdims=True)
        out=jnp.where(rows==m,row,out)
    return out.astype(BF)


def put_rows(ref, pos_ref, first, values, add):
    width=ref.shape[1]
    rows=lax.broadcasted_iota(jnp.int32,(GROUP,width),0)
    for m in range(MEM):
        pos=pos_ref[first+m]
        start=pl.multiple_of((pos//GROUP)*GROUP,GROUP)
        old=ref[pl.ds(start,GROUP),:].astype(F32)
        row=values[m:m+1,:]
        new=jnp.where(rows==pos-start,old+row if add else row,old)
        ref[pl.ds(start,GROUP),:]=new.astype(ref.dtype)


def transposed(x):
    return jnp.transpose(x)


def fwd_kernel(pos_ref, posv_ref, limit_ref, write_ref, qkv_ref, o_ref, lse_ref, vt_ref, qt_ref, acc_ref, *, bq, np_, qb0, qb1):
    rows_all=qkv_ref.shape[0]
    nq=rows_all//bq
    W=np_*128
    nh=2*np_
    cols=lambda part,p:slice(part*W+p*128,part*W+p*128+128)
    hr=lambda h:slice(80*h,80*h+80)
    mem=take_rows(qkv_ref,pos_ref,0)
    kr=[only(mem[:,cols(1,h//2)],h%2) for h in range(nh)]
    ones16=jnp.ones((16,GROUP),BF)
    vrt=[]
    for p in range(np_):
        vt=transposed(qkv_ref[:,cols(2,p)])
        mt=transposed(mem[:,cols(2,p)])
        qt_ref[p*128:p*128+128,:]=transposed(qkv_ref[:,cols(0,p)])
        for h in range(2):
            vt_ref[80*(2*p+h):80*(2*p+h)+64,:]=vt[64*h:64*h+64]
            vt_ref[80*(2*p+h)+64:80*(2*p+h)+80,:]=jnp.ones((16,rows_all),BF)
            vrt.append(jnp.concatenate([mt[64*h:64*h+64],ones16],0))
    read_pos=posv_ref[...]
    def q_step(qb, unused):
        q0=pl.multiple_of(qb*bq,bq)
        limit=limit_ref[:,pl.ds(q0,bq)][0:1]
        key_iota=lax.broadcasted_iota(jnp.int32,(bq,bq),0)
        zq=jnp.zeros((64,bq),BF)
        def qh(h):
            own=qt_ref[64*h:64*h+64,pl.ds(q0,bq)]
            return jnp.concatenate([own,zq] if h%2==0 else [zq,own],0)
        def soft(h,s,vt,m):
            m2=jnp.maximum(m,jnp.max(s,0,keepdims=True))
            fix=jnp.exp2(m-m2)
            p=jnp.exp2(s-m2)
            acc_ref[hr(h),:]=acc_ref[hr(h),:]*fix+mm(vt,p.astype(BF))
            return m2
        def block(kb,carry,mask,wide=1):
            k0=pl.multiple_of(kb*bq,bq)
            LEAD,LAG=nh,nh+1
            held={}
            peaks=[None]*nh
            def front(h):
                s=mm(qkv_ref[pl.ds(k0,wide*bq),cols(1,h//2)],qh(h))
                held[h]=jnp.where(key_iota+k0<=limit,s,masked_score) if mask else s
            def middle(h):
                s=held[h]
                peaks[h]=jnp.maximum(carry[h],jnp.max(s,0,keepdims=True))
                held[h]=jnp.exp2(s-peaks[h]).astype(BF)
            def back(h):
                fix=jnp.exp2(carry[h]-peaks[h])
                acc_ref[hr(h),:]=acc_ref[hr(h),:]*fix+mm(vt_ref[hr(h),pl.ds(k0,wide*bq)],held[h])
            for h in range(nh+LAG):
                if h<nh:
                    front(h)
                if 0<=h-LEAD<nh:
                    middle(h-LEAD)
                if h>=LAG:
                    back(h-LAG)
            return tuple(peaks)
        acc_ref[...]=jnp.zeros_like(acc_ref)
        carry=tuple(jnp.full((1,bq),masked_score,F32) for _ in range(nh))
        carry=block(qb,carry,True)
        carry=tuple(soft(h,jnp.where(read_pos>limit,mm(kr[h],qh(h)),masked_score),vrt[h],carry[h]) for h in range(nh))
        carry=lax.fori_loop(0,qb//2,lambda kb,c:block(2*kb,c,False,2),carry)
        carry=lax.cond(qb%2==1,lambda c:block(jnp.maximum(qb-1,0),c,False),lambda c:c,carry)
        far=jnp.max(limit)>=q0+bq
        carry=lax.cond(far,lambda c:block(jnp.minimum(qb+1,nq-1),c,True),lambda c:c,carry)
        wr=write_ref[:,pl.ds(q0,bq)][0:1]
        outs=[]
        for h in range(nh):
            l=acc_ref[80*h+64:80*h+65,:]
            outs.append(acc_ref[80*h:80*h+64,:]/l)
            lse=carry[h]+jnp.log2(l)
            lse_ref[h:h+1,pl.ds(q0,bq)]=jnp.where(wr>0,1e30,lse)
        o_ref[pl.ds(q0,bq),:]=transposed(jnp.concatenate(outs,0).astype(BF))
        return unused
    lax.fori_loop(qb0,qb1,q_step,0)
    rows=take_rows(qkv_ref,pos_ref,MEM)
    out=[]
    for p in range(np_):
        total=jnp.zeros((GROUP,128),F32)
        qw=rows[:,cols(0,p)]
        for h in range(2):
            s=mm(only(qw,h),qkv_ref[:,cols(1,p)],NT)
            m=jnp.max(s,1,keepdims=True)
            e=jnp.exp2(s-m)
            l=jnp.sum(e,1,keepdims=True)
            ow=mm(e.astype(BF),qkv_ref[:,cols(2,p)])/l
            total=total+jnp.where(half_mask((GROUP,128),h,1),ow,0.0)
        out.append(total)
    put_rows(o_ref,pos_ref,MEM,jnp.concatenate(out,1),False)


LN2=0.6931471805599453


def bwd_kernel(pos_ref, posv_ref, limit_ref, qkv_ref, do_ref, o_ref, lse_ref,
               dqkv_ref, bias_ref, qt_ref, kt_ref, dot_ref, dk_acc, dv_acc, dq_acc, dr_acc, *, bq, scale, np_):
    rows_all=qkv_ref.shape[0]
    nq=rows_all//bq
    W=np_*128
    nh=2*np_
    cols=lambda part,p:slice(part*W+p*128,part*W+p*128+128)
    pc=lambda p:slice(p*128,p*128+128)
    hr=lambda h:slice(64*h,64*h+64)
    for p in range(np_):
        qt_ref[pc(p),:]=transposed(qkv_ref[:,cols(0,p)])
        kt_ref[pc(p),:]=transposed(qkv_ref[:,cols(1,p)])
        dot_ref[pc(p),:]=transposed(do_ref[:,pc(p)])
    mem=take_rows(qkv_ref,pos_ref,0)
    kr=[mem[:,cols(1,p)] for p in range(np_)]
    vr=[mem[:,cols(2,p)] for p in range(np_)]
    krt=[transposed(kr[p]) for p in range(np_)]
    read_pos=posv_ref[...]
    rows=take_rows(qkv_ref,pos_ref,MEM)
    dow_all=take_rows(do_ref,pos_ref,MEM)
    valid=lax.broadcasted_iota(jnp.int32,(GROUP,1),0)<MEM
    dqw_all=[]
    for pr in range(np_):
        qw=rows[:,cols(0,pr)]
        dow=dow_all[:,pc(pr)]
        qwt=transposed(qw); dowt=transposed(dow)
        dqw=jnp.zeros((GROUP,128),F32)
        for h in range(2):
            s=mm(only(qw,h),qkv_ref[:,cols(1,pr)],NT)
            m=jnp.max(s,1,keepdims=True)
            p=jnp.exp2(s-m)
            p=p*jnp.where(valid,1.0/jnp.sum(p,1,keepdims=True),0.0)
            dp=mm(only(dow,h),qkv_ref[:,cols(2,pr)],NT)
            ds=(p*(dp-jnp.sum(p*dp,1,keepdims=True))).astype(BF)
            dqw=dqw+jnp.where(half_mask((GROUP,128),h,1),mm(ds,qkv_ref[:,cols(1,pr)]),0.0)
            dk_acc[hr(2*pr+h),:]=mm(qwt[64*h:64*h+64],ds)
            dv_acc[hr(2*pr+h),:]=mm(dowt[64*h:64*h+64],p.astype(BF))
        dqw_all.append(dqw)
    dr_acc[...]=jnp.zeros_like(dr_acc)
    def q_step(qb, unused):
        q0=pl.multiple_of(qb*bq,bq)
        limit=limit_ref[:,pl.ds(q0,bq)][0:1]
        zq=jnp.zeros((64,bq),BF)
        def padded(ref,h):
            own=ref[hr(h),pl.ds(q0,bq)]
            return jnp.concatenate([own,zq] if h%2==0 else [zq,own],0)
        prod=jnp.transpose(do_ref[pl.ds(q0,bq),:].astype(F32)*o_ref[pl.ds(q0,bq),:].astype(F32))
        delta=[jnp.sum(prod[hr(h)],0,keepdims=True) for h in range(nh)]
        lse=[lse_ref[h:h+1,pl.ds(q0,bq)] for h in range(nh)]
        key_iota=lax.broadcasted_iota(jnp.int32,(bq,bq),0)
        dq_acc[...]=jnp.zeros_like(dq_acc)
        def grads(h,s,v):
            p=jnp.exp2(s-lse[h])
            dp=mm(v,padded(dot_ref,h))
            return (p*(dp-delta[h])).astype(BF),p.astype(BF)
        def block(kb,mask):
            k0=pl.multiple_of(kb*bq,bq)
            ks=pl.ds(k0,bq)
            held={}
            def front(h):
                s=mm(qkv_ref[ks,cols(1,h//2)],padded(qt_ref,h))
                if mask:
                    s=jnp.where(key_iota+k0<=limit,s,masked_score)
                held[h]=(s,mm(qkv_ref[ks,cols(2,h//2)],padded(dot_ref,h)))
            def middle(h):
                s,dp=held[h]
                p=jnp.exp2(s-lse[h])
                held[h]=((p*(dp-delta[h])).astype(BF),p.astype(BF))
            def back(h):
                ds,p=held[h]
                dq_acc[hr(h),:]+=mm(kt_ref[hr(h),ks],ds)
                dk_acc[hr(h),ks]+=mm(qt_ref[hr(h),pl.ds(q0,bq)],ds,NT)
                dv_acc[hr(h),ks]+=mm(dot_ref[hr(h),pl.ds(q0,bq)],p,NT)
            for h in range(nh+2):
                if h<nh:
                    front(h)
                if 0<=h-1<nh:
                    middle(h-1)
                if h>=2:
                    back(h-2)
        block(qb,True)
        for h in range(nh):
            s=jnp.where(read_pos>limit,mm(kr[h//2],padded(qt_ref,h)),masked_score)
            ds,p=grads(h,s,vr[h//2])
            dr_acc[0,hr(h),:]+=mm(qt_ref[hr(h),pl.ds(q0,bq)],ds,NT)
            dr_acc[1,hr(h),:]+=mm(dot_ref[hr(h),pl.ds(q0,bq)],p,NT)
            dq_acc[hr(h),:]+=mm(krt[h//2][64*(h%2):64*(h%2)+64,:],ds)
        def step(kb,c):
            block(kb,False)
            return c
        lax.fori_loop(0,qb,step,0)
        @pl.when(jnp.max(limit)>=q0+bq)
        def _():
            block(jnp.minimum(qb+1,nq-1),True)
        dqkv_ref[pl.ds(q0,bq),0:W]=transposed((dq_acc[...]*scale).astype(BF))
        return unused
    lax.fori_loop(0,nq,q_step,0)
    put_rows(dqkv_ref.at[:,0:W],pos_ref,MEM,jnp.concatenate(dqw_all,1)*scale,False)
    for p in range(np_):
        dqkv_ref[:,cols(1,p)]=transposed((dk_acc[pc(p),:]*LN2).astype(BF))
        dqkv_ref[:,cols(2,p)]=transposed(dv_acc[pc(p),:].astype(BF))
    put_rows(dqkv_ref.at[:,W:2*W],pos_ref,0,jnp.transpose(dr_acc[0])*LN2,True)
    put_rows(dqkv_ref.at[:,2*W:3*W],pos_ref,0,jnp.transpose(dr_acc[1]),True)
    rows8=lax.broadcasted_iota(jnp.int32,(8,W),0)
    bq_sum=jnp.sum(dqkv_ref[:,0:W].astype(F32),0,keepdims=True)
    bv_sum=jnp.sum(dqkv_ref[:,2*W:3*W].astype(F32),0,keepdims=True)
    bias_ref[...]=jnp.where(rows8==0,bq_sum,jnp.where(rows8==1,bv_sum,0.0))


ONCE=pl.Buffered(1)


def attn_fwd(qkv, pos, posv, limit, write, np_, bq=256, qb0=0, qb1=None):
    L=qkv.shape[0]; W=np_*128
    row8=pl.BlockSpec((8,L),lambda i:(0,0),pipeline_mode=ONCE)
    full=lambda w:pl.BlockSpec((L,w),lambda i:(0,0),pipeline_mode=ONCE)
    return pl.pallas_call(partial(fwd_kernel,bq=bq,np_=np_,qb0=qb0,qb1=L//bq if qb1 is None else qb1),
        grid=(1,),
        in_specs=[pl.BlockSpec(memory_space=pltpu.SMEM),pl.BlockSpec((GROUP,1),lambda i:(0,0)),row8,row8,full(3*W)],
        out_specs=[full(W),row8],
        out_shape=[jax.ShapeDtypeStruct((L,W),BF),jax.ShapeDtypeStruct((8,L),F32)],
        scratch_shapes=[pltpu.VMEM((np_*160,L),BF),pltpu.VMEM((W,L),BF),pltpu.VMEM((np_*160,bq),F32)],
        name="attn_fwd",
    )(pos,posv,limit,write,qkv)


def attn_bwd(qkv, pos, posv, limit, do, o, lse, np_, scale, bq=256):
    L=qkv.shape[0]; W=np_*128
    row8=pl.BlockSpec((8,L),lambda i:(0,0),pipeline_mode=ONCE)
    full=lambda w:pl.BlockSpec((L,w),lambda i:(0,0),pipeline_mode=ONCE)
    return pl.pallas_call(partial(bwd_kernel,bq=bq,scale=scale,np_=np_),
        grid=(1,),
        in_specs=[pl.BlockSpec(memory_space=pltpu.SMEM),pl.BlockSpec((GROUP,1),lambda i:(0,0)),row8,full(3*W),full(W),full(W),row8],
        out_specs=[full(3*W),pl.BlockSpec((8,W),lambda i:(0,0))],
        out_shape=[jax.ShapeDtypeStruct((L,3*W),BF),jax.ShapeDtypeStruct((8,W),F32)],
        scratch_shapes=[pltpu.VMEM((W,L),BF)]*3+[pltpu.VMEM((W,L),F32)]*2+[pltpu.VMEM((W,bq),F32),pltpu.VMEM((2,W,GROUP),F32)],
        name="attn_bwd",
    )(pos,posv,limit,qkv,do,o,lse)


LANES = 128
LOG2E = 1.4426950408889634
ALL = ("dp", "seq")
RSQRT2 = 0.7071067811865476
RSQRT2PI = 0.3989422804014327


def bit_swap(x, axis, size, bit):
    return lax.ppermute(x, axis, [(i, i ^ bit) for i in range(size)])


def side(flag, own, peer, axis):
    low = jnp.where(flag, peer, own)
    high = jnp.where(flag, own, peer)
    return jnp.concatenate([low, high], axis)


def bits_of(size):
    out = []
    bit = 1
    while bit < size:
        out.append(bit)
        bit *= 2
    return out


def double_dp(out, size, bit):
    other = bit_swap(out, "dp", size, bit)
    up = (lax.axis_index("dp") & bit) != 0
    return jnp.stack([jnp.where(up, other, out), jnp.where(up, out, other)])


def halve_dp(rest, size, bit):
    up = (lax.axis_index("dp") & bit) != 0
    rest = rest.reshape((rest.shape[0] // 2, 2) + rest.shape[1:])
    give = jnp.where(up, rest[:, 0], rest[:, 1]).astype(BF)
    keep = jnp.where(up, rest[:, 1], rest[:, 0])
    got = bit_swap(give, "dp", size, bit)
    return keep + got.astype(F32)


def spread_lanes(rows, part):
    rows = jnp.pad(rows, ((0, 0), (0, part * LANES - rows.shape[1])))
    return rows.reshape(rows.shape[0], part, LANES)


def norm_parts(values):
    centre = jnp.mean(values, -1, keepdims=True)
    centred = values - centre
    spread = jnp.mean(centred * centred, -1, keepdims=True)
    factor = lax.rsqrt(spread + norm_epsilon)
    return centred * factor, factor


def norm_back(gradient, unit, factor):
    return factor * (
        gradient
        - jnp.mean(gradient, -1, keepdims=True)
        - unit * jnp.mean(gradient * unit, -1, keepdims=True)
    )


def fast_body(
    inputs,
    query_weight,
    query_bias,
    key_weight,
    value_weight,
    value_bias,
    output_weight,
    output_bias,
    first_gain,
    first_shift,
    inner_weight,
    inner_bias,
    outer_weight,
    outer_bias,
    second_gain,
    second_shift,
    cotangent,
    piece_start,
    memory_pos,
    *,
    n_dp,
):
    rows, width = inputs.shape
    inner_width = inner_weight.shape[1]
    devices = 2 * n_dp
    part = width // devices
    inner_part = inner_width // devices
    ratio = inner_width // width
    half = width // 2
    seq = lax.axis_index("seq")
    upper = seq == 1

    def swap(x):
        return bit_swap(x, "seq", 2, 1)

    wide = inner_weight.reshape(part, ratio, width).transpose(1, 0, 2).reshape(ratio * part, width)
    packed = jnp.concatenate([output_weight, wide, outer_weight], 0)
    columns_of = [
        query_bias,
        value_bias,
        output_bias,
        first_gain,
        first_shift,
        outer_bias,
        second_gain,
        second_shift,
    ] + [inner_bias[k * part : (k + 1) * part] for k in range(ratio)]
    line = jnp.pad(jnp.stack(columns_of, 1), ((0, 0), (0, LANES - len(columns_of))))

    def columns(upper_half):
        pick = lambda w: jnp.where(upper_half, w[:, half:], w[:, :half])
        return jnp.concatenate([pick(query_weight), pick(key_weight), pick(value_weight), line], 1)

    own_columns = columns(upper)
    peer_columns = swap(columns(jnp.logical_not(upper)))
    peer_inputs = swap(inputs)
    early = side(upper, own_columns[None], peer_columns[None], 0)
    bits = bits_of(n_dp)
    for bit in bits[::-1]:
        early = double_dp(early, n_dp, bit)
        if bit == bits[-1]:
            early, packed = lax.optimization_barrier((early, packed))
            late = lax.all_gather(packed, ALL, axis=0, tiled=False)
    count = len(bits)
    early = early.transpose(tuple(range(count))[::-1] + tuple(range(count, early.ndim)))
    early = early.reshape(width, 3 * half + LANES)
    w_three = early[:, : 3 * half]
    table = early[:, 3 * half :].T.astype(F32)
    b_query, b_value, b_output, g_first, s_first, b_outer, g_second, s_second = (
        table[k] for k in range(8)
    )
    b_inner = table[8 : 8 + ratio].reshape(ratio, devices, part).transpose(1, 0, 2)
    b_inner = b_inner.reshape(inner_width)
    own_half = lambda v: lax.dynamic_slice_in_dim(v, seq * half, half, 0)
    features = side(upper, inputs, peer_inputs, 0)
    scale = HD ** (-0.5)
    shift = jnp.concatenate([own_half(b_query), jnp.zeros((half,), F32), own_half(b_value)])
    grow = jnp.concatenate([jnp.full((half,), scale * LOG2E, F32), jnp.ones((2 * half,), F32)])
    qkv = ((dense(features, w_three) + shift) * grow).astype(BF)
    positions = jnp.arange(2 * rows, dtype=jnp.int32)
    limit = positions
    for piece in range(NPIC):
        start = piece_start[0, piece]
        inside = (positions >= start) & (positions < start + PIC)
        limit = jnp.where(inside, start + PIC - 1, limit)
    memories = memory_pos[0]
    writes = jnp.any(positions[None, :] == memories[MEM:, None], 0).astype(jnp.int32)
    limit = jnp.broadcast_to(limit, (8, 2 * rows))
    writes = jnp.broadcast_to(writes, (8, 2 * rows))
    reads = jnp.pad(memories[:MEM], (0, GROUP - MEM), constant_values=-1)[:, None]
    pairs = half // (2 * HD)
    out_heads, totals = attn_fwd(qkv, memories, reads, limit, writes, pairs)
    own_of = lambda v: lax.dynamic_slice_in_dim(v, seq * rows, rows, 0)
    peer_of = lambda v: lax.dynamic_slice_in_dim(v, (1 - seq) * rows, rows, 0)
    other_rows = peer_of(out_heads)
    own_rows = own_of(out_heads)
    attended = side(upper, own_rows, swap(other_rows), 1)
    w_output = late[:, :part].reshape(width, width)
    w_inner = jnp.concatenate(
        [
            late[:, part + k * part : 2 * part + k * part].reshape(width, width)
            for k in range(ratio)
        ],
        1,
    )
    w_outer = late[:, part + ratio * part :].reshape(inner_width, width)
    mixed = inputs.astype(F32) + dense(attended, w_output) + b_output
    first_unit, first_factor = norm_parts(mixed)
    hidden_norm = first_unit * g_first + s_first
    hidden_low = hidden_norm.astype(BF)
    inner = dense(hidden_low, w_inner) + b_inner
    chance = 0.5 * (1.0 + lax.erf(inner * RSQRT2))
    activated = (inner * chance).astype(BF)
    slope = (chance + inner * (RSQRT2PI * jnp.exp(-0.5 * inner * inner))).astype(BF)
    activated, slope = lax.optimization_barrier((activated, slope))
    second_in = hidden_norm + dense(activated, w_outer) + b_outer
    second_unit, second_factor = norm_parts(second_in)
    layer_out = (second_unit * g_second + s_second).astype(BF)
    cot = cotangent.astype(F32)
    grad_second_gain = jnp.sum(cot * second_unit, 0)
    grad_second_shift = jnp.sum(cot, 0)
    grad_second_in = norm_back(cot * g_second, second_unit, second_factor)
    grad_outer_bias = jnp.sum(grad_second_in, 0)
    second_low = grad_second_in.astype(BF)
    grad_inner = back_product(second_low, w_outer) * slope.astype(F32)
    grad_inner_bias = jnp.sum(grad_inner, 0)
    inner_low = grad_inner.astype(BF)
    column = lambda k: inner_low[:, k * width : (k + 1) * width]
    inner_blocks = [
        outer_product(hidden_low, column(k)).astype(BF).reshape(devices, part, width)
        for k in range(ratio)
    ]
    grad_outer_weight = outer_product(activated, second_low).astype(BF)
    bundle = jnp.concatenate(
        inner_blocks + [grad_outer_weight.reshape(devices, inner_part, width)], 1
    )
    bundle_rows = bundle.shape[1]
    bundle, inner_low = lax.optimization_barrier((bundle, inner_low))
    reduced = lax.psum_scatter(
        bundle.reshape(devices * bundle_rows, width), ALL, scatter_dimension=0, tiled=True
    )
    grad_hidden = grad_second_in + back_product(inner_low, w_inner)
    grad_first_gain = jnp.sum(grad_hidden * first_unit, 0)
    grad_first_shift = jnp.sum(grad_hidden, 0)
    grad_mixed = norm_back(grad_hidden * g_first, first_unit, first_factor)
    grad_output_bias = jnp.sum(grad_mixed, 0)
    mixed_low = grad_mixed.astype(BF)
    grad_attended = back_product(mixed_low, w_output).astype(BF)
    grad_other = lax.dynamic_slice_in_dim(grad_attended, (1 - seq) * half, half, 1)
    grad_own = lax.dynamic_slice_in_dim(grad_attended, seq * half, half, 1)
    grad_heads = side(upper, grad_own, swap(grad_other), 0)
    grad_output_weight = outer_product(attended, mixed_low).reshape(devices, part, width)
    thin = [
        grad_output_bias,
        grad_first_gain,
        grad_first_shift,
        grad_outer_bias,
        grad_second_gain,
        grad_second_shift,
    ]
    thin = jnp.concatenate(
        [v.reshape(devices, part) for v in thin] + [grad_inner_bias.reshape(devices, inner_part)], 1
    )
    mid = jnp.concatenate([grad_output_weight, spread_lanes(thin, part)], 2)
    mid = mid.reshape(n_dp, 2, part, width + LANES)
    mid = halve_dp(mid, n_dp, bits[0])
    mid = halve_dp(mid, n_dp, bits[1])
    grads, bias_sums = attn_bwd(
        qkv, memories, reads, limit, grad_heads, out_heads, totals, pairs, scale
    )
    other_grads = peer_of(grads)
    own_grads = own_of(grads)
    for_peer = back_product(other_grads, w_three).astype(BF)
    for_peer, grads = lax.optimization_barrier((for_peer, grads))
    sent = swap(for_peer)
    three_grad = outer_product(features, grads).reshape(devices, part, 3 * half)
    full = lambda v: side(upper, v, jnp.zeros_like(v), 0).reshape(devices, part)
    tails = jnp.concatenate([full(bias_sums[0]), full(bias_sums[1])], 1)
    blocks = jnp.concatenate([three_grad, spread_lanes(tails, part)], 2)
    wide_half = 3 * half + LANES
    blocks = blocks.reshape(n_dp, 2, part, wide_half)
    blocks = halve_dp(blocks, n_dp, bits[0])
    own_part = lax.optimization_barrier(grad_mixed + back_product(own_grads, w_three))
    blocks = halve_dp(blocks, n_dp, bits[1])
    for bit in bits[2:]:
        mid = halve_dp(mid, n_dp, bit)
        blocks = halve_dp(blocks, n_dp, bit)
    mine = jnp.concatenate([blocks[0], mid[0]], 2)
    give = jnp.where(upper, mine[0], mine[1]).astype(BF)
    keep = jnp.where(upper, mine[1], mine[0])
    own_inner = jnp.concatenate(
        [reduced[k * part : (k + 1) * part] for k in range(ratio)], 1
    ).astype(F32)
    own_outer = reduced[ratio * part :].astype(F32)
    give, own_inner, own_outer = lax.optimization_barrier((give, own_inner, own_outer))
    got = swap(give).astype(F32)
    grad_inputs = own_part + sent.astype(F32)
    span = lambda x, k, n: x[:, k : k + n]
    both = lambda k, n: span(keep, k, n) + span(got, k, n)
    matrix = lambda k: side(upper, span(keep, k * half, half), span(got, k * half, half), 1)
    grad_output = both(wide_half, width)
    thin_sum = both(wide_half + width, LANES).reshape(-1)
    tail_sum = both(3 * half, LANES).reshape(-1)
    thin_part = lambda k: thin_sum[k * part : (k + 1) * part]
    return (
        layer_out,
        grad_inputs,
        matrix(0),
        tail_sum[:part],
        matrix(1),
        matrix(2),
        tail_sum[part : 2 * part],
        grad_output,
        thin_part(0),
        thin_part(1),
        thin_part(2),
        own_inner,
        thin_sum[6 * part : 6 * part + inner_part],
        own_outer,
        thin_part(3),
        thin_part(4),
        thin_part(5),
    )


def solution(mesh):
    in_specs = (
        P(("dp", "seq"), None),
        P(("dp", "seq"), None),
        P(("dp", "seq")),
        P(("dp", "seq"), None),
        P(("dp", "seq"), None),
        P(("dp", "seq")),
        P(("dp", "seq"), None),
        P(("dp", "seq")),
        P(("dp", "seq")),
        P(("dp", "seq")),
        P(("dp", "seq"), None),
        P(("dp", "seq")),
        P(("dp", "seq"), None),
        P(("dp", "seq")),
        P(("dp", "seq")),
        P(("dp", "seq")),
        P(("dp", "seq"), None),
        P("dp", None),
        P("dp", None),
    )
    out_specs = (
        P(("dp", "seq"), None),
        P(("dp", "seq"), None),
        P(("dp", "seq"), None),
        P(("dp", "seq")),
        P(("dp", "seq"), None),
        P(("dp", "seq"), None),
        P(("dp", "seq")),
        P(("dp", "seq"), None),
        P(("dp", "seq")),
        P(("dp", "seq")),
        P(("dp", "seq")),
        P(("dp", "seq"), None),
        P(("dp", "seq")),
        P(("dp", "seq"), None),
        P(("dp", "seq")),
        P(("dp", "seq")),
        P(("dp", "seq")),
    )
    n_dp = mesh.shape["dp"]
    if mesh.shape["seq"] != 2 or n_dp & (n_dp - 1) != 0 or n_dp < 4:
        return jax.shard_map(
            body, mesh=mesh, in_specs=in_specs, out_specs=out_specs, check_vma=False
        )

    def chosen(*arrays):
        return fast_body(*arrays, n_dp=n_dp)

    return jax.shard_map(
        chosen, mesh=mesh, in_specs=in_specs, out_specs=out_specs, check_vma=False
    )
```
